32 devices in a mesh: shard: 4 (over z), ctx: 2 (over y), tp: 4 (over x, core).
Axes of the slice: x: 2, y: 2, z: 4, core: 2. Of those that a mesh axis runs over, the one named last changes fastest.
Arguments:
- video_in: bfloat16 [16, 8, 196, 768], P('shard', 'tp', 'ctx'), may hold values from -6 to 6
- cotangent: bfloat16 [16, 8, 196, 768], P('shard', 'tp', 'ctx'), may hold values from -6 to 6
- qkv_time: bfloat16 [768, 3, 768], P(('shard', 'ctx'), None, 'tp'), may hold values from -0.21875 to 0.21875
- proj_time: bfloat16 [768, 768], P('tp', ('shard', 'ctx')), may hold values from -0.4375 to 0.4375
- qkv_space: bfloat16 [768, 3, 768], P(('shard', 'ctx'), None, 'tp'), may hold values from -0.21875 to 0.21875
- proj_space: bfloat16 [768, 768], P('tp', ('shard', 'ctx')), may hold values from -1.5 to 1.5
- fc_in: bfloat16 [768, 3072], P(('shard', 'ctx'), 'tp'), may hold values from -0.21875 to 0.21875
- fc_out: bfloat16 [3072, 768], P('tp', ('shard', 'ctx')), may hold values from -0.15625 to 0.15625
- gain_time: float32 [768], P(('shard', 'ctx', 'tp')), may hold values from 0.25 to 1.75
- shift_time: float32 [768], P(('shard', 'ctx', 'tp')), may hold values from -3 to 3
- bias_time: float32 [768], P(('shard', 'ctx', 'tp')), may hold values from -3 to 3
- gain_space: float32 [768], P(('shard', 'ctx', 'tp')), may hold values from 0.25 to 1.75
- shift_space: float32 [768], P(('shard', 'ctx', 'tp')), may hold values from -3 to 3
- bias_space: float32 [768], P(('shard', 'ctx', 'tp')), may hold values from -3 to 3
- gain_mlp: float32 [768], P(('shard', 'ctx', 'tp')), may hold values from 0.25 to 1.75
- shift_mlp: float32 [768], P(('shard', 'ctx', 'tp')), may hold values from -3 to 3
- bias_in: float32 [3072], P(('shard', 'ctx', 'tp')), may hold values from -3 to 3
- bias_out: float32 [768], P(('shard', 'ctx', 'tp')), may hold values from -3 to 3
Outputs:
- result: bfloat16 [16, 8, 196, 768], P('shard', 'tp', 'ctx')
- grad_video: float32 [16, 8, 196, 768], P('shard', 'tp', 'ctx')
- grad_qkv_time: float32 [768, 3, 768], P(('shard', 'ctx'), None, 'tp')
- grad_proj_time: float32 [768, 768], P('tp', ('shard', 'ctx'))
- grad_qkv_space: float32 [768, 3, 768], P(('shard', 'ctx'), None, 'tp')
- grad_proj_space: float32 [768, 768], P('tp', ('shard', 'ctx'))
- grad_fc_in: float32 [768, 3072], P(('shard', 'ctx'), 'tp')
- grad_fc_out: float32 [3072, 768], P('tp', ('shard', 'ctx'))
- grad_gain_time: float32 [768], P(('shard', 'ctx', 'tp'))
- grad_shift_time: float32 [768], P(('shard', 'ctx', 'tp'))
- grad_bias_time: float32 [768], P(('shard', 'ctx', 'tp'))
- grad_gain_space: float32 [768], P(('shard', 'ctx', 'tp'))
- grad_shift_space: float32 [768], P(('shard', 'ctx', 'tp'))
- grad_bias_space: float32 [768], P(('shard', 'ctx', 'tp'))
- grad_gain_mlp: float32 [768], P(('shard', 'ctx', 'tp'))
- grad_shift_mlp: float32 [768], P(('shard', 'ctx', 'tp'))
- grad_bias_in: float32 [3072], P(('shard', 'ctx', 'tp'))
- grad_bias_out: float32 [768], P(('shard', 'ctx', 'tp'))
The draws below stay inside these ranges and needn't reach their ends.
All inputs are finite; a program needn't handle non-finite values.
Results may differ from the reference program's by a relative error of at most 0.03.
Values may be sent and summed in bfloat16 or wider, within the bound.
No kernel may reach another device: no remote copies, remote signals or barrier semaphores. Data moves between devices by JAX's collectives and lax.ppermute only.
A program may use at most 256 MiB of HBM per device.

```python
import jax
import jax.numpy as jnp
from jax import lax

D = 768
HEADS = 12
HEAD_DIM = 64
FF = 3072
FRAMES = 8
PLACES = 196
CLIPS = 16


def level_of(own_key, shape, split, low, largest):
    loudness = 1.0
    for dim, blocks in split:
        draws = jax.random.uniform(jax.random.fold_in(jax.random.fold_in(own_key, 6), dim), (blocks,), jnp.float32, low / len(split), largest / len(split))
        loudness = loudness * jnp.repeat(jnp.exp(draws), shape[dim] // blocks).reshape((-1,) + (1,) * (len(shape) - 1 - dim))
    return loudness


def noise(own_key, dims, deviation, most, split=(), kind=jnp.bfloat16):
    level = level_of(own_key, dims, split, -0.22, 0.18) if split else 1.0
    values = jax.random.normal(own_key, dims, jnp.float32) * deviation * level
    return jnp.minimum(jnp.maximum(values, -most), most).astype(kind)


def setup_inputs(seed: int = 0) -> dict:
    arg_keys = jax.random.split(jax.random.key(seed), 19)
    return {
        "video_in": noise(arg_keys[0], (CLIPS, FRAMES, PLACES, D), 1.0, 6.0, ((0, 4), (1, 4), (2, 2))),
        "cotangent": noise(arg_keys[1], (CLIPS, FRAMES, PLACES, D), 1.0, 6.0, ((0, 4), (1, 4), (2, 2))),
        "qkv_time": noise(arg_keys[2], (D, 3, D), D ** -0.5, 0.21875, ((0, 8), (2, 4))),
        "proj_time": noise(arg_keys[3], (D, D), (D // 4) ** -0.5, 0.4375, ((0, 4), (1, 8))),
        "qkv_space": noise(arg_keys[4], (D, 3, D), D ** -0.5, 0.21875, ((0, 8), (2, 4))),
        "proj_space": noise(arg_keys[5], (D, D), (D // 48) ** -0.5, 1.5, ((0, 4), (1, 8))),
        "fc_in": noise(arg_keys[6], (D, FF), D ** -0.5, 0.21875, ((0, 8), (1, 4))),
        "fc_out": noise(arg_keys[7], (FF, D), (FF // 2) ** -0.5, 0.15625, ((0, 4), (1, 8))),
        "gain_time": jnp.clip(1.0 + 0.15 * jax.random.normal(arg_keys[8], (D,), jnp.float32), 0.25, 1.75),
        "shift_time": noise(arg_keys[9], (D,), 0.5, 3.0, ((0, 32),), jnp.float32),
        "bias_time": noise(arg_keys[10], (D,), 0.5, 3.0, ((0, 32),), jnp.float32),
        "gain_space": jnp.clip(1.0 + 0.15 * jax.random.normal(arg_keys[11], (D,), jnp.float32), 0.25, 1.75),
        "shift_space": noise(arg_keys[12], (D,), 0.5, 3.0, ((0, 32),), jnp.float32),
        "bias_space": noise(arg_keys[13], (D,), 0.5, 3.0, ((0, 32),), jnp.float32),
        "gain_mlp": jnp.clip(1.0 + 0.15 * jax.random.normal(arg_keys[14], (D,), jnp.float32), 0.25, 1.75),
        "shift_mlp": noise(arg_keys[15], (D,), 0.5, 3.0, ((0, 32),), jnp.float32),
        "bias_in": noise(arg_keys[16], (FF,), 0.5, 3.0, ((0, 32),), jnp.float32),
        "bias_out": noise(arg_keys[17], (D,), 0.5, 3.0, ((0, 32),), jnp.float32),
    }


@jax.custom_vjp
def low(v):
    return lax.optimization_barrier(v.astype(jnp.bfloat16)).astype(jnp.float32)

@jax.custom_vjp
def low_back(v):
    return v

def low_keep(v):
    return (low(v), None)

def low_pass(kept, grad):
    return (grad,)

def back_keep(v):
    return (v, None)

def back_low(kept, grad):
    return (low(grad),)
low.defvjp(low_keep, low_pass)
low_back.defvjp(back_keep, back_low)
HIGHEST = lax.Precision.HIGHEST
EPSILON = 1e-06

def layer_norm(inputs, gain_vec, shift_vec):
    average = lax.optimization_barrier(jnp.mean(inputs, axis=-1, keepdims=True))
    centred = inputs - average
    spread = lax.optimization_barrier(jnp.mean(centred * centred, axis=-1, keepdims=True))
    return centred * lax.rsqrt(spread + EPSILON) * gain_vec + shift_vec

def split_heads(packed):
    split_up = packed.reshape(FRAMES, PLACES, 3, HEADS, HEAD_DIM)
    return (split_up[:, :, 0], split_up[:, :, 1], split_up[:, :, 2])

def forward(clip, params):
    qkv_time, proj_time, qkv_space, proj_space, fc_in, fc_out, gain_time, shift_time, bias_time, gain_space, shift_space, bias_space, gain_mlp, shift_mlp, bias_in, bias_out = params
    scaling = HEAD_DIM ** (-0.5)
    normed = low(layer_norm(clip, gain_time, shift_time))
    packed = low(low_back(jnp.einsum('fpd,dkj->fpkj', normed, qkv_time, precision=HIGHEST)))
    queries, keys_in, values = split_heads(packed)
    scores = low_back(jnp.einsum('fphe,gphe->phfg', queries, keys_in, precision=HIGHEST))
    attn_prob = jax.nn.softmax(scores * scaling, axis=-1)
    mixed = jnp.einsum('phfg,gphe->fphe', low(attn_prob), values, precision=HIGHEST).reshape(FRAMES, PLACES, D)
    mixed = low(low_back(mixed))
    stream_one = clip + low_back(jnp.einsum('fpj,jd->fpd', mixed, proj_time, precision=HIGHEST)) + bias_time
    normed = low(layer_norm(stream_one, gain_space, shift_space))
    packed = low(low_back(jnp.einsum('fpd,dkj->fpkj', normed, qkv_space, precision=HIGHEST)))
    queries, keys_in, values = split_heads(packed)
    scores = low_back(jnp.einsum('fqhe,fkhe->fhqk', queries, keys_in, precision=HIGHEST))
    attn_prob = jax.nn.softmax(scores * scaling, axis=-1)
    mixed = jnp.einsum('fhqk,fkhe->fqhe', low(attn_prob), values, precision=HIGHEST).reshape(FRAMES, PLACES, D)
    mixed = low(low_back(mixed))
    stream_two = stream_one + low_back(jnp.einsum('fpj,jd->fpd', mixed, proj_space, precision=HIGHEST)) + bias_space
    normed = low(layer_norm(stream_two, gain_mlp, shift_mlp))
    hidden_pre = low_back(jnp.einsum('fpd,dj->fpj', normed, fc_in, precision=HIGHEST) + bias_in)
    hidden_act = low(jax.nn.gelu(hidden_pre, approximate=False))
    return stream_two + low_back(jnp.einsum('fpj,jd->fpd', hidden_act, fc_out, precision=HIGHEST)) + bias_out

def reference(video_in, cotangent, qkv_time, proj_time, qkv_space, proj_space, fc_in, fc_out, gain_time, shift_time, bias_time, gain_space, shift_space, bias_space, gain_mlp, shift_mlp, bias_in, bias_out):
    params = tuple((item.astype(jnp.float32) for item in (qkv_time, proj_time, qkv_space, proj_space, fc_in, fc_out, gain_time, shift_time, bias_time, gain_space, shift_space, bias_space, gain_mlp, shift_mlp, bias_in, bias_out)))

    def one_clip(totals, pair):
        clip, slope = pair
        output, pullback = jax.vjp(forward, clip.astype(jnp.float32), params)
        d_clip, d_params = pullback(slope.astype(jnp.float32))
        totals = tuple((total + extra for total, extra in zip(totals, d_params)))
        return (totals, (output.astype(jnp.bfloat16), d_clip))
    start = tuple((jnp.zeros(item.shape, jnp.float32) for item in params))
    totals, (result, grad_video) = lax.scan(one_clip, start, (video_in, cotangent))
    g_qkv_t, g_proj_t, g_qkv_s, g_proj_s, g_fc_in, g_fc_out, g_gain_t, g_shift_t, g_bias_t, g_gain_s, g_shift_s, g_bias_s, g_gain_m, g_shift_m, g_bias_in, g_bias_out = totals
    return (result, grad_video, g_qkv_t, g_proj_t, g_qkv_s, g_proj_s, g_fc_in, g_fc_out, g_gain_t, g_shift_t, g_bias_t, g_gain_s, g_shift_s, g_bias_s, g_gain_m, g_shift_m, g_bias_in, g_bias_out)
```

```python
import functools

import jax
import jax.numpy as jnp
from jax import lax
from jax.experimental import pallas as pl
from jax.experimental.pallas import tpu as pltpu
from jax.sharding import Mesh
from jax.sharding import PartitionSpec as P

F32 = jnp.float32
B16 = jnp.bfloat16
HEAD_DIM = 64
SCALING = HEAD_DIM ** (-0.5)
EPSILON = 1e-06
NEGATIVE = -1e30
PAD = 104
NT_DIMS = (((1,), (1,)), ((), ()))
TN_DIMS = (((0,), (0,)), ((), ()))
FLIP = [(0, 1), (1, 0)]
VMEM_LIMIT = 64 * 1024 * 1024 - 65536


def over_x(v):
    return lax.ppermute(v, "x", FLIP)


def over_y(v):
    return lax.ppermute(v, "ctx", FLIP)


def over_xy(v):
    return lax.ppermute(v, ("ctx", "x"), [(i, 3 - i) for i in range(4)])


def over_core(v):
    return lax.ppermute(v, "core", FLIP)


def over_z(v):
    return lax.all_to_all(v, "shard", split_axis=0, concat_axis=0, tiled=True)


def after(values, *results):
    return lax.optimization_barrier((values, results))[0]


def layout(chunks, n):
    full = [(z, k) for z in range(n) for k in range(chunks)]
    h = len(full) // 2
    return [(0, 0, full), (1, 0, full), (0, 1, full), (1, 1, full[:h]), (1, 1, full[h:])]


class Gather:
    def __init__(self, owns, n, shifts=False):
        self.own, self.n, self.shifts = jnp.stack(owns), n, shifts

    def stage_z(self, *deps):
        own, n = self.own, self.n
        if self.shifts:
            own = after(own, *deps)
            self.z = [own] + [
                lax.ppermute(own, "shard", [((i + d) % n, i) for i in range(n)])
                for d in range(1, n)
            ]
            return self.z[1:]
        spread = lax.optimization_barrier(jnp.broadcast_to(own[None], (n,) + own.shape))
        self.z = [over_z(after(spread, *deps))]
        return self.z

    def stage_xy(self, *deps):
        z = after(tuple(self.z), *deps)
        self.blk = jnp.concatenate([v.reshape((-1,) + v.shape[-2:]) for v in z], axis=0)
        self.x, self.y = over_x(self.blk), over_y(self.blk)
        self.sent = [self.blk]
        return [self.x, self.y]

    def stage_rest(self, *deps):
        h = self.blk.shape[0] // 2
        x, y = after((self.x, self.y), *deps)
        self.sent = [x[:h], y[h:]]
        self.rest = [over_y(self.sent[0]), over_x(self.sent[1])]
        self.far = [over_core(v) for v in (self.blk, x, y)]
        return self.rest

    def stage_core(self, *deps):
        rest = after(tuple(self.rest), *deps)
        return [self.blk, self.x, self.y] + self.rest + self.far + [over_core(v) for v in rest]


def block_sums(name, outs):
    terms = [t for ts, _, _ in outs for t in ts]
    tail = terms[0][0].shape[1:]

    def kernel(*refs):
        ins, res = refs[: len(terms)], refs[len(terms) :]
        k = 0
        for (ts, count, dtype), out in zip(outs, res):
            for i in range(count):
                acc = None
                for j, (_, blocks, _, first) in enumerate(ts):
                    if first <= i < first + blocks:
                        v = ins[k + j][i - first].astype(F32)
                        acc = v if acc is None else acc + v
                out[i] = acc.astype(dtype)
            k += len(ts)

    def spec(blocks, index):
        return pl.BlockSpec((blocks,) + tail, lambda i: (index, 0, 0))

    return pl.pallas_call(
        kernel,
        name=name,
        grid=(1,),
        in_specs=[spec(blocks, index) for _, blocks, index, _ in terms],
        out_specs=[pl.BlockSpec((count,) + tail, lambda i: (0, 0, 0)) for _, count, _ in outs],
        out_shape=[jax.ShapeDtypeStruct((count,) + tail, dt) for _, count, dt in outs],
        compiler_params=pltpu.CompilerParams(vmem_limit_bytes=24 * 2**20),
        cost_estimate=pl.CostEstimate(flops=10**8, bytes_accessed=10**5, transcendentals=0),
    )(*[t[0] for t in terms])


class Reduce:
    def __init__(self, parts, n, name, shifts=False):
        self.near, self.far = parts
        self.shifts = shifts
        self.n, self.name = n, name
        self.size = self.near.shape[0] // 4

    def stage_core(self, *deps):
        self.got = over_core(after(self.far, *deps))
        return [self.got]

    def stage_rest(self, *deps):
        h = self.size // 2
        self.got = after(self.got, *deps)
        lo, hi = block_sums(
            self.name + "_rest",
            [([(v, h, k, 0) for v in (self.near, self.got)], h, B16) for k in (6, 7)],
        )
        self.sent = [lo, hi]
        self.rest = [over_y(lo), over_x(hi)]
        return self.rest

    def stage_xy(self, *deps):
        size, h = self.size, self.size // 2
        lo, hi = after(tuple(self.rest), *deps)
        both = (self.near, self.got)
        sx, sy = block_sums(
            self.name + "_xy",
            [
                ([(v, size, 1, 0) for v in both] + [(lo, h, 0, 0)], size, B16),
                ([(v, size, 2, 0) for v in both] + [(hi, h, 0, h)], size, B16),
            ],
        )
        self.sent = [sx, sy]
        self.xy = [over_x(sx), over_y(sy)]
        return self.xy

    def stage_z(self, *deps):
        rx, ry = after(tuple(self.xy), *deps)
        all_four = (self.near, self.got, rx, ry)
        if self.shifts:
            own, *self.sent = block_sums(
                self.name + "_z",
                [
                    ([(v, 1, d, 0) for v in all_four], 1, B16 if d else F32)
                    for d in range(self.n)
                ],
            )
            self.z = [own] + [
                lax.ppermute(v, "shard", [(i, (i + d) % self.n) for i in range(self.n)])
                for d, v in enumerate(self.sent, 1)
            ]
            return self.z[1:]
        self.sent = block_sums(
            self.name + "_z", [([(v, self.size, 0, 0) for v in all_four], self.size, B16)]
        )
        v = self.sent[0]
        self.z = over_z(v.reshape((self.n, self.size // self.n) + v.shape[1:]))
        return [self.z]

    def results(self, *deps):
        if self.shifts:
            z = after(tuple(self.z), *deps)
            return [functools.reduce(lambda a, b: a + b, [v[0].astype(F32) for v in z])]
        z = jnp.sum(after(self.z, *deps).astype(F32), axis=0)
        return [z[k] for k in range(z.shape[0])]


EVERY = ("x", "core", "shard", "ctx")


def gather_whole(own):
    return lax.all_gather(own, EVERY, axis=0, tiled=False)


def reduce_whole(parts):
    return lax.psum_scatter(parts, EVERY, scatter_dimension=0, tiled=False).astype(F32)


class GatherWhole:
    sent = ()

    def __init__(self, owns, n, shifts=False):
        d = owns[0].shape[1]
        self.out = [gather_whole(v).reshape(4, d, d) for v in owns]

    def stage_z(self, *deps):
        return []

    stage_xy = stage_rest = stage_z

    def stage_core(self, *deps):
        return self.out


class ReduceWhole:
    sent = ()

    def __init__(self, parts, n, name, shifts=False):
        self.parts = parts

    def stage_z(self, *deps):
        return []

    stage_core = stage_rest = stage_xy = stage_z

    def results(self, *deps):
        rows = self.parts[0].shape[1] // (2 * lax.axis_size("shard"))
        return [reduce_whole(p.reshape(-1, rows, p.shape[2]).astype(F32)) for p in self.parts]


def dot(a, b):
    return jnp.dot(a, b, preferred_element_type=F32)


def dot_nt(a, b):
    return lax.dot_general(a, b, NT_DIMS, preferred_element_type=F32)


def dot_tn(a, b):
    return lax.dot_general(a, b, TN_DIMS, preferred_element_type=F32)


def low_lanes(shape):
    return lax.broadcasted_iota(jnp.int32, shape, 1) % 128 < 64


def keep_low(v):
    return jnp.where(low_lanes(v.shape), v, jnp.zeros_like(v))


def keep_high(v):
    return jnp.where(low_lanes(v.shape), jnp.zeros_like(v), v)


def swap_halves(v):
    return jnp.concatenate([v[:, 64:], v[:, :64]], axis=1)


def norm_parts(x):
    centred = x - jnp.mean(x, axis=-1, keepdims=True)
    rstd = lax.rsqrt(jnp.mean(centred * centred, axis=-1, keepdims=True) + EPSILON)
    return centred * rstd, rstd


def norm_back(x, gain, up):
    unit, rstd = norm_parts(x)
    w = up * gain
    inner = jnp.mean(w * unit, axis=-1, keepdims=True)
    down = rstd * (w - jnp.mean(w, axis=-1, keepdims=True) - unit * inner)
    return down, jnp.sum(up * unit, axis=0, keepdims=True), jnp.sum(up, axis=0, keepdims=True)


def weight_copies(meta, bufs, w_refs, sems, n, back=False, shifts=False):
    moves = []
    if bufs[0].shape == w_refs[0].shape:
        moves = list(zip(bufs, w_refs))
    else:
        x, y, c = meta[0], meta[1], meta[2]
        rows = bufs[0].shape[1]
        for dc in range(2):
            first = 0
            for k, (dx, dy, blocks) in enumerate(layout(len(w_refs), n)):
                tp = 2 * (x ^ dx) + (c ^ dc)
                for i, (z, chunk) in enumerate(blocks):
                    if shifts:
                        z = lax.rem(meta[3] + z, n)
                    row = pl.multiple_of((z * 2 + (y ^ dy)) * rows, rows)
                    piece = bufs[dc].at[first + i] if back else bufs[dc * 5 + k].at[i]
                    moves.append((piece, w_refs[chunk].at[tp, pl.ds(row, rows), :]))
                first += len(blocks)
    if back:
        moves = [(whole, piece) for piece, whole in moves]
    return [pltpu.make_async_copy(*m, sems.at[i]) for i, m in enumerate(moves)]


def copy_sems(sz, chunks):
    return pltpu.SemaphoreType.DMA((8 * chunks * sz["n"],))


def start_all(copies):
    for c in copies:
        c.start()


def wait_all(copies):
    for c in copies:
        c.wait()


def take_blocks(blocks, dst, places):
    for k, blk in enumerate(blocks):
        dx, dy = k % 2, k // 2
        for f in range(2):
            row = (2 * dx + f) * 2 * PAD + dy * PAD
            dst[row + PAD - 8 : row + PAD, :] = jnp.zeros((8, dst.shape[1]), dst.dtype)
            dst[row : row + places, :] = blk[f].astype(dst.dtype)


def give_blocks(src, blocks, places):
    for k, blk in enumerate(blocks):
        dx, dy = k % 2, k // 2
        for f in range(2):
            row = (2 * dx + f) * 2 * PAD + dy * PAD
            blk[f] = src[row : row + places, :].astype(blk.dtype)


def project_heads(normed, w_ref, q_out, kv_out, rows, step):
    @pl.loop(0, 2)
    def _(u):
        @pl.loop(0, rows // step)
        def _(r):
            at = pl.ds(pl.multiple_of(r * step, step), step)
            xn = normed[at, :]
            thirds = []
            for t in (2 * u, 2 * u + 1):
                y = dot(xn, w_ref[t, :, 0:512]).astype(B16)
                q_out[t, at, :] = y[:, 0:128]
                kv_out[t, at, :] = y[:, 128:256]
                kv_out[6 + t, at, :] = y[:, 256:384]
                thirds.append((y[:, 384:512], dot(xn, w_ref[t, :, 640:768]).astype(B16)))
            (a3, a5), (b3, b5) = thirds
            low = low_lanes(a3.shape)
            q_out[4 + u, at, :] = jnp.where(low, a3, b3)
            kv_out[4 + u, at, :] = swap_halves(jnp.where(low, b3, a3))
            kv_out[10 + u, at, :] = swap_halves(jnp.where(low, b5, a5))


def third_head(v, t):
    return keep_low(v) if t % 2 == 0 else keep_high(v)


def project_out(mixed, w_ref, stream, bias, out, rows, step):
    @pl.loop(0, rows // step)
    def _(r):
        at = pl.ds(pl.multiple_of(r * step, step), step)
        acc = stream[at, :] + bias
        for t in range(4):
            m = jnp.concatenate([mixed[t, at, :], third_head(mixed[4 + t // 2, at, :], t)], axis=1)
            acc = acc + dot_nt(m, w_ref[t, :, 512:768])
        out[at, :] = acc


def run(kernel, name, ins, outs, scratch, micros):
    space = {
        "v": pl.BlockSpec(memory_space=pltpu.VMEM),
        "s": pl.BlockSpec(memory_space=pltpu.SMEM),
        "a": pl.BlockSpec(memory_space=pl.ANY),
    }
    return pl.pallas_call(
        kernel,
        name=name,
        in_specs=[space[s] for _, s in ins],
        out_specs=[space[s] for _, _, s in outs],
        out_shape=[jax.ShapeDtypeStruct(s, d) for s, d, _ in outs],
        scratch_shapes=scratch,
        compiler_params=pltpu.CompilerParams(vmem_limit_bytes=VMEM_LIMIT),
        cost_estimate=pl.CostEstimate(
            flops=micros * 10**9, bytes_accessed=micros * 3 * 10**6, transcendentals=0
        ),
    )(*[a for a, _ in ins])


def row_slices(r, step=208):
    return pl.ds(pl.multiple_of(r * step, step), step)


def time_qkv(sz, meta, vec, blocks, weights):
    rows, d = sz["rows"], sz["d"]
    nb, nw = len(blocks), len(weights)

    def kernel(*refs):
        meta, vec = refs[0], refs[1]
        blks, bufs = refs[2 : 2 + nb], refs[2 + nb : 2 + nb + nw]
        x, normed, q, kv, w, sems = refs[2 + nb + nw :]
        copies = weight_copies(meta, bufs, [w], sems, sz["n"], shifts=True)
        start_all(copies)
        take_blocks(blks, x, sz["places"])

        @pl.loop(0, 4)
        def _(r):
            at = row_slices(r)
            unit, _ = norm_parts(x[at, :])
            normed[at, :] = (unit * vec[0:1, :] + vec[1:2, :]).astype(B16)

        wait_all(copies)
        project_heads(normed, w, q, kv, rows, 416)

    ins = [(meta, "s"), (vec, "v")] + [(b, "v") for b in blocks] + [(w, "a") for w in weights]
    outs = [
        ((rows, d), F32, "v"),
        ((rows, d), B16, "v"),
        ((6, rows, 128), B16, "v"),
        ((12, rows, 128), B16, "v"),
    ]
    scratch = [pltpu.VMEM((4, d, d), B16), copy_sems(sz, 1)]
    return run(kernel, "time_qkv", ins, outs, scratch, 12)


def head_sums(ref):
    for f in range(4):
        for j in range(6):
            col = lax.broadcasted_iota(jnp.int32, (128, 128), 1)
            lane = lax.broadcasted_iota(jnp.int32, (128, 128), 0)
            hit = col == 16 * f + 2 * j + lane // 64
            ref[(f * 6 + j) * 128 : (f * 6 + j) * 128 + 128, :] = hit.astype(F32).astype(B16)


def head_spreads(ref):
    for f in range(4):
        for j in range(6):
            row = lax.broadcasted_iota(jnp.int32, (128, 128), 0)
            lane = lax.broadcasted_iota(jnp.int32, (128, 128), 1)
            hit = row == 16 * f + 2 * j + lane // 64
            ref[:, (f * 6 + j) * 128 : (f * 6 + j) * 128 + 128] = hit.astype(F32).astype(B16)


def pair_sums(a_ref, b_ref, b_tile, g, sums):
    at = row_slices(g)
    products = [
        a_ref[j, f * 208 : f * 208 + 208, :] * b_ref[b_tile + j, at, :]
        for f in range(4)
        for j in range(6)
    ]
    return dot(jnp.concatenate(products, axis=1), sums[...])


def two_tiles(ref, tile, at):
    return jnp.concatenate([ref[tile, at, :], ref[tile + 1, at, :]], axis=1).astype(F32)


def time_mix(sz, meta, vec, stream, q, kv, kvo, weights):
    rows, d = sz["rows"], sz["d"]
    nw = len(weights)

    def kernel(*refs):
        meta, vec, stream, q, kv, kvo = refs[:6]
        bufs = refs[6 : 6 + nw]
        mixed, out, prob, w, sums, spreads, acc, sems = refs[6 + nw :]
        copies = weight_copies(meta, bufs, [w], sems, sz["n"], shifts=True)
        start_all(copies)
        head_sums(sums)
        head_spreads(spreads)
        for h, ref in enumerate((kv, kvo)):

            @pl.loop(0, 4)
            def _(g):
                prob[4 * h + g] = pair_sums(q, ref, 0, g, sums) * SCALING

        @pl.loop(0, 13)
        def _(r):
            at = row_slices(r, 16)
            s = [prob[g, at, :] for g in range(8)]
            top = functools.reduce(jnp.maximum, s)
            e = [jnp.exp(v - top) for v in s]
            inv = 1.0 / functools.reduce(lambda a, b: a + b, e)
            for g in range(8):
                prob[g, at, :] = e[g] * inv

        acc[...] = jnp.zeros_like(acc)
        for h, ref in enumerate((kv, kvo)):

            @pl.loop(0, 4)
            def _(g):
                at = row_slices(g)
                p = prob[4 * h + g].astype(B16)
                for jj in range(3):
                    v = two_tiles(ref, 6 + 2 * jj, at)
                    for f in range(4):
                        lanes = slice(f * d + 256 * jj, f * d + 256 * jj + 256)
                        acc[f * 208 : f * 208 + 208, 256 * jj : 256 * jj + 256] += (
                            dot(p, spreads[:, lanes]) * v
                        )

        for j in range(6):
            mixed[j] = acc[:, 128 * j : 128 * j + 128].astype(B16)
        wait_all(copies)
        project_out(mixed, w, stream, vec[2:3, :], out, rows, 416)

    ins = [(meta, "s"), (vec, "v"), (stream, "v"), (q, "v"), (kv, "v"), (kvo, "v")]
    ins += [(w, "a") for w in weights]
    outs = [((6, rows, 128), B16, "v"), ((rows, d), F32, "v"), ((8, 208, 128), F32, "v")]
    scratch = [
        pltpu.VMEM((4, d, d), B16),
        pltpu.VMEM((4 * d, 128), B16),
        pltpu.VMEM((128, 4 * d), B16),
        pltpu.VMEM((rows, d), F32),
        copy_sems(sz, 1),
    ]
    return run(kernel, "time_mix", ins, outs, scratch, 17)


def space_mask(places):
    return lax.broadcasted_iota(jnp.int32, (208, 208), 0) % PAD < places


def space_forward(sz, meta, vec, stream, weights):
    rows, d, places = sz["rows"], sz["d"], sz["places"]
    nw = len(weights)

    def kernel(*refs):
        meta, vec, stream = refs[:3]
        bufs = refs[3 : 3 + nw]
        normed, q, kv, mixed, logs, out, w, sems = refs[3 + nw :]
        copies = weight_copies(meta, bufs, [w], sems, sz["n"])
        start_all(copies)

        @pl.loop(0, 4)
        def _(r):
            at = row_slices(r)
            unit, _ = norm_parts(stream[at, :])
            normed[at, :] = (unit * vec[3:4, :] + vec[4:5, :]).astype(B16)

        wait_all(copies)
        project_heads(normed, w, q, kv, rows, 416)

        @pl.loop(0, 6)
        def _(j):
            @pl.loop(0, 4)
            def _(f):
                at = row_slices(f)
                qj, kj, vj = q[j, at, :], kv[j, at, :], kv[6 + j, at, :]
                mask = space_mask(places)
                o = None
                for h, keep in enumerate((keep_low, keep_high)):
                    s = jnp.where(mask, dot_nt(kj, keep(qj)) * SCALING, NEGATIVE)
                    top = jnp.max(s, axis=0, keepdims=True)
                    e = jnp.exp(s - top)
                    size = jnp.sum(e, axis=0, keepdims=True)
                    logs[j * 4 + f, h : h + 1, :] = top + jnp.log(size)
                    part = dot_tn((e * (1.0 / size)).astype(B16), keep(vj))
                    o = part if o is None else o + part
                mixed[j, at, :] = o.astype(B16)

        project_out(mixed, w, stream, vec[5:6, :], out, rows, 416)

    ins = [(meta, "s"), (vec, "v"), (stream, "v")] + [(w, "a") for w in weights]
    outs = [
        ((rows, d), B16, "v"),
        ((6, rows, 128), B16, "v"),
        ((12, rows, 128), B16, "v"),
        ((6, rows, 128), B16, "v"),
        ((24, 8, 208), F32, "v"),
        ((rows, d), F32, "v"),
    ]
    scratch = [pltpu.VMEM((4, d, d), B16), copy_sems(sz, 1)]
    return run(kernel, "space_forward", ins, outs, scratch, 29)


def gradient_outs(sz, chunks, fast):
    d, n = sz["d"], sz["n"]
    if not fast:
        return [((4, d, d), B16, "a")] * chunks
    return [((4 * chunks * n, d // (2 * n), d), B16, "a")] * 2


def transpose_into(src, dst):
    for j in range(src.shape[1] // 128):
        dst[128 * j : 128 * j + 128, :] = src[:, 128 * j : 128 * j + 128].T


def gelu_pair(x):
    half = 0.5 * (1.0 + lax.erf(x * 0.7071067811865476))
    slope = half + x * (0.3989422804014327 * jnp.exp(-0.5 * x * x))
    return x * half, slope


def feed_forward(sz, meta, vec, stream, blocks, weights, fast):
    rows, d, places = sz["rows"], sz["d"], sz["places"]
    nb, nw = len(blocks), len(weights)
    g_outs = gradient_outs(sz, 2, fast)
    ng = len(g_outs)

    def kernel(*refs):
        meta, vec, stream = refs[:3]
        blks = refs[3 : 3 + nb]
        refs = refs[3 + nb :]
        bufs, refs = refs[:nw], refs[nw:]
        res, refs = refs[:nb], refs[nb:]
        d2, vgrad = refs[0], refs[1]
        g_bufs, refs = refs[2 : 2 + ng], refs[2 + ng :]
        w1, w2, dw1, dw2, dz, dzr, normed, normed_t, dzr_t, act, dpre, y, dn, sems = refs
        copies = weight_copies(meta, bufs, [w1, w2], sems, sz["n"])
        start_all(copies)
        take_blocks(blks, dz, places)
        vgrad[...] = jnp.zeros_like(vgrad)

        @pl.loop(0, 4)
        def _(r):
            at = pl.ds(pl.multiple_of(r * 208, 208), 208)
            unit, _ = norm_parts(stream[at, :])
            normed[at, :] = (unit * vec[6:7, :] + vec[7:8, :]).astype(B16)
            up = dz[at, :]
            dzr[at, :] = up.astype(B16)
            vgrad[2:3, :] += jnp.sum(up, axis=0, keepdims=True)
            y[at, :] = stream[at, :] + vec[8:9, :]
            dn[at, :] = jnp.zeros_like(up)

        transpose_into(normed, normed_t)
        transpose_into(dzr, dzr_t)
        wait_all(copies)

        @pl.loop(0, 4)
        def _(t):
            @pl.loop(0, rows // 208)
            def _(r):
                at = pl.ds(pl.multiple_of(r * 208, 208), 208)
                pre = dot(normed[at, :], w1[t]) + vec[pl.ds(9 + t, 1), :]
                a, slope = gelu_pair(pre)
                a = a.astype(B16)
                act[at, :] = a
                y[at, :] += dot_nt(a, w2[t])
                g = (dot(dzr[at, :], w2[t]) * slope).astype(B16)
                dpre[at, :] = g
                vgrad[pl.ds(4 + t, 1), :] += jnp.sum(g.astype(F32), axis=0, keepdims=True)
                dn[at, :] += dot_nt(g, w1[t])

            @pl.loop(0, d // 256)
            def _(m):
                at = pl.ds(pl.multiple_of(m * 256, 256), 256)
                dw1[t, at, :] = dot(normed_t[at, :], dpre[...]).astype(B16)
                dw2[t, at, :] = dot(dzr_t[at, :], act[...]).astype(B16)

        back = weight_copies(meta, g_bufs, [dw1, dw2], sems, sz["n"], back=True)
        start_all(back)
        give_blocks(y, res, places)

        @pl.loop(0, 4)
        def _(r):
            at = pl.ds(pl.multiple_of(r * 208, 208), 208)
            down, gg, gs = norm_back(stream[at, :], vec[6:7, :], dn[at, :])
            d2[at, :] = dz[at, :] + down
            vgrad[0:1, :] += gg
            vgrad[1:2, :] += gs

        wait_all(back)

    ins = [(meta, "s"), (vec, "v"), (stream, "v")] + [(b, "v") for b in blocks]
    ins += [(w, "a") for w in weights]
    outs = [((2, places, d), B16, "v")] * nb + [((rows, d), F32, "v"), ((8, d), F32, "v")]
    outs += g_outs
    scratch = [pltpu.VMEM((4, d, d), B16)] * 4
    scratch += [pltpu.VMEM((rows, d), F32), pltpu.VMEM((rows, d), B16), pltpu.VMEM((rows, d), B16)]
    scratch += [pltpu.VMEM((d, rows), B16)] * 2 + [pltpu.VMEM((rows, d), B16)] * 2
    scratch += [pltpu.VMEM((rows, d), F32)] * 2
    scratch += [copy_sems(sz, 2)]
    r = run(kernel, "feed_forward", ins, outs, scratch, 47)
    return r[:nb], r[nb], r[nb + 1], r[nb + 2 :]


def mixed_slopes(up, w_ref, dm, rows, step):
    @pl.loop(0, 2)
    def _(u):
        @pl.loop(0, rows // step)
        def _(r):
            at = pl.ds(pl.multiple_of(r * step, step), step)
            thirds = []
            for t in (2 * u, 2 * u + 1):
                v = dot(up[at, :], w_ref[t, :, 512:768]).astype(B16)
                dm[t, at, :] = v[:, 0:128]
                thirds.append(v[:, 128:256])
            dm[4 + u, at, :] = jnp.where(low_lanes(thirds[0].shape), *thirds)


def place_third(dq, dk, dv, dy, u, at):
    k, v = swap_halves(dk), swap_halves(dv)
    low = low_lanes(dq.shape)
    dy[2 * u, at, 384:512] = jnp.where(low, dq, k)
    dy[2 * u + 1, at, 384:512] = jnp.where(low, k, dq)
    dy[2 * u, at, 512:640] = keep_high(v)
    dy[2 * u + 1, at, 512:640] = keep_low(v)


def head_gradients(dw, normed_t, up_t, dy, mixed, d):
    @pl.loop(0, 2)
    def _(u):
        @pl.loop(0, d // 256)
        def _(m):
            at = pl.ds(pl.multiple_of(m * 256, 256), 256)
            nt, ut = normed_t[at, :], up_t[at, :]
            for odd in range(2):
                t = 2 * u + odd
                g = dot(nt, dy[t])
                dw[t, at, 0:512] = g[:, 0:512].astype(B16)
                m2 = jnp.concatenate([mixed[t], third_head(mixed[4 + u], odd)], axis=1)
                out = dot(ut, m2)
                dw[t, at, 512:640] = out[:, 0:128].astype(B16)
                dw[t, at, 640:768] = (out[:, 128:256] + g[:, 512:640]).astype(B16)


def norm_slopes(at, dy, w_ref):
    up = None
    for t in range(4):
        part = dot_nt(dy[t, at, 0:512], w_ref[t, :, 0:512]) + dot_nt(
            dy[t, at, 512:640], w_ref[t, :, 640:768]
        )
        up = part if up is None else up + part
    return up


def space_backward_scores(sz, meta, d2, q, kv, logs, weights):
    rows, d, places = sz["rows"], sz["d"], sz["places"]
    nw = len(weights)

    def kernel(*refs):
        meta, d2, q, kv, logs = refs[:5]
        bufs, refs = refs[5 : 5 + nw], refs[5 + nw :]
        up, dy, w, dm, third, sems = refs
        copies = weight_copies(meta, bufs, [w], sems, sz["n"])
        start_all(copies)

        @pl.loop(0, 4)
        def _(r):
            up[row_slices(r), :] = d2[row_slices(r), :].astype(B16)

        wait_all(copies)
        mixed_slopes(up, w, dm, rows, 416)

        def slopes(j, at, f):
            qj, kj, vj, mj = q[j, at, :], kv[j, at, :], kv[6 + j, at, :], dm[j, at, :]
            mask = space_mask(places)
            dq = dk = dv = None
            for h, keep in enumerate((keep_low, keep_high)):
                qh, mh = keep(qj), keep(mj)
                s = dot_nt(kj, qh) * SCALING - logs[j * 4 + f, h : h + 1, :]
                p = jnp.exp(jnp.where(mask, s, NEGATIVE))
                dp = dot_nt(vj, mh)
                inner = jnp.sum(p * dp, axis=0, keepdims=True)
                ds = (p * (dp - inner) * SCALING).astype(B16)
                a, b, c = dot_tn(ds, keep(kj)), dot(ds, qh), dot(p.astype(B16), mh)
                dq, dk, dv = (a, b, c) if dq is None else (dq + a, dk + b, dv + c)
            return dq.astype(B16), dk.astype(B16), dv.astype(B16)

        @pl.loop(0, 4)
        def _(j):
            @pl.loop(0, 4)
            def _(f):
                at = row_slices(f)
                dq, dk, dv = slopes(j, at, f)
                dy[j, at, 0:128] = dq
                dy[j, at, 128:256] = dk
                dy[j, at, 256:384] = dv

        @pl.loop(0, 2)
        def _(u):
            @pl.loop(0, 4)
            def _(f):
                at = row_slices(f)
                place_third(*slopes(4 + u, at, f), dy, u, at)

    ins = [(meta, "s")] + [(v, "v") for v in (d2, q, kv, logs)] + [(w, "a") for w in weights]
    outs = [((rows, d), B16, "v"), ((4, rows, 640), B16, "v")]
    scratch = [pltpu.VMEM((4, d, d), B16), pltpu.VMEM((6, rows, 128), B16)]
    scratch += [pltpu.VMEM((rows, 128), B16), copy_sems(sz, 1)]
    return run(kernel, "space_backward_scores", ins, outs, scratch, 30)


def weight_slopes(sz, name, meta, up, normed, mixed, slopes, fast):
    rows, d = sz["rows"], sz["d"]
    g_outs = gradient_outs(sz, 1, fast)
    join = len(slopes) == 3

    def kernel(*refs):
        meta, up, normed, mixed = refs[:4]
        given, refs = refs[4 : 4 + len(slopes)], refs[4 + len(slopes) :]
        dy = refs[0] if join else given[0]
        g_bufs, (dw, up_t, normed_t, sems) = refs[1 if join else 0 : -4], refs[-4:]
        if join:
            dq, dkv, got = given

            def both(j, at):
                return (dkv[j, at, :].astype(F32) + got[j, at, :].astype(F32)).astype(B16)

            @pl.loop(0, 4)
            def _(r):
                at = row_slices(r)
                for j in range(4):
                    dy[j, at, 0:128] = dq[j, at, :]
                    dy[j, at, 128:256] = both(j, at)
                    dy[j, at, 256:384] = both(6 + j, at)
                for u in range(2):
                    place_third(dq[4 + u, at, :], both(4 + u, at), both(10 + u, at), dy, u, at)

        transpose_into(normed, normed_t)
        transpose_into(up, up_t)
        head_gradients(dw, normed_t, up_t, dy, mixed, d)
        back = weight_copies(meta, g_bufs, [dw], sems, sz["n"], back=True, shifts=join)
        start_all(back)
        wait_all(back)

    ins = [(meta, "s")] + [(v, "v") for v in (up, normed, mixed, *slopes)]
    outs = ([((4, rows, 640), B16, "v")] if join else []) + g_outs
    scratch = [pltpu.VMEM((4, d, d), B16)] + [pltpu.VMEM((d, rows), B16)] * 2
    scratch += [copy_sems(sz, 1)]
    return run(kernel, name, ins, outs, scratch, 14)


def input_slopes(sz, name, meta, vec, up, stream, dy, weights, gain_row, blocks):
    rows, d, places = sz["rows"], sz["d"], sz["places"]
    nw = len(weights)

    def kernel(*refs):
        meta, vec, up, stream, dy = refs[:5]
        bufs, refs = refs[5 : 5 + nw], refs[5 + nw :]
        outs, vgrad, w, sems = refs[:-3], refs[-3], refs[-2], refs[-1]
        if blocks:
            outs, vgrad, dx, w, sems = refs[:4], refs[4], refs[5], refs[6], refs[7]
        else:
            dx = outs[0]
        copies = weight_copies(meta, bufs, [w], sems, sz["n"], shifts=bool(blocks))
        start_all(copies)
        vgrad[...] = jnp.zeros_like(vgrad)
        wait_all(copies)

        @pl.loop(0, 4)
        def _(r):
            at = row_slices(r)
            v = up[at, :]
            gain = vec[gain_row : gain_row + 1, :]
            down, gg, gs = norm_back(stream[at, :], gain, norm_slopes(at, dy, w))
            dx[at, :] = v + down
            vgrad[0:1, :] += gg
            vgrad[1:2, :] += gs
            vgrad[2:3, :] += jnp.sum(v, axis=0, keepdims=True)

        if blocks:
            give_blocks(dx, outs, places)

    ins = [(meta, "s")] + [(v, "v") for v in (vec, up, stream, dy)] + [(w, "a") for w in weights]
    outs = [((rows, d), F32, "v")]
    scratch = []
    if blocks:
        outs = [((2, places, d), F32, "v")] + [((2, places, d), B16, "v")] * 3
        scratch = [pltpu.VMEM((rows, d), F32)]
    outs += [((8, d), F32, "v")]
    scratch += [pltpu.VMEM((4, d, d), B16), copy_sems(sz, 1)]
    return run(kernel, name, ins, outs, scratch, 14)


def time_backward_scores(sz, meta, d1, q, kv, kvo, prob, weights):
    rows, d = sz["rows"], sz["d"]
    nw = len(weights)

    def kernel(*refs):
        meta, d1, q, kv, kvo, prob = refs[:6]
        bufs, refs = refs[6 : 6 + nw], refs[6 + nw :]
        up, dq, dkv, dkvo, w, dm, sums, spreads, ds, acc, sems = refs
        copies = weight_copies(meta, bufs, [w], sems, sz["n"], shifts=True)
        start_all(copies)
        head_sums(sums)
        head_spreads(spreads)

        @pl.loop(0, 4)
        def _(r):
            up[row_slices(r), :] = d1[row_slices(r), :].astype(B16)

        wait_all(copies)
        mixed_slopes(up, w, dm, rows, 416)
        for h, ref in enumerate((kv, kvo)):

            @pl.loop(0, 4)
            def _(g):
                ds[4 * h + g] = pair_sums(dm, ref, 6, g, sums)

        @pl.loop(0, 13)
        def _(r):
            at = row_slices(r, 16)
            p = [prob[g, at, :] for g in range(8)]
            dp = [ds[g, at, :] for g in range(8)]
            inner = functools.reduce(lambda a, b: a + b, [a * b for a, b in zip(p, dp)])
            for g in range(8):
                ds[g, at, :] = p[g] * (dp[g] - inner) * SCALING

        acc[...] = jnp.zeros_like(acc)
        for h, (ref, out) in enumerate(((kv, dkv), (kvo, dkvo))):

            @pl.loop(0, 4)
            def _(g):
                at = row_slices(g)
                both = jnp.concatenate([ds[4 * h + g], prob[4 * h + g]], axis=0).astype(B16)
                for jj in range(3):
                    k = two_tiles(ref, 2 * jj, at)
                    dk = dv = None
                    for f in range(4):
                        fr = slice(f * 208, f * 208 + 208)
                        e = dot(both, spreads[:, f * d + 256 * jj : f * d + 256 * jj + 256])
                        se, pe = e[:208], e[208:]
                        acc[fr, 256 * jj : 256 * jj + 256] += se * k
                        a = se * two_tiles(q, 2 * jj, fr)
                        b = pe * two_tiles(dm, 2 * jj, fr)
                        dk, dv = (a, b) if dk is None else (dk + a, dv + b)
                    dk, dv = dk.astype(B16), dv.astype(B16)
                    for i in range(2):
                        out[2 * jj + i, at, :] = dk[:, 128 * i : 128 * i + 128]
                        out[6 + 2 * jj + i, at, :] = dv[:, 128 * i : 128 * i + 128]

        for j in range(6):
            dq[j] = acc[:, 128 * j : 128 * j + 128].astype(B16)

    ins = [(meta, "s")] + [(v, "v") for v in (d1, q, kv, kvo, prob)] + [(w, "a") for w in weights]
    outs = [
        ((rows, d), B16, "v"),
        ((6, rows, 128), B16, "v"),
        ((12, rows, 128), B16, "v"),
        ((12, rows, 128), B16, "v"),
    ]
    scratch = [
        pltpu.VMEM((4, d, d), B16),
        pltpu.VMEM((6, rows, 128), B16),
        pltpu.VMEM((4 * d, 128), B16),
        pltpu.VMEM((128, 4 * d), B16),
        pltpu.VMEM((8, 208, 128), F32),
        pltpu.VMEM((rows, d), F32),
        copy_sems(sz, 1),
    ]
    return run(kernel, "time_backward_scores", ins, outs, scratch, 23)


def pack_heads(qkv, proj, odd):
    q, k, v = qkv[:, 0], qkv[:, 1], qkv[:, 2]
    o = proj.T
    first = [q[:, :128], k[:, :128], v[:, :128]]
    even = first + [q[:, 128:], k[:, 128:], o[:, :128], o[:, 128:], v[:, 128:]]
    other = first + [k[:, 128:], q[:, 128:], o[:, :128], v[:, 128:], o[:, 128:]]
    return jnp.where(odd, jnp.concatenate(other, axis=1), jnp.concatenate(even, axis=1))


def unpack_heads(g, odd):
    def pick(a, b):
        return jnp.where(odd, g[:, b : b + 64], g[:, a : a + 64])

    q = jnp.concatenate([g[:, 0:128], pick(384, 448)], axis=1)
    k = jnp.concatenate([g[:, 128:256], pick(448, 384)], axis=1)
    v = jnp.concatenate([g[:, 256:384], pick(704, 640)], axis=1)
    o = jnp.concatenate([g[:, 512:640], pick(640, 704)], axis=1)
    return jnp.stack([q, k, v], axis=1), o.T


def local(mesh_shape, video, cotangent, *params):
    qkv_time, proj_time, qkv_space, proj_space, fc_in, fc_out = params[:6]
    vectors = params[6:]
    n = mesh_shape["shard"]
    d = proj_time.shape[0] * 4
    places = video.shape[2]
    rows_here = fc_in.shape[0]
    fast = rows_here % 16 == 0
    sz = {"n": n, "d": d, "places": places, "rows": 8 * PAD}
    x, y = lax.axis_index("x"), lax.axis_index("ctx")
    c, z = lax.axis_index("core"), lax.axis_index("shard")
    meta = jnp.stack([x, y, c, z]).astype(jnp.int32)
    every = ("shard", "ctx", "x", "core")
    count = 8 * n

    share = jnp.concatenate([v.reshape(1, -1) for v in vectors], axis=1)
    share = jnp.broadcast_to(share, (count, share.shape[1]))
    shares = lax.all_to_all(share, every, split_axis=0, concat_axis=0, tiled=True)
    per = d // count
    order = [0, 1, 2, 3, 4, 5, 6, 7, 9]
    starts = [per * i for i in range(9)] + [per * 12]
    vec = jnp.stack([shares[:, starts[i] : starts[i] + per].reshape(d) for i in order])
    hidden = shares[:, starts[8] : starts[8] + 4 * per].reshape(4, d)
    vec = jnp.concatenate([vec, hidden, jnp.zeros((3, d), F32)], axis=0)

    def clips_of(v):
        return [
            lax.dynamic_index_in_dim(v, 2 * (x ^ dx) + (y ^ dy), 0, keepdims=False)
            for dx, dy in ((0, 0), (1, 0), (0, 1), (1, 1))
        ]

    def frames_back(blocks):
        return [blocks[0], over_x(blocks[1]), over_y(blocks[2]), over_xy(blocks[3])]

    def join_clips(blocks, dtype):
        out = jnp.zeros((4,) + blocks[0].shape, dtype)
        for k, b in enumerate(blocks):
            at = 2 * (x ^ (k % 2)) + (y ^ (k // 2))
            out = lax.dynamic_update_slice_in_dim(out, b.astype(dtype)[None], at, 0)
        return out

    gather, reduce = (Gather, Reduce) if fast else (GatherWhole, ReduceWhole)

    g_t = gather([pack_heads(qkv_time, proj_time, c == 1)], n, True)
    g_s = gather([pack_heads(qkv_space, proj_space, c == 1)], n)
    g_m = gather([fc_in, fc_out.T], n)
    t_z = g_t.stage_z()
    clips = clips_of(video)
    video_blocks = [clips[0], over_x(clips[1]), over_y(clips[2])]
    t_xy = g_t.stage_xy(*video_blocks[1:])
    video_blocks.append(over_xy(after(clips[3], *t_z)))
    s_z = g_s.stage_z(vec)
    t_rest = g_t.stage_rest(*s_z)
    s_xy = g_s.stage_xy(*t_rest)
    m_z = g_m.stage_z(*s_z)
    w_time = g_t.stage_core()
    cot_sent = clips_of(after(cotangent, *t_xy))
    vec_t = after(vec, *g_s.sent, *cot_sent)
    stream0, normed_t, q_t, kv_t = time_qkv(sz, meta, vec_t, video_blocks, w_time)

    kv_o = over_core(after(kv_t, *s_xy))
    s_rest = g_s.stage_rest(kv_t)
    cot_blocks = frames_back(after(tuple(cot_sent), kv_t))
    kv_o = after(kv_o, *g_s.sent)
    mixed_t, stream1, prob_t = time_mix(sz, meta, vec, stream0, q_t, kv_t, kv_o, w_time)

    w_space = g_s.stage_core(stream1)
    m_xy = g_m.stage_xy(stream1)
    stream1s = after(stream1, *g_m.sent, *cot_blocks)
    normed_s, q_s, kv_s, mixed_s, logs, stream2 = space_forward(sz, meta, vec, stream1s, w_space)

    m_rest = g_m.stage_rest(stream2)
    w_mlp = g_m.stage_core()
    res, d2, vg_m, parts_m = feed_forward(sz, meta, vec, stream2, cot_blocks, w_mlp, fast)

    r_m = reduce(parts_m, n, "mlp")
    m_core = r_m.stage_core()
    result_back = frames_back(res)
    up_s, dy_s = space_backward_scores(sz, meta, d2, q_s, kv_s, logs, w_space)

    m_rest = r_m.stage_rest(up_s)
    dy_s = after(dy_s, *result_back, *r_m.sent)
    parts_s = weight_slopes(sz, "space_weights", meta, up_s, normed_s, mixed_s, [dy_s], fast)
    r_s = reduce(parts_s, n, "space")
    s_core = r_s.stage_core(*m_rest)
    m_xy = r_m.stage_xy(*parts_s)
    d2b = after(d2, *parts_s, *r_m.sent)
    d1, vg_s = input_slopes(sz, "space_input", meta, vec, d2b, stream1, dy_s, w_space, 3, False)
    s_rest = r_s.stage_rest(d1)
    d1b = after(d1, *r_s.sent)
    up_t, dq, dkv, dkvo = time_backward_scores(sz, meta, d1b, q_t, kv_t, kv_o, prob_t, w_time)

    dkv_got = over_core(after(dkvo, *m_xy, *s_rest))
    m_z = r_m.stage_z(dkvo)
    s_xy = r_s.stage_xy(dkvo)
    dkv_got = after(dkv_got, *r_s.sent, *r_m.sent)
    dy_t, *parts_t = weight_slopes(
        sz, "time_weights", meta, up_t, normed_t, mixed_t, [dq, dkv, dkv_got], fast
    )

    r_t = reduce(parts_t, n, "time", True)
    t_core = r_t.stage_core(*m_z, *s_xy)
    s_z = r_s.stage_z(*parts_t)
    t_rest = r_t.stage_rest(*r_s.sent)
    d1c = after(d1, *r_s.sent, *r_t.sent)
    *dx, vg_t = input_slopes(sz, "time_input", meta, vec, d1c, stream0, dy_t, w_time, 0, True)

    t_xy = r_t.stage_xy(vg_t)
    t_z = r_t.stage_z()
    vg_t2 = after(vg_t, *r_t.sent)
    video_back = frames_back(after(tuple(dx), *r_t.sent))
    result = join_clips(after(tuple(result_back), vg_t), B16)
    grad_video = join_clips(video_back, F32)
    grad_in, grad_out = r_m.results(*parts_t)
    (grad_s,) = r_s.results(vg_t)
    (grad_t,) = r_t.results()

    rows = jnp.concatenate([vg_t2[0:3], vg_s[0:3], vg_m[0:2]], axis=0)
    parts = jnp.concatenate(
        [
            rows.reshape(8, count, per).transpose(1, 0, 2).reshape(count, 8 * per),
            vg_m[4:8].reshape(count, 4 * per),
            vg_m[2].reshape(count, per),
        ],
        axis=1,
    )
    got = lax.all_to_all(parts, every, split_axis=0, concat_axis=0, tiled=True)
    sums = jnp.sum(got, axis=0)
    cuts = [sums[starts[i] : starts[i] + (4 * per if i == 8 else per)] for i in range(10)]

    qkv_t_grad, proj_t_grad = unpack_heads(grad_t, c == 1)
    qkv_s_grad, proj_s_grad = unpack_heads(grad_s, c == 1)
    return (
        result,
        grad_video,
        qkv_t_grad,
        proj_t_grad,
        qkv_s_grad,
        proj_s_grad,
        grad_in,
        grad_out.T,
        *cuts,
    )


def solution(mesh):
    shape = dict(mesh.shape)
    fine = Mesh(
        mesh.devices.reshape(shape["shard"], shape["ctx"], 2, shape["tp"] // 2),
        ("shard", "ctx", "x", "core"),
    )
    tp = ("x", "core")
    sc = ("shard", "ctx")
    tokens = P("shard", tp, "ctx", None)
    weights = (P(sc, None, tp), P(tp, sc), P(sc, None, tp), P(tp, sc), P(sc, tp), P(tp, sc))
    vectors = (P(("shard", "ctx", "x", "core")),) * 10
    return jax.shard_map(
        functools.partial(local, shape),
        mesh=fine,
        in_specs=(tokens, tokens) + weights + vectors,
        out_specs=(tokens, tokens) + weights + vectors,
        check_vma=False,
    )
```

```python
import functools

import jax
import jax.numpy as jnp
from jax import lax
from jax.experimental import pallas as pl
from jax.experimental.pallas import tpu as pltpu
from jax.sharding import Mesh
from jax.sharding import PartitionSpec as P

F32 = jnp.float32
B16 = jnp.bfloat16
HEAD_DIM = 64
SCALING = HEAD_DIM ** (-0.5)
EPSILON = 1e-06
NEGATIVE = -1e30
PAD = 104
NT_DIMS = (((1,), (1,)), ((), ()))
TN_DIMS = (((0,), (0,)), ((), ()))
FLIP = [(0, 1), (1, 0)]
VMEM_LIMIT = 64 * 1024 * 1024 - 65536


def over_x(v):
    return lax.ppermute(v, "x", FLIP)


def over_y(v):
    return lax.ppermute(v, "ctx", FLIP)


def over_xy(v):
    return lax.ppermute(v, ("ctx", "x"), [(i, 3 - i) for i in range(4)])


def over_core(v):
    return lax.ppermute(v, "core", FLIP)


def over_z(v):
    return lax.all_to_all(v, "shard", split_axis=0, concat_axis=0, tiled=True)


def after(values, *results):
    return lax.optimization_barrier((values, results))[0]


def layout(chunks, n):
    full = [(z, k) for z in range(n) for k in range(chunks)]
    h = len(full) // 2
    return [(0, 0, full), (1, 0, full), (0, 1, full), (1, 1, full[:h]), (1, 1, full[h:])]


class Gather:
    def __init__(self, owns, n):
        own = jnp.stack(owns)
        self.n = n
        self.spread = lax.optimization_barrier(jnp.broadcast_to(own[None], (n,) + own.shape))

    def stage_z(self, *deps):
        self.z = [over_z(after(self.spread, *deps))]
        return self.z

    def stage_xy(self, *deps):
        z = after(tuple(self.z), *deps)
        self.blk = z[0].reshape((-1,) + z[0].shape[-2:])
        self.x, self.y = over_x(self.blk), over_y(self.blk)
        self.sent = [self.blk]
        return [self.x, self.y]

    def stage_rest(self, *deps):
        h = self.blk.shape[0] // 2
        x, y = after((self.x, self.y), *deps)
        self.sent = [x[:h], y[h:]]
        self.rest = [over_y(self.sent[0]), over_x(self.sent[1])]
        self.far = [over_core(v) for v in (self.blk, x, y)]
        return self.rest

    def stage_core(self, *deps):
        rest = after(tuple(self.rest), *deps)
        return [self.blk, self.x, self.y] + self.rest + self.far + [over_core(v) for v in rest]


def block_sums(name, outs):
    terms = [t for ts, _, _ in outs for t in ts]
    tail = terms[0][0].shape[1:]

    def kernel(*refs):
        ins, res = refs[: len(terms)], refs[len(terms) :]
        k = 0
        for (ts, count, dtype), out in zip(outs, res):
            for i in range(count):
                acc = None
                for j, (_, blocks, _, first) in enumerate(ts):
                    if first <= i < first + blocks:
                        v = ins[k + j][i - first].astype(F32)
                        acc = v if acc is None else acc + v
                out[i] = acc.astype(dtype)
            k += len(ts)

    def spec(blocks, index):
        return pl.BlockSpec((blocks,) + tail, lambda i: (index, 0, 0))

    return pl.pallas_call(
        kernel,
        name=name,
        grid=(1,),
        in_specs=[spec(blocks, index) for _, blocks, index, _ in terms],
        out_specs=[pl.BlockSpec((count,) + tail, lambda i: (0, 0, 0)) for _, count, _ in outs],
        out_shape=[jax.ShapeDtypeStruct((count,) + tail, dt) for _, count, dt in outs],
        compiler_params=pltpu.CompilerParams(vmem_limit_bytes=VMEM_LIMIT),
        cost_estimate=pl.CostEstimate(flops=10**8, bytes_accessed=10**5, transcendentals=0),
    )(*[t[0] for t in terms])


class Reduce:
    def __init__(self, parts, n, name, shifts=False):
        self.near, self.far = parts
        self.shifts = shifts
        self.n, self.name = n, name
        self.size = self.near.shape[0] // 4

    def stage_core(self, *deps):
        self.got = over_core(after(self.far, *deps))
        return [self.got]

    def stage_rest(self, *deps):
        h = self.size // 2
        self.got = after(self.got, *deps)
        lo, hi = block_sums(
            self.name + "_rest",
            [([(v, h, k, 0) for v in (self.near, self.got)], h, B16) for k in (6, 7)],
        )
        self.sent = [lo, hi]
        self.rest = [over_y(lo), over_x(hi)]
        return self.rest

    def stage_xy(self, *deps):
        size, h = self.size, self.size // 2
        lo, hi = after(tuple(self.rest), *deps)
        both = (self.near, self.got)
        sx, sy = block_sums(
            self.name + "_xy",
            [
                ([(v, size, 1, 0) for v in both] + [(lo, h, 0, 0)], size, B16),
                ([(v, size, 2, 0) for v in both] + [(hi, h, 0, h)], size, B16),
            ],
        )
        self.sent = [sx, sy]
        self.xy = [over_x(sx), over_y(sy)]
        return self.xy

    def stage_z(self, *deps):
        rx, ry = after(tuple(self.xy), *deps)
        all_four = (self.near, self.got, rx, ry)
        if self.shifts:
            own, *self.sent = block_sums(
                self.name + "_z",
                [
                    ([(v, 1, d, 0) for v in all_four], 1, B16 if d else F32)
                    for d in range(self.n)
                ],
            )
            self.z = [own] + [
                lax.ppermute(v, "shard", [(i, (i + d) % self.n) for i in range(self.n)])
                for d, v in enumerate(self.sent, 1)
            ]
            return self.z[1:]
        self.sent = block_sums(
            self.name + "_z", [([(v, self.size, 0, 0) for v in all_four], self.size, B16)]
        )
        v = self.sent[0]
        self.z = [over_z(v.reshape((self.n, self.size // self.n) + v.shape[1:]))]
        return self.z

    def results(self, *deps):
        z = after(tuple(self.z), *deps)
        if self.shifts:
            return [functools.reduce(lambda a, b: a + b, [v[0].astype(F32) for v in z])]
        z = jnp.sum(z[0].astype(F32), axis=0)
        return [z[k] for k in range(z.shape[0])]


def joint_z(parts, n, name):
    terms, count = [], len(parts)
    for i, (r, k) in enumerate(parts):
        chunks = r.size // n
        for z in range(n):
            terms += [(v, 1, z * chunks + k, z * count + i) for v in (r.near, r.got, *r.xy)]
    (v,) = block_sums(name, [(terms, n * count, B16)])
    return v.reshape((n, count) + v.shape[1:])


EVERY = ("x", "core", "shard", "ctx")


def gather_whole(own):
    return lax.all_gather(own, EVERY, axis=0, tiled=False)


def reduce_whole(parts):
    return lax.psum_scatter(parts, EVERY, scatter_dimension=0, tiled=False).astype(F32)


class GatherWhole:
    sent = ()
    spread = ()

    def __init__(self, owns, n):
        d = owns[0].shape[1]
        self.out = [gather_whole(v).reshape(4, d, d) for v in owns]

    def stage_z(self, *deps):
        return []

    stage_xy = stage_rest = stage_z

    def stage_core(self, *deps):
        return self.out


class ReduceWhole:
    sent = ()

    def __init__(self, parts, n, name, shifts=False):
        self.parts = parts

    def stage_z(self, *deps):
        return []

    stage_core = stage_rest = stage_xy = stage_z

    def results(self, *deps):
        rows = self.parts[0].shape[1] // (2 * lax.axis_size("shard"))
        return [reduce_whole(p.reshape(-1, rows, p.shape[2]).astype(F32)) for p in self.parts]


def dot(a, b):
    return jnp.dot(a, b, preferred_element_type=F32)


def dot_nt(a, b):
    return lax.dot_general(a, b, NT_DIMS, preferred_element_type=F32)


def dot_tn(a, b):
    return lax.dot_general(a, b, TN_DIMS, preferred_element_type=F32)


def low_lanes(shape):
    return lax.broadcasted_iota(jnp.int32, shape, 1) % 128 < 64


def keep_low(v):
    return jnp.where(low_lanes(v.shape), v, jnp.zeros_like(v))


def keep_high(v):
    return jnp.where(low_lanes(v.shape), jnp.zeros_like(v), v)


def swap_halves(v):
    return jnp.concatenate([v[:, 64:], v[:, :64]], axis=1)


def norm_parts(x):
    centred = x - jnp.mean(x, axis=-1, keepdims=True)
    rstd = lax.rsqrt(jnp.mean(centred * centred, axis=-1, keepdims=True) + EPSILON)
    return centred * rstd, rstd


def norm_back(x, gain, up):
    unit, rstd = norm_parts(x)
    w = up * gain
    inner = jnp.mean(w * unit, axis=-1, keepdims=True)
    down = rstd * (w - jnp.mean(w, axis=-1, keepdims=True) - unit * inner)
    return down, jnp.sum(up * unit, axis=0, keepdims=True), jnp.sum(up, axis=0, keepdims=True)


def weight_copies(meta, bufs, w_refs, sems, n, back=False, shifts=False):
    moves = []
    if bufs[0].shape == w_refs[0].shape:
        moves = list(zip(bufs, w_refs))
    else:
        x, y, c = meta[0], meta[1], meta[2]
        rows = w_refs[0].shape[1] // (2 * n)
        for dc in range(2):
            first = 0
            for k, (dx, dy, blocks) in enumerate(layout(len(w_refs), n)):
                tp = 2 * (x ^ dx) + (c ^ dc)
                for i, (z, chunk) in enumerate(blocks):
                    if shifts:
                        z = lax.rem(meta[3] + z, n)
                    row = pl.multiple_of((z * 2 + (y ^ dy)) * rows, rows)
                    piece = bufs[dc].at[first + i] if back else bufs[dc * 5 + k].at[i, 0:rows, :]
                    moves.append((piece, w_refs[chunk].at[tp, pl.ds(row, rows), :]))
                first += len(blocks)
    if back:
        moves = [(whole, piece) for piece, whole in moves]
    return [pltpu.make_async_copy(*m, sems.at[i]) for i, m in enumerate(moves)]


def copy_sems(sz, chunks):
    return pltpu.SemaphoreType.DMA((8 * chunks * sz["n"],))


def start_all(copies):
    for c in copies:
        c.start()


def wait_all(copies):
    for c in copies:
        c.wait()


def take_blocks(blocks, dst, places):
    for k, blk in enumerate(blocks):
        dx, dy = k % 2, k // 2
        for f in range(2):
            row = (2 * dx + f) * 2 * PAD + dy * PAD
            dst[row + PAD - 8 : row + PAD, :] = jnp.zeros((8, dst.shape[1]), dst.dtype)
            dst[row : row + places, :] = blk[f].astype(dst.dtype)


def give_blocks(src, blocks, places):
    for k, blk in enumerate(blocks):
        dx, dy = k % 2, k // 2
        for f in range(2):
            row = (2 * dx + f) * 2 * PAD + dy * PAD
            blk[f] = src[row : row + places, :].astype(blk.dtype)


def project_heads(normed, w_ref, q_out, kv_out):
    @pl.loop(0, 2)
    def _(u):
        thirds = []
        for t in (2 * u, 2 * u + 1):
            xn = normed[...]
            y = dot(xn, w_ref[t, :, 0:512]).astype(B16)
            q_out[t] = y[:, 0:128]
            kv_out[t] = y[:, 128:256]
            kv_out[6 + t] = y[:, 256:384]
            thirds.append((y[:, 384:512], dot(xn, w_ref[t, :, 640:768]).astype(B16)))
        (a3, a5), (b3, b5) = thirds
        low = low_lanes(a3.shape)
        q_out[4 + u] = jnp.where(low, a3, b3)
        kv_out[4 + u] = swap_halves(jnp.where(low, b3, a3))
        kv_out[10 + u] = swap_halves(jnp.where(low, b5, a5))


def third_head(v, t):
    return keep_low(v) if t % 2 == 0 else keep_high(v)


def project_out(mixed, w_ref, stream, bias, out):
    for n in range(3):
        cols = slice(256 * n, 256 * n + 256)
        acc = stream[:, cols] + bias[:, cols]
        for t in range(4):
            m = jnp.concatenate([mixed[t], third_head(mixed[4 + t // 2], t)], axis=1)
            acc = acc + dot_nt(m, w_ref[t, cols, 512:768])
        out[:, cols] = acc


def run(kernel, name, ins, outs, scratch, micros):
    space = {
        "v": pl.BlockSpec(memory_space=pltpu.VMEM),
        "s": pl.BlockSpec(memory_space=pltpu.SMEM),
        "a": pl.BlockSpec(memory_space=pl.ANY),
    }
    return pl.pallas_call(
        kernel,
        name=name,
        in_specs=[space[s] for _, s in ins],
        out_specs=[space[s] for _, _, s in outs],
        out_shape=[jax.ShapeDtypeStruct(s, d) for s, d, _ in outs],
        scratch_shapes=scratch,
        compiler_params=pltpu.CompilerParams(vmem_limit_bytes=VMEM_LIMIT),
        cost_estimate=pl.CostEstimate(
            flops=micros * 10**9, bytes_accessed=micros * 3 * 10**6, transcendentals=0
        ),
    )(*[a for a, _ in ins])


def row_slices(r, step=208):
    return pl.ds(pl.multiple_of(r * step, step), step)


VECTORS = 9


def norm_vectors(sz, meta, weights):
    d, n, nw = sz["d"], sz["n"], len(weights)
    count, rows = 8 * n, d // (2 * n)
    per = d // count
    hidden = VECTORS * per

    def kernel(*refs):
        meta, bufs = refs[0], refs[1 : 1 + nw]
        out, shares, sems = refs[1 + nw :]
        x, y, c = meta[0], meta[1], meta[2]
        copies = []
        for dc in range(2):
            for k, (dx, dy, blocks) in enumerate(layout(1, n)):
                tp = 2 * (x ^ dx) + (c ^ dc)
                for i, (z, _) in enumerate(blocks):
                    dev = (z * 2 + (y ^ dy)) * 4 + tp
                    piece = bufs[dc * 5 + k].at[i, rows : rows + 8, :]
                    copies.append(
                        pltpu.make_async_copy(piece, shares.at[dev], sems.at[len(copies)])
                    )
        start_all(copies)
        lane = lax.broadcasted_iota(jnp.int32, (128, d), 1)
        row = lax.broadcasted_iota(jnp.int32, (128, d), 0)
        one = ((lane % per == row) & (row < per)).astype(F32).astype(B16)
        four = ((lane % (4 * per) == row) & (row < 4 * per)).astype(F32).astype(B16)
        dev = lax.broadcasted_iota(jnp.int32, (count, d), 0)
        lanes = lax.broadcasted_iota(jnp.int32, (count, d), 1)
        mine = lanes // per == dev
        ours = lanes // (4 * per) == dev % 8
        wait_all(copies)
        rows_in = shares[:, 0, :].astype(F32)
        pad = jnp.zeros((count, 128), F32)
        rows_in = jnp.concatenate([rows_in, pad], axis=1)

        def spread(first, pick):
            parts = [rows_in[:, o + first : o + first + 128].astype(B16) for o in (0, 384)]
            return dot(parts[0], pick) + dot(parts[1], pick)

        for v in range(VECTORS):
            got = jnp.where(mine, spread(v * per, one), 0.0)
            out[v : v + 1, :] = jnp.sum(got, axis=0, keepdims=True)
        got = jnp.where(ours, spread(hidden, four), 0.0)
        for t in range(4):
            part = got[t * 8 : t * 8 + 8] if count == 32 else got
            out[VECTORS + t : VECTORS + t + 1, :] = jnp.sum(part, axis=0, keepdims=True)

    ins = [(meta, "s")] + [(w, "a") for w in weights]
    outs = [((16, d), F32, "v")]
    scratch = [pltpu.VMEM((count, 8, d), B16), copy_sems(sz, 1)]
    return run(kernel, "norm_vectors", ins, outs, scratch, 2)[0]


def time_qkv(sz, meta, vec, blocks, weights):
    rows, d = sz["rows"], sz["d"]
    nb, nw = len(blocks), len(weights)

    def kernel(*refs):
        meta, vec = refs[0], refs[1]
        blks, bufs = refs[2 : 2 + nb], refs[2 + nb : 2 + nb + nw]
        x, normed, q, kv, w, sems = refs[2 + nb + nw :]
        copies = weight_copies(meta, bufs, [w], sems, sz["n"])
        start_all(copies)
        take_blocks(blks, x, sz["places"])

        @pl.loop(0, 4)
        def _(r):
            at = row_slices(r)
            unit, _ = norm_parts(x[at, :])
            normed[at, :] = (unit * vec[0:1, :] + vec[1:2, :]).astype(B16)

        wait_all(copies)
        project_heads(normed, w, q, kv)

    ins = [(meta, "s"), (vec, "v")] + [(b, "v") for b in blocks] + [(w, "a") for w in weights]
    outs = [
        ((rows, d), F32, "v"),
        ((rows, d), B16, "v"),
        ((6, rows, 128), B16, "v"),
        ((12, rows, 128), B16, "v"),
    ]
    scratch = [pltpu.VMEM((4, d, d), B16), copy_sems(sz, 1)]
    return run(kernel, "time_qkv", ins, outs, scratch, 12)


def head_sums(ref):
    for f in range(4):
        for j in range(6):
            col = lax.broadcasted_iota(jnp.int32, (128, 128), 1)
            lane = lax.broadcasted_iota(jnp.int32, (128, 128), 0)
            hit = col == 16 * f + 2 * j + lane // 64
            ref[(f * 6 + j) * 128 : (f * 6 + j) * 128 + 128, :] = hit.astype(F32).astype(B16)


def head_spreads(ref):
    for f in range(4):
        for j in range(6):
            row = lax.broadcasted_iota(jnp.int32, (128, 128), 0)
            lane = lax.broadcasted_iota(jnp.int32, (128, 128), 1)
            hit = row == 16 * f + 2 * j + lane // 64
            ref[:, (f * 6 + j) * 128 : (f * 6 + j) * 128 + 128] = hit.astype(F32).astype(B16)


def pair_sums(a_ref, b_ref, b_tile, g, sums):
    at = row_slices(g)
    products = [
        a_ref[j, f * 208 : f * 208 + 208, :] * b_ref[b_tile + j, at, :]
        for f in range(4)
        for j in range(6)
    ]
    return dot(jnp.concatenate(products, axis=1), sums[...])


def two_tiles(ref, tile, at):
    return jnp.concatenate([ref[tile, at, :], ref[tile + 1, at, :]], axis=1).astype(F32)


def time_mix(sz, meta, vec, stream, q, kv, kvo, weights):
    rows, d = sz["rows"], sz["d"]
    nw = len(weights)

    def kernel(*refs):
        meta, vec, stream, q, kv, kvo = refs[:6]
        bufs = refs[6 : 6 + nw]
        mixed, out, prob, w, sums, spreads, acc, sems = refs[6 + nw :]
        copies = weight_copies(meta, bufs, [w], sems, sz["n"])
        start_all(copies)
        head_sums(sums)
        head_spreads(spreads)
        for h, ref in enumerate((kv, kvo)):

            @pl.loop(0, 4)
            def _(g):
                prob[4 * h + g] = pair_sums(q, ref, 0, g, sums) * SCALING

        @pl.loop(0, 13)
        def _(r):
            at = row_slices(r, 16)
            s = [prob[g, at, :] for g in range(8)]
            top = functools.reduce(jnp.maximum, s)
            e = [jnp.exp(v - top) for v in s]
            inv = 1.0 / functools.reduce(lambda a, b: a + b, e)
            for g in range(8):
                prob[g, at, :] = e[g] * inv

        acc[...] = jnp.zeros_like(acc)
        for h, ref in enumerate((kv, kvo)):

            @pl.loop(0, 4)
            def _(g):
                at = row_slices(g)
                p = prob[4 * h + g].astype(B16)
                for jj in range(3):
                    v = two_tiles(ref, 6 + 2 * jj, at)
                    for f in range(4):
                        lanes = slice(f * d + 256 * jj, f * d + 256 * jj + 256)
                        acc[f * 208 : f * 208 + 208, 256 * jj : 256 * jj + 256] += (
                            dot(p, spreads[:, lanes]) * v
                        )

        for j in range(6):
            mixed[j] = acc[:, 128 * j : 128 * j + 128].astype(B16)
        wait_all(copies)
        project_out(mixed, w, stream, vec[2:3, :], out)

    ins = [(meta, "s"), (vec, "v"), (stream, "v"), (q, "v"), (kv, "v"), (kvo, "v")]
    ins += [(w, "a") for w in weights]
    outs = [((6, rows, 128), B16, "v"), ((rows, d), F32, "v"), ((8, 208, 128), F32, "v")]
    scratch = [
        pltpu.VMEM((4, d, d), B16),
        pltpu.VMEM((4 * d, 128), B16),
        pltpu.VMEM((128, 4 * d), B16),
        pltpu.VMEM((rows, d), F32),
        copy_sems(sz, 1),
    ]
    return run(kernel, "time_mix", ins, outs, scratch, 17)


def space_mask(places):
    return lax.broadcasted_iota(jnp.int32, (208, 208), 0) % PAD < places


def space_qkv(sz, meta, vec, stream, weights):
    rows, d = sz["rows"], sz["d"]
    nw = len(weights)

    def kernel(*refs):
        meta, vec, stream = refs[:3]
        bufs = refs[3 : 3 + nw]
        normed, q, kv, w, sems = refs[3 + nw :]
        copies = weight_copies(meta, bufs, [w], sems, sz["n"])
        start_all(copies)

        @pl.loop(0, 4)
        def _(r):
            at = row_slices(r)
            unit, _ = norm_parts(stream[at, :])
            normed[at, :] = (unit * vec[3:4, :] + vec[4:5, :]).astype(B16)

        wait_all(copies)
        project_heads(normed, w, q, kv)

    ins = [(meta, "s"), (vec, "v"), (stream, "v")] + [(w, "a") for w in weights]
    outs = [((rows, d), B16, "v"), ((6, rows, 128), B16, "v"), ((12, rows, 128), B16, "v")]
    scratch = [pltpu.VMEM((4, d, d), B16), copy_sems(sz, 1)]
    return run(kernel, "space_qkv", ins, outs, scratch, 12)


def space_mix(sz, meta, vec, stream, q, kv, weights):
    rows, d, places = sz["rows"], sz["d"], sz["places"]
    nw = len(weights)

    def kernel(*refs):
        meta, vec, stream, q, kv = refs[:5]
        bufs = refs[5 : 5 + nw]
        mixed, logs, out, w, sems = refs[5 + nw :]
        copies = weight_copies(meta, bufs, [w], sems, sz["n"])
        start_all(copies)

        @pl.loop(0, 6)
        def _(j):
            @pl.loop(0, 4)
            def _(f):
                at = row_slices(f)
                qj, kj, vj = q[j, at, :], kv[j, at, :], kv[6 + j, at, :]
                mask = space_mask(places)
                o = None
                for h, keep in enumerate((keep_low, keep_high)):
                    s = jnp.where(mask, dot_nt(kj, keep(qj)) * SCALING, NEGATIVE)
                    top = jnp.max(s, axis=0, keepdims=True)
                    e = jnp.exp(s - top)
                    size = jnp.sum(e, axis=0, keepdims=True)
                    logs[j * 4 + f, h : h + 1, :] = top + jnp.log(size)
                    part = dot_tn((e * (1.0 / size)).astype(B16), keep(vj))
                    o = part if o is None else o + part
                mixed[j, at, :] = o.astype(B16)

        wait_all(copies)
        project_out(mixed, w, stream, vec[5:6, :], out)

    ins = [(meta, "s"), (vec, "v"), (stream, "v"), (q, "v"), (kv, "v")]
    ins += [(w, "a") for w in weights]
    outs = [((6, rows, 128), B16, "v"), ((24, 8, 208), F32, "v"), ((rows, d), F32, "v")]
    scratch = [pltpu.VMEM((4, d, d), B16), copy_sems(sz, 1)]
    return run(kernel, "space_mix", ins, outs, scratch, 17)


def gradient_outs(sz, chunks, fast):
    d, n = sz["d"], sz["n"]
    if not fast:
        return [((4, d, d), B16, "a")] * chunks
    return [((4 * chunks * n, d // (2 * n), d), B16, "a")] * 2


def gelu_pair(x):
    half = 0.5 * (1.0 + lax.erf(x * 0.7071067811865476))
    slope = half + x * (0.3989422804014327 * jnp.exp(-0.5 * x * x))
    return x * half, slope


def feed_forward(sz, meta, vec, stream, blocks, weights, fast):
    rows, d, places = sz["rows"], sz["d"], sz["places"]
    nb, nw = len(blocks), len(weights)
    g_outs = gradient_outs(sz, 2, fast)
    ng = len(g_outs)

    def kernel(*refs):
        meta, vec, stream = refs[:3]
        blks = refs[3 : 3 + nb]
        refs = refs[3 + nb :]
        bufs, refs = refs[:nw], refs[nw:]
        res, refs = refs[:nb], refs[nb:]
        d2, vgrad = refs[0], refs[1]
        g_bufs, refs = refs[2 : 2 + ng], refs[2 + ng :]
        w1, w2, dw1, dw2, dz, dzr, normed, act, dpre, y, dn, sems = refs
        copies = weight_copies(meta, bufs, [w1, w2], sems, sz["n"])
        start_all(copies)
        take_blocks(blks, dz, places)
        vgrad[...] = jnp.zeros_like(vgrad)

        @pl.loop(0, 4)
        def _(r):
            at = pl.ds(pl.multiple_of(r * 208, 208), 208)
            unit, _ = norm_parts(stream[at, :])
            normed[at, :] = (unit * vec[6:7, :] + vec[7:8, :]).astype(B16)
            up = dz[at, :]
            dzr[at, :] = up.astype(B16)
            vgrad[2:3, :] += jnp.sum(up, axis=0, keepdims=True)
            y[at, :] = stream[at, :] + vec[8:9, :]
            dn[at, :] = jnp.zeros_like(up)

        wait_all(copies)

        @pl.loop(0, 4)
        def _(t):
            thirds = [slice(256 * i, 256 * i + 256) for i in range(3)]
            for cols in thirds:
                pre = dot(normed[...], w1[t, :, cols]) + vec[pl.ds(9 + t, 1), cols]
                a, slope = gelu_pair(pre)
                act[:, cols] = a.astype(B16)
                g = (dot(dzr[...], w2[t, :, cols]) * slope).astype(B16)
                dpre[:, cols] = g
                vgrad[pl.ds(4 + t, 1), cols] += jnp.sum(g.astype(F32), axis=0, keepdims=True)
            for cols in thirds:
                y[:, cols] += dot_nt(act[...], w2[t, cols, :])
                dn[:, cols] += dot_nt(dpre[...], w1[t, cols, :])
            for cols in thirds:
                dw1[t, :, cols] = dot_tn(normed[...], dpre[:, cols]).astype(B16)
                dw2[t, :, cols] = dot_tn(dzr[...], act[:, cols]).astype(B16)

        back = weight_copies(meta, g_bufs, [dw1, dw2], sems, sz["n"], back=True)
        start_all(back)
        give_blocks(y, res, places)

        @pl.loop(0, 4)
        def _(r):
            at = pl.ds(pl.multiple_of(r * 208, 208), 208)
            down, gg, gs = norm_back(stream[at, :], vec[6:7, :], dn[at, :])
            d2[at, :] = dz[at, :] + down
            vgrad[0:1, :] += gg
            vgrad[1:2, :] += gs

        wait_all(back)

    ins = [(meta, "s"), (vec, "v"), (stream, "v")] + [(b, "v") for b in blocks]
    ins += [(w, "a") for w in weights]
    outs = [((2, places, d), B16, "v")] * nb + [((rows, d), F32, "v"), ((8, d), F32, "v")]
    outs += g_outs
    scratch = [pltpu.VMEM((4, d, d), B16)] * 4
    scratch += [pltpu.VMEM((rows, d), F32), pltpu.VMEM((rows, d), B16), pltpu.VMEM((rows, d), B16)]
    scratch += [pltpu.VMEM((rows, d), B16)] * 2 + [pltpu.VMEM((rows, d), F32)] * 2
    scratch += [copy_sems(sz, 2)]
    r = run(kernel, "feed_forward", ins, outs, scratch, 47)
    return r[:nb], r[nb], r[nb + 1], r[nb + 2 :]


def mixed_slopes(up, w_ref, dm):
    for u in range(2):
        thirds = []
        for t in (2 * u, 2 * u + 1):
            v = dot(up[...], w_ref[t, :, 512:768]).astype(B16)
            dm[t] = v[:, 0:128]
            thirds.append(v[:, 128:256])
        dm[4 + u] = jnp.where(low_lanes(thirds[0].shape), *thirds)


def place_third(dq, dk, dv, dy, u, at):
    k, v = swap_halves(dk), swap_halves(dv)
    low = low_lanes(dq.shape)
    dy[2 * u, at, 384:512] = jnp.where(low, dq, k)
    dy[2 * u + 1, at, 384:512] = jnp.where(low, k, dq)
    dy[2 * u, at, 512:640] = keep_high(v)
    dy[2 * u + 1, at, 512:640] = keep_low(v)


def head_gradients(dw, normed, up, dy, mixed):
    @pl.loop(0, 2)
    def _(u):
        for odd in range(2):
            t = 2 * u + odd
            dw[t, :, 0:512] = dot_tn(normed[...], dy[t, :, 0:512]).astype(B16)
            m2 = jnp.concatenate([mixed[t], third_head(mixed[4 + u], odd)], axis=1)
            out = dot_tn(up[...], m2)
            dw[t, :, 512:640] = out[:, 0:128].astype(B16)
            third = dot_tn(normed[...], dy[t, :, 512:640])
            dw[t, :, 640:768] = (out[:, 128:256] + third).astype(B16)


def norm_slopes(dy, w_ref, out):
    for n in range(3):
        cols = slice(256 * n, 256 * n + 256)
        acc = None
        for t in range(4):
            part = dot_nt(dy[t, :, 0:512], w_ref[t, cols, 0:512])
            part = part + dot_nt(dy[t, :, 512:640], w_ref[t, cols, 640:768])
            acc = part if acc is None else acc + part
        out[:, cols] = acc


def space_backward_scores(sz, meta, d2, q, kv, logs, weights):
    rows, d, places = sz["rows"], sz["d"], sz["places"]
    nw = len(weights)

    def kernel(*refs):
        meta, d2, q, kv, logs = refs[:5]
        bufs, refs = refs[5 : 5 + nw], refs[5 + nw :]
        up, dy, w, dm, third, sems = refs
        copies = weight_copies(meta, bufs, [w], sems, sz["n"])
        start_all(copies)

        @pl.loop(0, 4)
        def _(r):
            up[row_slices(r), :] = d2[row_slices(r), :].astype(B16)

        wait_all(copies)
        mixed_slopes(up, w, dm)

        def slopes(j, at, f):
            qj, kj, vj, mj = q[j, at, :], kv[j, at, :], kv[6 + j, at, :], dm[j, at, :]
            mask = space_mask(places)
            dq = dk = dv = None
            for h, keep in enumerate((keep_low, keep_high)):
                qh, mh = keep(qj), keep(mj)
                s = dot_nt(kj, qh) * SCALING - logs[j * 4 + f, h : h + 1, :]
                p = jnp.exp(jnp.where(mask, s, NEGATIVE))
                dp = dot_nt(vj, mh)
                inner = jnp.sum(p * dp, axis=0, keepdims=True)
                ds = (p * (dp - inner) * SCALING).astype(B16)
                a, b, c = dot_tn(ds, keep(kj)), dot(ds, qh), dot(p.astype(B16), mh)
                dq, dk, dv = (a, b, c) if dq is None else (dq + a, dk + b, dv + c)
            return dq.astype(B16), dk.astype(B16), dv.astype(B16)

        @pl.loop(0, 4)
        def _(j):
            @pl.loop(0, 4)
            def _(f):
                at = row_slices(f)
                dq, dk, dv = slopes(j, at, f)
                dy[j, at, 0:128] = dq
                dy[j, at, 128:256] = dk
                dy[j, at, 256:384] = dv

        @pl.loop(0, 2)
        def _(u):
            @pl.loop(0, 4)
            def _(f):
                at = row_slices(f)
                place_third(*slopes(4 + u, at, f), dy, u, at)

    ins = [(meta, "s")] + [(v, "v") for v in (d2, q, kv, logs)] + [(w, "a") for w in weights]
    outs = [((rows, d), B16, "v"), ((4, rows, 640), B16, "v")]
    scratch = [pltpu.VMEM((4, d, d), B16), pltpu.VMEM((6, rows, 128), B16)]
    scratch += [pltpu.VMEM((rows, 128), B16), copy_sems(sz, 1)]
    return run(kernel, "space_backward_scores", ins, outs, scratch, 30)


def weight_slopes(sz, name, meta, up, normed, mixed, slopes, fast):
    rows, d = sz["rows"], sz["d"]
    g_outs = gradient_outs(sz, 1, fast)
    join = len(slopes) == 3

    def kernel(*refs):
        meta, up, normed, mixed = refs[:4]
        given, refs = refs[4 : 4 + len(slopes)], refs[4 + len(slopes) :]
        dy = refs[0] if join else given[0]
        g_bufs, (dw, sems) = refs[1 if join else 0 : -2], refs[-2:]
        if join:
            dq, dkv, got = given

            def both(j, at):
                return (dkv[j, at, :].astype(F32) + got[j, at, :].astype(F32)).astype(B16)

            @pl.loop(0, 4)
            def _(r):
                at = row_slices(r)
                for j in range(4):
                    dy[j, at, 0:128] = dq[j, at, :]
                    dy[j, at, 128:256] = both(j, at)
                    dy[j, at, 256:384] = both(6 + j, at)
                for u in range(2):
                    place_third(dq[4 + u, at, :], both(4 + u, at), both(10 + u, at), dy, u, at)

        head_gradients(dw, normed, up, dy, mixed)
        back = weight_copies(meta, g_bufs, [dw], sems, sz["n"], back=True, shifts=join)
        start_all(back)
        wait_all(back)

    ins = [(meta, "s")] + [(v, "v") for v in (up, normed, mixed, *slopes)]
    outs = ([((4, rows, 640), B16, "v")] if join else []) + g_outs
    scratch = [pltpu.VMEM((4, d, d), B16), copy_sems(sz, 1)]
    return run(kernel, name, ins, outs, scratch, 14)


def input_slopes(sz, name, meta, vec, up, stream, dy, weights, gain_row, blocks):
    rows, d, places = sz["rows"], sz["d"], sz["places"]
    nw = len(weights)

    def kernel(*refs):
        meta, vec, up, stream, dy = refs[:5]
        bufs, refs = refs[5 : 5 + nw], refs[5 + nw :]
        w, dn, sems = refs[-3:]
        if blocks:
            outs, vgrad, dx = refs[:4], refs[4], refs[5]
        else:
            dx, vgrad = refs[:2]
        copies = weight_copies(meta, bufs, [w], sems, sz["n"])
        start_all(copies)
        vgrad[...] = jnp.zeros_like(vgrad)
        wait_all(copies)
        norm_slopes(dy, w, dn)

        @pl.loop(0, 4)
        def _(r):
            at = row_slices(r)
            v = up[at, :]
            gain = vec[gain_row : gain_row + 1, :]
            down, gg, gs = norm_back(stream[at, :], gain, dn[at, :])
            dx[at, :] = v + down
            vgrad[0:1, :] += gg
            vgrad[1:2, :] += gs
            vgrad[2:3, :] += jnp.sum(v, axis=0, keepdims=True)

        if blocks:
            give_blocks(dx, outs, places)

    ins = [(meta, "s")] + [(v, "v") for v in (vec, up, stream, dy)] + [(w, "a") for w in weights]
    outs = [((rows, d), F32, "v")]
    scratch = []
    if blocks:
        outs = [((2, places, d), F32, "v")] + [((2, places, d), B16, "v")] * 3
        scratch = [pltpu.VMEM((rows, d), F32)]
    outs += [((8, d), F32, "v")]
    scratch += [pltpu.VMEM((4, d, d), B16), pltpu.VMEM((rows, d), F32), copy_sems(sz, 1)]
    return run(kernel, name, ins, outs, scratch, 14)


def time_backward_scores(sz, meta, d1, q, kv, kvo, prob, weights):
    rows, d = sz["rows"], sz["d"]
    nw = len(weights)

    def kernel(*refs):
        meta, d1, q, kv, kvo, prob = refs[:6]
        bufs, refs = refs[6 : 6 + nw], refs[6 + nw :]
        up, dq, dkv, dkvo, w, dm, sums, spreads, ds, acc, sems = refs
        copies = weight_copies(meta, bufs, [w], sems, sz["n"])
        start_all(copies)
        head_sums(sums)
        head_spreads(spreads)

        @pl.loop(0, 4)
        def _(r):
            up[row_slices(r), :] = d1[row_slices(r), :].astype(B16)

        wait_all(copies)
        mixed_slopes(up, w, dm)
        for h, ref in enumerate((kv, kvo)):

            @pl.loop(0, 4)
            def _(g):
                ds[4 * h + g] = pair_sums(dm, ref, 6, g, sums)

        @pl.loop(0, 13)
        def _(r):
            at = row_slices(r, 16)
            p = [prob[g, at, :] for g in range(8)]
            dp = [ds[g, at, :] for g in range(8)]
            inner = functools.reduce(lambda a, b: a + b, [a * b for a, b in zip(p, dp)])
            for g in range(8):
                ds[g, at, :] = p[g] * (dp[g] - inner) * SCALING

        acc[...] = jnp.zeros_like(acc)
        for h, (ref, out) in enumerate(((kv, dkv), (kvo, dkvo))):

            @pl.loop(0, 4)
            def _(g):
                at = row_slices(g)
                both = jnp.concatenate([ds[4 * h + g], prob[4 * h + g]], axis=0).astype(B16)
                for jj in range(3):
                    k = two_tiles(ref, 2 * jj, at)
                    dk = dv = None
                    for f in range(4):
                        fr = slice(f * 208, f * 208 + 208)
                        e = dot(both, spreads[:, f * d + 256 * jj : f * d + 256 * jj + 256])
                        se, pe = e[:208], e[208:]
                        acc[fr, 256 * jj : 256 * jj + 256] += se * k
                        a = se * two_tiles(q, 2 * jj, fr)
                        b = pe * two_tiles(dm, 2 * jj, fr)
                        dk, dv = (a, b) if dk is None else (dk + a, dv + b)
                    dk, dv = dk.astype(B16), dv.astype(B16)
                    for i in range(2):
                        out[2 * jj + i, at, :] = dk[:, 128 * i : 128 * i + 128]
                        out[6 + 2 * jj + i, at, :] = dv[:, 128 * i : 128 * i + 128]

        for j in range(6):
            dq[j] = acc[:, 128 * j : 128 * j + 128].astype(B16)

    ins = [(meta, "s")] + [(v, "v") for v in (d1, q, kv, kvo, prob)] + [(w, "a") for w in weights]
    outs = [
        ((rows, d), B16, "v"),
        ((6, rows, 128), B16, "v"),
        ((12, rows, 128), B16, "v"),
        ((12, rows, 128), B16, "v"),
    ]
    scratch = [
        pltpu.VMEM((4, d, d), B16),
        pltpu.VMEM((6, rows, 128), B16),
        pltpu.VMEM((4 * d, 128), B16),
        pltpu.VMEM((128, 4 * d), B16),
        pltpu.VMEM((8, 208, 128), F32),
        pltpu.VMEM((rows, d), F32),
        copy_sems(sz, 1),
    ]
    return run(kernel, "time_backward_scores", ins, outs, scratch, 23)


def pack_heads(qkv, proj, odd):
    q, k, v = qkv[:, 0], qkv[:, 1], qkv[:, 2]
    o = proj.T
    first = [q[:, :128], k[:, :128], v[:, :128]]
    even = first + [q[:, 128:], k[:, 128:], o[:, :128], o[:, 128:], v[:, 128:]]
    other = first + [k[:, 128:], q[:, 128:], o[:, :128], v[:, 128:], o[:, 128:]]
    return jnp.where(odd, jnp.concatenate(other, axis=1), jnp.concatenate(even, axis=1))


def unpack_heads(g, odd):
    def pick(a, b):
        return jnp.where(odd, g[:, b : b + 64], g[:, a : a + 64])

    q = jnp.concatenate([g[:, 0:128], pick(384, 448)], axis=1)
    k = jnp.concatenate([g[:, 128:256], pick(448, 384)], axis=1)
    v = jnp.concatenate([g[:, 256:384], pick(704, 640)], axis=1)
    o = jnp.concatenate([g[:, 512:640], pick(640, 704)], axis=1)
    return jnp.stack([q, k, v], axis=1), o.T


def local(mesh_shape, video, cotangent, *params):
    qkv_time, proj_time, qkv_space, proj_space, fc_in, fc_out = params[:6]
    vectors = params[6:]
    n = mesh_shape["shard"]
    d = proj_time.shape[0] * 4
    places = video.shape[2]
    rows_here = fc_in.shape[0]
    fast = rows_here % 16 == 0
    sz = {"n": n, "d": d, "places": places, "rows": 8 * PAD}
    x, y = lax.axis_index("x"), lax.axis_index("ctx")
    c, z = lax.axis_index("core"), lax.axis_index("shard")
    meta = jnp.stack([x, y, c, z]).astype(jnp.int32)
    every = ("shard", "ctx", "x", "core")
    count = 8 * n

    gather, reduce = (Gather, Reduce) if fast else (GatherWhole, ReduceWhole)
    per = d // count
    order = [0, 1, 2, 3, 4, 5, 6, 7, 9, 8]
    share = jnp.concatenate([vectors[i] for i in order])
    first_rows = pack_heads(qkv_time, proj_time, c == 1)
    if fast:
        kept = lax.reduce_precision(share, exponent_bits=8, mantissa_bits=7)
        high, low = kept.astype(B16), (share - kept).astype(B16)
        gap = jnp.zeros((384 - share.shape[0],), B16)
        row = jnp.concatenate([high, gap, low, gap])[None]
        first_rows = jnp.concatenate([first_rows, row, jnp.zeros((7, d), B16)], axis=0)

    def clips_of(v):
        return [
            lax.dynamic_index_in_dim(v, 2 * (x ^ dx) + (y ^ dy), 0, keepdims=False)
            for dx, dy in ((0, 0), (1, 0), (0, 1), (1, 1))
        ]

    def frames_back(blocks):
        return [blocks[0], over_x(blocks[1]), over_y(blocks[2]), over_xy(blocks[3])]

    def join_clips(blocks, dtype):
        out = jnp.zeros((4,) + blocks[0].shape, dtype)
        for k, b in enumerate(blocks):
            at = 2 * (x ^ (k % 2)) + (y ^ (k // 2))
            out = lax.dynamic_update_slice_in_dim(out, b.astype(dtype)[None], at, 0)
        return out

    g_t = gather([first_rows], n)
    g_s = gather([pack_heads(qkv_space, proj_space, c == 1)], n)
    g_m = gather([fc_in, fc_out.T], n)
    t_z = g_t.stage_z()
    cot_clips, video_clips = [clips_of(v) for v in after((cotangent, video), g_t.spread)]
    cot_blocks, video_blocks = frames_back(cot_clips), frames_back(video_clips)
    t_xy = g_t.stage_xy(*cot_blocks[1:], *video_blocks[1:3])
    s_z = g_s.stage_z(*t_z)
    t_rest = g_t.stage_rest()
    m_z = g_m.stage_z(*s_z)
    s_xy = g_s.stage_xy(*t_rest)
    w_time = g_t.stage_core()
    if fast:
        vec = norm_vectors(sz, meta, w_time)
    else:
        shares = lax.all_gather(share, every, axis=0, tiled=False)
        vec = shares[:, : VECTORS * per].reshape(count, VECTORS, per).transpose(1, 0, 2)
        hidden = shares[:, VECTORS * per :].reshape(4, d)
        vec = jnp.concatenate([vec.reshape(VECTORS, d), hidden, jnp.zeros((3, d), F32)], axis=0)
    vec_t = after(vec, *g_s.sent, g_m.spread)
    stream0, normed_t, q_t, kv_t = time_qkv(sz, meta, vec_t, video_blocks, w_time)

    kv_o = over_core(after(kv_t, *s_xy, *m_z))
    s_rest = g_s.stage_rest(kv_t)
    m_xy = g_m.stage_xy(kv_t)
    kv_o = after(kv_o, *s_rest, *g_m.sent)
    mixed_t, stream1, prob_t = time_mix(sz, meta, vec, stream0, q_t, kv_t, kv_o, w_time)

    w_space = g_s.stage_core()
    normed_s, q_s, kv_s = space_qkv(sz, meta, vec, stream1, w_space)
    m_rest = g_m.stage_rest(kv_s)
    kv_sb = after(kv_s, *g_m.sent)
    mixed_s, logs, stream2 = space_mix(sz, meta, vec, stream1, q_s, kv_sb, w_space)

    w_mlp = g_m.stage_core(stream2)
    res, d2, vg_m, parts_m = feed_forward(sz, meta, vec, stream2, cot_blocks, w_mlp, fast)

    r_m = reduce(parts_m, n, "mlp")
    m_core = r_m.stage_core()
    result_back = frames_back(res)
    up_s, dy_s = space_backward_scores(sz, meta, d2, q_s, kv_s, logs, w_space)

    m_rest = r_m.stage_rest(up_s)
    dy_s = after(dy_s, *result_back, *r_m.sent)
    parts_s = weight_slopes(sz, "space_weights", meta, up_s, normed_s, mixed_s, [dy_s], fast)
    r_s = reduce(parts_s, n, "space")
    s_core = r_s.stage_core(*m_rest)
    m_xy = r_m.stage_xy(*parts_s)
    d2b = after(d2, *parts_s, *r_m.sent)
    d1, vg_s = input_slopes(sz, "space_input", meta, vec, d2b, stream1, dy_s, w_space, 3, False)
    s_rest = r_s.stage_rest(d1)
    d1b = after(d1, *r_s.sent)
    up_t, dq, dkv, dkvo = time_backward_scores(sz, meta, d1b, q_t, kv_t, kv_o, prob_t, w_time)

    dkv_got = over_core(after(dkvo, *m_xy, *s_rest))
    first_z = ()
    if fast:
        r_m.xy = after(tuple(m_xy), dkvo)
        first_sent = joint_z([(r_m, 0)], n, "mlp_z")
        first_z = (over_z(first_sent),)
    s_xy = r_s.stage_xy(dkvo)
    dkv_got = after(dkv_got, *r_s.sent, first_sent) if fast else dkv_got
    dy_t, *parts_t = weight_slopes(
        sz, "time_weights", meta, up_t, normed_t, mixed_t, [dq, dkv, dkv_got], fast
    )

    r_t = reduce(parts_t, n, "time", True)
    t_core = r_t.stage_core(*s_xy, *first_z)
    t_rest = r_t.stage_rest()
    if fast:
        r_s.xy = after(tuple(s_xy), *r_t.sent)
        sent = joint_z([(r_s, 0), (r_m, 1)], n, "joint_z")
        got = over_z(sent)
    else:
        sent = ()
    t_xy = r_t.stage_xy(sent)
    d1c = after(d1, *r_t.sent)
    *dx, vg_t = input_slopes(sz, "time_input", meta, vec, d1c, stream0, dy_t, w_time, 0, True)

    t_z = r_t.stage_z(vg_t)
    vg_t2, result_back, dx = after((vg_t, tuple(result_back), tuple(dx)), *r_t.sent)
    video_back = frames_back(dx)
    if fast:
        vg_t2 = after(vg_t2, got)

    rows = jnp.concatenate([vg_t2[0:3], vg_s[0:3], vg_m[0:2]], axis=0)
    parts = jnp.concatenate(
        [
            rows.reshape(8, count, per).transpose(1, 0, 2).reshape(count, 8 * per),
            vg_m[4:8].reshape(count, 4 * per),
            vg_m[2].reshape(count, per),
        ],
        axis=1,
    )
    got_parts = lax.all_to_all(parts, every, split_axis=0, concat_axis=0, tiled=True)
    result = join_clips(result_back, B16)
    if fast:
        vec_got, video_back, r_t.z, joint, first = lax.optimization_barrier(
            (got_parts, tuple(video_back), tuple(r_t.z), got, first_z[0])
        )
        joint = jnp.sum(joint.astype(F32), axis=0)
        grad_s, grad_out = joint[0], joint[1]
        grad_in = jnp.sum(first.astype(F32), axis=0)[0]
    else:
        vec_got = got_parts
        grad_in, grad_out = r_m.results()
        (grad_s,) = r_s.results()
    (grad_t,) = r_t.results()
    grad_video = join_clips(video_back, F32)
    sums = jnp.sum(vec_got, axis=0)
    starts = [per * i for i in range(9)] + [per * 12]
    cuts = [sums[starts[i] : starts[i] + (4 * per if i == 8 else per)] for i in range(10)]

    qkv_t_grad, proj_t_grad = unpack_heads(grad_t, c == 1)
    qkv_s_grad, proj_s_grad = unpack_heads(grad_s, c == 1)
    return (
        result,
        grad_video,
        qkv_t_grad,
        proj_t_grad,
        qkv_s_grad,
        proj_s_grad,
        grad_in,
        grad_out.T,
        *cuts,
    )


def solution(mesh):
    shape = dict(mesh.shape)
    fine = Mesh(
        mesh.devices.reshape(shape["shard"], shape["ctx"], 2, shape["tp"] // 2),
        ("shard", "ctx", "x", "core"),
    )
    tp = ("x", "core")
    sc = ("shard", "ctx")
    tokens = P("shard", tp, "ctx", None)
    weights = (P(sc, None, tp), P(tp, sc), P(sc, None, tp), P(tp, sc), P(sc, tp), P(tp, sc))
    vectors = (P(("shard", "ctx", "x", "core")),) * 10
    return jax.shard_map(
        functools.partial(local, shape),
        mesh=fine,
        in_specs=(tokens, tokens) + weights + vectors,
        out_specs=(tokens, tokens) + weights + vectors,
        check_vma=False,
    )
```

```python
import functools

import jax
import jax.numpy as jnp
from jax import lax
from jax.experimental import pallas as pl
from jax.experimental.pallas import tpu as pltpu
from jax.sharding import Mesh
from jax.sharding import PartitionSpec as P

F32 = jnp.float32
B16 = jnp.bfloat16
HEAD_DIM = 64
SCALING = HEAD_DIM ** (-0.5)
EPSILON = 1e-06
NEGATIVE = -1e30
PAD = 104
NT_DIMS = (((1,), (1,)), ((), ()))
TN_DIMS = (((0,), (0,)), ((), ()))
FLIP = [(0, 1), (1, 0)]
VMEM_LIMIT = 64 * 1024 * 1024 - 65536


def over_x(v):
    return lax.ppermute(v, "x", FLIP)


def over_y(v):
    return lax.ppermute(v, "ctx", FLIP)


def over_xy(v):
    return lax.ppermute(v, ("ctx", "x"), [(i, 3 - i) for i in range(4)])


def over_core(v):
    return lax.ppermute(v, "core", FLIP)


def over_z(v):
    return lax.all_to_all(v, "shard", split_axis=0, concat_axis=0, tiled=True)


def after(values, *results):
    return lax.optimization_barrier((values, results))[0]


def layout(chunks, n):
    full = [(z, k) for z in range(n) for k in range(chunks)]
    h = len(full) // 2
    return [(0, 0, full), (1, 0, full), (0, 1, full), (1, 1, full[:h]), (1, 1, full[h:])]


class Gather:
    def __init__(self, owns, n):
        own = jnp.stack(owns)
        self.n = n
        self.spread = lax.optimization_barrier(jnp.broadcast_to(own[None], (n,) + own.shape))

    def stage_z(self, *deps):
        self.z = [over_z(after(self.spread, *deps))]
        return self.z

    def stage_xy(self, *deps):
        z = after(tuple(self.z), *deps)
        self.blk = z[0].reshape((-1,) + z[0].shape[-2:])
        self.x, self.y = over_x(self.blk), over_y(self.blk)
        self.sent = [self.blk]
        return [self.x, self.y]

    def stage_rest(self, *deps):
        h = self.blk.shape[0] // 2
        x, y = after((self.x, self.y), *deps)
        self.sent = [x[:h], y[h:]]
        self.rest = [over_y(self.sent[0]), over_x(self.sent[1])]
        self.far = [over_core(v) for v in (self.blk, x, y)]
        return self.rest

    def stage_core(self, *deps):
        rest = after(tuple(self.rest), *deps)
        return [self.blk, self.x, self.y] + self.rest + self.far + [over_core(v) for v in rest]


def block_sums(name, outs):
    terms = [t for ts, _, _ in outs for t in ts]
    tail = terms[0][0].shape[1:]

    def kernel(*refs):
        ins, res = refs[: len(terms)], refs[len(terms) :]
        k = 0
        for (ts, count, dtype), out in zip(outs, res):
            for i in range(count):
                acc = None
                for j, (_, blocks, _, first) in enumerate(ts):
                    if first <= i < first + blocks:
                        v = ins[k + j][i - first].astype(F32)
                        acc = v if acc is None else acc + v
                out[i] = acc.astype(dtype)
            k += len(ts)

    def spec(blocks, index):
        return pl.BlockSpec((blocks,) + tail, lambda i: (index, 0, 0))

    return pl.pallas_call(
        kernel,
        name=name,
        grid=(1,),
        in_specs=[spec(blocks, index) for _, blocks, index, _ in terms],
        out_specs=[pl.BlockSpec((count,) + tail, lambda i: (0, 0, 0)) for _, count, _ in outs],
        out_shape=[jax.ShapeDtypeStruct((count,) + tail, dt) for _, count, dt in outs],
        compiler_params=pltpu.CompilerParams(vmem_limit_bytes=VMEM_LIMIT),
        cost_estimate=pl.CostEstimate(flops=10**8, bytes_accessed=10**5, transcendentals=0),
    )(*[t[0] for t in terms])


class Reduce:
    def __init__(self, parts, n, name, shifts=False):
        self.near, self.far = parts
        self.shifts = shifts
        self.n, self.name = n, name
        self.size = self.near.shape[0] // 4

    def stage_core(self, *deps):
        self.got = over_core(after(self.far, *deps))
        return [self.got]

    def stage_rest(self, *deps):
        h = self.size // 2
        self.got = after(self.got, *deps)
        lo, hi = block_sums(
            self.name + "_rest",
            [([(v, h, k, 0) for v in (self.near, self.got)], h, B16) for k in (6, 7)],
        )
        self.sent = [lo, hi]
        self.rest = [over_y(lo), over_x(hi)]
        return self.rest

    def stage_xy(self, *deps):
        size, h = self.size, self.size // 2
        lo, hi = after(tuple(self.rest), *deps)
        both = (self.near, self.got)
        sx, sy = block_sums(
            self.name + "_xy",
            [
                ([(v, size, 1, 0) for v in both] + [(lo, h, 0, 0)], size, B16),
                ([(v, size, 2, 0) for v in both] + [(hi, h, 0, h)], size, B16),
            ],
        )
        self.sent = [sx, sy]
        self.xy = [over_x(sx), over_y(sy)]
        return self.xy

    def stage_z(self, *deps):
        rx, ry = after(tuple(self.xy), *deps)
        all_four = (self.near, self.got, rx, ry)
        if self.shifts:
            own, *self.sent = block_sums(
                self.name + "_z",
                [
                    ([(v, 1, d, 0) for v in all_four], 1, B16 if d else F32)
                    for d in range(self.n)
                ],
            )
            self.z = [own] + [
                lax.ppermute(v, "shard", [(i, (i + d) % self.n) for i in range(self.n)])
                for d, v in enumerate(self.sent, 1)
            ]
            return self.z[1:]
        self.sent = block_sums(
            self.name + "_z", [([(v, self.size, 0, 0) for v in all_four], self.size, B16)]
        )
        v = self.sent[0]
        self.z = [over_z(v.reshape((self.n, self.size // self.n) + v.shape[1:]))]
        return self.z

    def results(self, *deps):
        z = after(tuple(self.z), *deps)
        if self.shifts:
            return [functools.reduce(lambda a, b: a + b, [v[0].astype(F32) for v in z])]
        z = jnp.sum(z[0].astype(F32), axis=0)
        return [z[k] for k in range(z.shape[0])]


def joint_z(parts, n, name):
    terms, count = [], len(parts)
    for i, (r, k) in enumerate(parts):
        chunks = r.size // n
        for z in range(n):
            terms += [(v, 1, z * chunks + k, z * count + i) for v in (r.near, r.got, *r.xy)]
    (v,) = block_sums(name, [(terms, n * count, B16)])
    return v.reshape((n, count) + v.shape[1:])


EVERY = ("x", "core", "shard", "ctx")


def gather_whole(own):
    return lax.all_gather(own, EVERY, axis=0, tiled=False)


def reduce_whole(parts):
    return lax.psum_scatter(parts, EVERY, scatter_dimension=0, tiled=False).astype(F32)


class GatherWhole:
    sent = ()
    spread = ()

    def __init__(self, owns, n):
        d = owns[0].shape[1]
        self.out = [gather_whole(v).reshape(4, d, d) for v in owns]

    def stage_z(self, *deps):
        return []

    stage_xy = stage_rest = stage_z

    def stage_core(self, *deps):
        return self.out


class ReduceWhole:
    sent = ()

    def __init__(self, parts, n, name, shifts=False):
        self.parts = parts

    def stage_z(self, *deps):
        return []

    stage_core = stage_rest = stage_xy = stage_z

    def results(self, *deps):
        rows = self.parts[0].shape[1] // (2 * lax.axis_size("shard"))
        return [reduce_whole(p.reshape(-1, rows, p.shape[2]).astype(F32)) for p in self.parts]


def dot(a, b):
    return jnp.dot(a, b, preferred_element_type=F32)


def dot_nt(a, b):
    return lax.dot_general(a, b, NT_DIMS, preferred_element_type=F32)


def dot_tn(a, b):
    return lax.dot_general(a, b, TN_DIMS, preferred_element_type=F32)


def low_lanes(shape):
    return lax.broadcasted_iota(jnp.int32, shape, 1) % 128 < 64


def keep_low(v):
    return jnp.where(low_lanes(v.shape), v, jnp.zeros_like(v))


def keep_high(v):
    return jnp.where(low_lanes(v.shape), jnp.zeros_like(v), v)


def swap_halves(v):
    return jnp.concatenate([v[:, 64:], v[:, :64]], axis=1)


def norm_parts(x):
    centred = x - jnp.mean(x, axis=-1, keepdims=True)
    rstd = lax.rsqrt(jnp.mean(centred * centred, axis=-1, keepdims=True) + EPSILON)
    return centred * rstd, rstd


def norm_back(x, gain, up):
    unit, rstd = norm_parts(x)
    w = up * gain
    inner = jnp.mean(w * unit, axis=-1, keepdims=True)
    down = rstd * (w - jnp.mean(w, axis=-1, keepdims=True) - unit * inner)
    return down, jnp.sum(up * unit, axis=0, keepdims=True), jnp.sum(up, axis=0, keepdims=True)


def weight_copies(meta, bufs, w_refs, sems, n, back=False, shifts=False, first_column=0):
    moves = []
    if bufs[0].shape == w_refs[0].shape:
        moves = list(zip(bufs, w_refs))
    else:
        x, y, c = meta[0], meta[1], meta[2]
        rows = w_refs[0].shape[1] // (2 * n)
        groups = {}
        cols = slice(first_column, w_refs[0].shape[2])
        for dc in range(2):
            first = 0
            for k, (dx, dy, blocks) in enumerate(layout(len(w_refs), n)):
                tp = 2 * (x ^ dx) + (c ^ dc)
                for i, (z, chunk) in enumerate(blocks):
                    if shifts:
                        z = lax.rem(meta[3] + z, n)
                    row = pl.multiple_of((z * 2 + (y ^ dy)) * rows, rows)
                    piece = bufs[dc].at[first + i] if back else bufs[dc * 5 + k].at[i, 0:rows, cols]
                    whole = w_refs[chunk].at[tp, pl.ds(row, rows), cols]
                    groups.setdefault((dx, dc), []).append((piece, whole))
                first += len(blocks)
        moves = [m for g in sorted(groups) for m in groups[g]]
    if back:
        moves = [(whole, piece) for piece, whole in moves]
    return [pltpu.make_async_copy(*m, sems.at[i]) for i, m in enumerate(moves)]


def copy_sems(sz, chunks):
    return pltpu.SemaphoreType.DMA((8 * chunks * sz["n"],))


def start_all(copies):
    for c in copies:
        c.start()


def wait_all(copies):
    for c in copies:
        c.wait()


def take_blocks(blocks, dst, places):
    for k, blk in enumerate(blocks):
        dx, dy = k % 2, k // 2
        for f in range(2):
            row = (2 * dx + f) * 2 * PAD + dy * PAD
            dst[row + PAD - 8 : row + PAD, :] = jnp.zeros((8, dst.shape[1]), dst.dtype)
            dst[row : row + places, :] = blk[f].astype(dst.dtype)


def give_blocks(src, blocks, places):
    for k, blk in enumerate(blocks):
        dx, dy = k % 2, k // 2
        for f in range(2):
            row = (2 * dx + f) * 2 * PAD + dy * PAD
            blk[f] = src[row : row + places, :].astype(blk.dtype)


def project_heads(normed, w_ref, q_out, kv_out):
    @pl.loop(0, 2)
    def _(u):
        thirds = []
        for t in (2 * u, 2 * u + 1):
            xn = normed[...]
            y = dot(xn, w_ref[t, :, 0:512]).astype(B16)
            q_out[t] = y[:, 0:128]
            kv_out[t] = y[:, 128:256]
            kv_out[6 + t] = y[:, 256:384]
            thirds.append((y[:, 384:512], dot(xn, w_ref[t, :, 640:768]).astype(B16)))
        (a3, a5), (b3, b5) = thirds
        low = low_lanes(a3.shape)
        q_out[4 + u] = jnp.where(low, a3, b3)
        kv_out[4 + u] = swap_halves(jnp.where(low, b3, a3))
        kv_out[10 + u] = swap_halves(jnp.where(low, b5, a5))


def third_head(v, t):
    return keep_low(v) if t % 2 == 0 else keep_high(v)


def project_out(mixed, w_ref, stream, bias, out):
    for n in range(3):
        cols = slice(256 * n, 256 * n + 256)
        acc = stream[:, cols] + bias[:, cols]
        for t in range(4):
            m = jnp.concatenate([mixed[t], third_head(mixed[4 + t // 2], t)], axis=1)
            acc = acc + dot_nt(m, w_ref[t, cols, 512:768])
        out[:, cols] = acc


class Late:
    def __init__(self, source, ref, sem):
        self.ref, self.copy = ref, pltpu.make_async_copy(source, ref, sem)
        self.copy.start()

    def get(self):
        self.copy.wait()
        return self.ref


class Early:
    def __init__(self, ref, target, sem):
        self.ref, self.copy = ref, pltpu.make_async_copy(ref, target, sem)

    def send(self):
        self.copy.start()


def run(kernel, name, ins, outs, scratch, micros):
    space = {
        "v": pl.BlockSpec(memory_space=pltpu.VMEM),
        "s": pl.BlockSpec(memory_space=pltpu.SMEM),
        "a": pl.BlockSpec(memory_space=pl.ANY),
    }
    space["l"] = space["e"] = space["a"]
    late = [i for i, (_, k) in enumerate(ins) if k == "l"]
    early = [i for i, (_, _, k) in enumerate(outs) if k == "e"]
    extra = [pltpu.VMEM(ins[i][0].shape, ins[i][0].dtype) for i in late]
    extra += [pltpu.VMEM(outs[i][0], outs[i][1]) for i in early]
    if extra:
        extra.append(pltpu.SemaphoreType.DMA((len(extra),)))

    def body(*refs):
        refs = list(refs)
        held = refs[len(ins) + len(outs) + len(scratch) :]
        refs = refs[: len(ins) + len(outs) + len(scratch)]
        for j, i in enumerate(late):
            refs[i] = Late(refs[i], held[j], held[-1].at[j])
        for j, i in enumerate(early, len(late)):
            refs[len(ins) + i] = Early(held[j], refs[len(ins) + i], held[-1].at[j])
        kernel(*refs)
        for i in early:
            refs[len(ins) + i].copy.wait()

    return pl.pallas_call(
        body,
        name=name,
        in_specs=[space[s] for _, s in ins],
        out_specs=[space[s] for _, _, s in outs],
        out_shape=[jax.ShapeDtypeStruct(s, d) for s, d, _ in outs],
        scratch_shapes=list(scratch) + extra,
        compiler_params=pltpu.CompilerParams(vmem_limit_bytes=VMEM_LIMIT),
        cost_estimate=pl.CostEstimate(
            flops=micros * 10**9, bytes_accessed=micros * 3 * 10**6, transcendentals=0
        ),
    )(*[a for a, _ in ins])


def row_slices(r, step=208):
    return pl.ds(pl.multiple_of(r * step, step), step)


VECTORS = 9


def norm_vectors(sz, meta, weights):
    d, n, nw = sz["d"], sz["n"], len(weights)
    count, rows = 8 * n, d // (2 * n)
    per = d // count
    hidden = VECTORS * per

    def kernel(*refs):
        meta, bufs = refs[0], refs[1 : 1 + nw]
        out, shares, sems = refs[1 + nw :]
        x, y, c = meta[0], meta[1], meta[2]
        copies = []
        for dc in range(2):
            for k, (dx, dy, blocks) in enumerate(layout(1, n)):
                tp = 2 * (x ^ dx) + (c ^ dc)
                for i, (z, _) in enumerate(blocks):
                    dev = (z * 2 + (y ^ dy)) * 4 + tp
                    piece = bufs[dc * 5 + k].at[i, rows : rows + 8, :]
                    copies.append(
                        pltpu.make_async_copy(piece, shares.at[dev], sems.at[len(copies)])
                    )
        start_all(copies)
        lane = lax.broadcasted_iota(jnp.int32, (128, d), 1)
        row = lax.broadcasted_iota(jnp.int32, (128, d), 0)
        one = ((lane % per == row) & (row < per)).astype(F32).astype(B16)
        four = ((lane % (4 * per) == row) & (row < 4 * per)).astype(F32).astype(B16)
        dev = lax.broadcasted_iota(jnp.int32, (count, d), 0)
        lanes = lax.broadcasted_iota(jnp.int32, (count, d), 1)
        mine = lanes // per == dev
        ours = lanes // (4 * per) == dev % 8
        wait_all(copies)
        rows_in = shares[:, 0, :].astype(F32)
        pad = jnp.zeros((count, 128), F32)
        rows_in = jnp.concatenate([rows_in, pad], axis=1)

        def spread(first, pick):
            parts = [rows_in[:, o + first : o + first + 128].astype(B16) for o in (0, 384)]
            return dot(parts[0], pick) + dot(parts[1], pick)

        for v in range(VECTORS):
            got = jnp.where(mine, spread(v * per, one), 0.0)
            out[v : v + 1, :] = jnp.sum(got, axis=0, keepdims=True)
        got = jnp.where(ours, spread(hidden, four), 0.0)
        for t in range(4):
            part = got[t * 8 : t * 8 + 8] if count == 32 else got
            out[VECTORS + t : VECTORS + t + 1, :] = jnp.sum(part, axis=0, keepdims=True)

    ins = [(meta, "s")] + [(w, "a") for w in weights]
    outs = [((16, d), F32, "v")]
    scratch = [pltpu.VMEM((count, 8, d), B16), copy_sems(sz, 1)]
    return run(kernel, "norm_vectors", ins, outs, scratch, 2)[0]


def time_qkv(sz, meta, vec, blocks, weights):
    rows, d = sz["rows"], sz["d"]
    nb, nw = len(blocks), len(weights)

    def kernel(*refs):
        meta, vec = refs[0], refs[1]
        blks, bufs = refs[2 : 2 + nb], refs[2 + nb : 2 + nb + nw]
        x, normed, q, kv, w, sems = refs[2 + nb + nw :]
        copies = weight_copies(meta, bufs, [w], sems, sz["n"])
        start_all(copies)
        take_blocks(blks, x, sz["places"])

        @pl.loop(0, 4)
        def _(r):
            at = row_slices(r)
            unit, _ = norm_parts(x[at, :])
            normed[at, :] = (unit * vec[0:1, :] + vec[1:2, :]).astype(B16)

        wait_all(copies)
        project_heads(normed, w, q, kv)

    ins = [(meta, "s"), (vec, "v")] + [(b, "v") for b in blocks] + [(w, "a") for w in weights]
    outs = [
        ((rows, d), F32, "v"),
        ((rows, d), B16, "v"),
        ((6, rows, 128), B16, "v"),
        ((12, rows, 128), B16, "v"),
    ]
    scratch = [pltpu.VMEM((4, d, d), B16), copy_sems(sz, 1)]
    return run(kernel, "time_qkv", ins, outs, scratch, 12)


def head_sums(ref):
    for f in range(4):
        for j in range(6):
            col = lax.broadcasted_iota(jnp.int32, (128, 128), 1)
            lane = lax.broadcasted_iota(jnp.int32, (128, 128), 0)
            hit = col == 16 * f + 2 * j + lane // 64
            ref[(f * 6 + j) * 128 : (f * 6 + j) * 128 + 128, :] = hit.astype(F32).astype(B16)


def head_spreads(ref):
    for f in range(4):
        for j in range(6):
            row = lax.broadcasted_iota(jnp.int32, (128, 128), 0)
            lane = lax.broadcasted_iota(jnp.int32, (128, 128), 1)
            hit = row == 16 * f + 2 * j + lane // 64
            ref[:, (f * 6 + j) * 128 : (f * 6 + j) * 128 + 128] = hit.astype(F32).astype(B16)


def pair_sums(a_ref, b_ref, b_tile, g, sums):
    at = row_slices(g)
    products = [
        a_ref[j, f * 208 : f * 208 + 208, :] * b_ref[b_tile + j, at, :]
        for f in range(4)
        for j in range(6)
    ]
    return dot(jnp.concatenate(products, axis=1), sums[...])


def two_tiles(ref, tile, at):
    return jnp.concatenate([ref[tile, at, :], ref[tile + 1, at, :]], axis=1).astype(F32)


def time_mix(sz, meta, vec, stream, q, kv, kvo, weights):
    rows, d = sz["rows"], sz["d"]
    nw = len(weights)

    def kernel(*refs):
        meta, vec, stream, q, kv, kvo = refs[:6]
        bufs = refs[6 : 6 + nw]
        mixed_out, out, prob_out, w, sums, spreads, acc, sems = refs[6 + nw :]
        mixed, prob = mixed_out.ref, prob_out.ref
        copies = weight_copies(meta, bufs, [w], sems, sz["n"], first_column=512)
        start_all(copies)
        head_sums(sums)
        head_spreads(spreads)
        for h in range(2):
            if h == 1:
                kvo = kvo.get()
            ref = (kv, kvo)[h]

            @pl.loop(0, 4)
            def _(g, ref=ref, h=h):
                prob[4 * h + g] = pair_sums(q, ref, 0, g, sums) * SCALING

        @pl.loop(0, 13)
        def _(r):
            at = row_slices(r, 16)
            s = [prob[g, at, :] for g in range(8)]
            top = functools.reduce(jnp.maximum, s)
            e = [jnp.exp(v - top) for v in s]
            inv = 1.0 / functools.reduce(lambda a, b: a + b, e)
            for g in range(8):
                prob[g, at, :] = e[g] * inv

        prob_out.send()
        acc[...] = jnp.zeros_like(acc)
        for h, ref in enumerate((kv, kvo)):

            @pl.loop(0, 4)
            def _(g):
                at = row_slices(g)
                p = prob[4 * h + g].astype(B16)
                for jj in range(3):
                    v = two_tiles(ref, 6 + 2 * jj, at)
                    for f in range(4):
                        lanes = slice(f * d + 256 * jj, f * d + 256 * jj + 256)
                        acc[f * 208 : f * 208 + 208, 256 * jj : 256 * jj + 256] += (
                            dot(p, spreads[:, lanes]) * v
                        )

        for j in range(6):
            mixed[j] = acc[:, 128 * j : 128 * j + 128].astype(B16)
        mixed_out.send()
        wait_all(copies)
        project_out(mixed, w, stream.get(), vec[2:3, :], out)

    ins = [(meta, "s"), (vec, "v"), (stream, "l"), (q, "v"), (kv, "v"), (kvo, "l")]
    ins += [(w, "a") for w in weights]
    outs = [((6, rows, 128), B16, "e"), ((rows, d), F32, "v"), ((8, 208, 128), F32, "e")]
    scratch = [
        pltpu.VMEM((4, d, d), B16),
        pltpu.VMEM((4 * d, 128), B16),
        pltpu.VMEM((128, 4 * d), B16),
        pltpu.VMEM((rows, d), F32),
        copy_sems(sz, 1),
    ]
    return run(kernel, "time_mix", ins, outs, scratch, 17)


def space_mask(places):
    return lax.broadcasted_iota(jnp.int32, (208, 208), 0) % PAD < places


def space_qkv(sz, meta, vec, stream, weights):
    rows, d = sz["rows"], sz["d"]
    nw = len(weights)

    def kernel(*refs):
        meta, vec, stream = refs[:3]
        bufs = refs[3 : 3 + nw]
        normed, q, kv, w, sems = refs[3 + nw :]
        copies = weight_copies(meta, bufs, [w], sems, sz["n"])
        start_all(copies)

        @pl.loop(0, 4)
        def _(r):
            at = row_slices(r)
            unit, _ = norm_parts(stream[at, :])
            normed[at, :] = (unit * vec[3:4, :] + vec[4:5, :]).astype(B16)

        wait_all(copies)
        project_heads(normed, w, q, kv)

    ins = [(meta, "s"), (vec, "v"), (stream, "v")] + [(w, "a") for w in weights]
    outs = [((rows, d), B16, "v"), ((6, rows, 128), B16, "v"), ((12, rows, 128), B16, "v")]
    scratch = [pltpu.VMEM((4, d, d), B16), copy_sems(sz, 1)]
    return run(kernel, "space_qkv", ins, outs, scratch, 12)


def space_mix(sz, meta, vec, stream, q, kv, weights):
    rows, d, places = sz["rows"], sz["d"], sz["places"]
    nw = len(weights)

    def kernel(*refs):
        meta, vec, stream, q, kv = refs[:5]
        bufs = refs[5 : 5 + nw]
        mixed_out, logs, out, w, sems = refs[5 + nw :]
        mixed = mixed_out.ref
        copies = weight_copies(meta, bufs, [w], sems, sz["n"], first_column=512)
        start_all(copies)

        def mix(j, f):
            at = row_slices(f)
            qj, kj, vj = q[j, at, :], kv[j, at, :], kv[6 + j, at, :]
            mask = space_mask(places)
            o = None
            for h, keep in enumerate((keep_low, keep_high)):
                s = jnp.where(mask, dot_nt(kj, keep(qj)) * SCALING, NEGATIVE)
                top = jnp.max(s, axis=0, keepdims=True)
                e = jnp.exp(s - top)
                size = jnp.sum(e, axis=0, keepdims=True)
                logs[j * 4 + f, h : h + 1, :] = top + jnp.log(size)
                part = dot_tn((e * (1.0 / size)).astype(B16), keep(vj))
                o = part if o is None else o + part
            return o.astype(B16)

        @pl.loop(0, 6)
        def _(j):
            @pl.loop(0, 2)
            def _(g):
                pair = [mix(j, 2 * g + i) for i in range(2)]
                for i in range(2):
                    mixed[j, row_slices(2 * g + i), :] = pair[i]

        mixed_out.send()
        wait_all(copies)
        project_out(mixed, w, stream.get(), vec[5:6, :], out)

    ins = [(meta, "s"), (vec, "v"), (stream, "l"), (q, "v"), (kv, "v")]
    ins += [(w, "a") for w in weights]
    outs = [((6, rows, 128), B16, "e"), ((24, 8, 208), F32, "v"), ((rows, d), F32, "v")]
    scratch = [pltpu.VMEM((4, d, d), B16), copy_sems(sz, 1)]
    return run(kernel, "space_mix", ins, outs, scratch, 17)


def gradient_outs(sz, chunks, fast):
    d, n = sz["d"], sz["n"]
    if not fast:
        return [((4, d, d), B16, "a")] * chunks
    return [((4 * chunks * n, d // (2 * n), d), B16, "a")] * 2


def gelu_pair(x):
    half = 0.5 * (1.0 + lax.erf(x * 0.7071067811865476))
    slope = half + x * (0.3989422804014327 * jnp.exp(-0.5 * x * x))
    return x * half, slope


def feed_forward(sz, meta, vec, stream, blocks, weights, fast):
    rows, d, places = sz["rows"], sz["d"], sz["places"]
    nb, nw = len(blocks), len(weights)
    g_outs = gradient_outs(sz, 2, fast)
    ng = len(g_outs)

    def kernel(*refs):
        meta, vec, stream = refs[:3]
        blks = refs[3 : 3 + nb]
        refs = refs[3 + nb :]
        bufs, refs = refs[:nw], refs[nw:]
        res, refs = refs[:nb], refs[nb:]
        d2, vgrad = refs[0], refs[1]
        g_bufs, refs = refs[2 : 2 + ng], refs[2 + ng :]
        w1, w2, dw1, dw2, dz, dzr, normed, act, dpre, y, dn, sems, back_sems = refs
        copies = weight_copies(meta, bufs, [w1, w2], sems, sz["n"])
        start_all(copies)
        take_blocks(blks, dz, places)
        vgrad[...] = jnp.zeros_like(vgrad)

        @pl.loop(0, 4)
        def _(r):
            at = pl.ds(pl.multiple_of(r * 208, 208), 208)
            unit, _ = norm_parts(stream[at, :])
            normed[at, :] = (unit * vec[6:7, :] + vec[7:8, :]).astype(B16)
            up = dz[at, :]
            dzr[at, :] = up.astype(B16)
            vgrad[2:3, :] += jnp.sum(up, axis=0, keepdims=True)
            y[at, :] = stream[at, :] + vec[8:9, :]
            dn[at, :] = jnp.zeros_like(up)

        back = weight_copies(meta, g_bufs, [dw1, dw2], back_sems, sz["n"], back=True)
        group = len(copies) // 4
        if not fast:
            wait_all(copies)

        @pl.loop(0, 4)
        def _(k):
            t = k
            if fast:
                t = 2 * (meta[0] ^ (k // 2)) + (meta[2] ^ (k % 2))
                rows_here = w1.shape[1] // (2 * sz["n"])
                piece = (bufs[0].at[0, 0:rows_here, :], w1.at[0, 0:rows_here, :])
                for i in range(group):
                    pltpu.make_async_copy(*piece, sems.at[k * group + i]).wait()
            thirds = [slice(256 * i, 256 * i + 256) for i in range(3)]
            for cols in thirds:
                pre = dot(normed[...], w1[t, :, cols]) + vec[pl.ds(9 + t, 1), cols]
                a, slope = gelu_pair(pre)
                act[:, cols] = a.astype(B16)
                g = (dot(dzr[...], w2[t, :, cols]) * slope).astype(B16)
                dpre[:, cols] = g
                vgrad[pl.ds(4 + t, 1), cols] += jnp.sum(g.astype(F32), axis=0, keepdims=True)
            for cols in thirds:
                y[:, cols] += dot_nt(act[...], w2[t, cols, :])
                dn[:, cols] += dot_nt(dpre[...], w1[t, cols, :])
            for cols in thirds:
                dw1[t, :, cols] = dot_tn(normed[...], dpre[:, cols]).astype(B16)
                dw2[t, :, cols] = dot_tn(dzr[...], act[:, cols]).astype(B16)
            if fast:
                for i in range(4):
                    pl.when(k == i)(lambda i=i: start_all(back[i * group : i * group + group]))

        if not fast:
            start_all(back)
        give_blocks(y, res, places)

        @pl.loop(0, 4)
        def _(r):
            at = pl.ds(pl.multiple_of(r * 208, 208), 208)
            down, gg, gs = norm_back(stream[at, :], vec[6:7, :], dn[at, :])
            d2[at, :] = dz[at, :] + down
            vgrad[0:1, :] += gg
            vgrad[1:2, :] += gs

        wait_all(back)

    ins = [(meta, "s"), (vec, "v"), (stream, "v")] + [(b, "v") for b in blocks]
    ins += [(w, "a") for w in weights]
    outs = [((2, places, d), B16, "v")] * nb + [((rows, d), F32, "v"), ((8, d), F32, "v")]
    outs += g_outs
    scratch = [pltpu.VMEM((4, d, d), B16)] * 4
    scratch += [pltpu.VMEM((rows, d), F32), pltpu.VMEM((rows, d), B16), pltpu.VMEM((rows, d), B16)]
    scratch += [pltpu.VMEM((rows, d), B16)] * 2 + [pltpu.VMEM((rows, d), F32)] * 2
    scratch += [copy_sems(sz, 2)] * 2
    r = run(kernel, "feed_forward", ins, outs, scratch, 47)
    return r[:nb], r[nb], r[nb + 1], r[nb + 2 :]


def mixed_slopes(up, w_ref, dm):
    for u in range(2):
        thirds = []
        for t in (2 * u, 2 * u + 1):
            v = dot(up[...], w_ref[t, :, 512:768]).astype(B16)
            dm[t] = v[:, 0:128]
            thirds.append(v[:, 128:256])
        dm[4 + u] = jnp.where(low_lanes(thirds[0].shape), *thirds)


def place_third(dq, dk, dv, dy, u, at):
    k, v = swap_halves(dk), swap_halves(dv)
    low = low_lanes(dq.shape)
    dy[2 * u, at, 384:512] = jnp.where(low, dq, k)
    dy[2 * u + 1, at, 384:512] = jnp.where(low, k, dq)
    dy[2 * u, at, 512:640] = keep_high(v)
    dy[2 * u + 1, at, 512:640] = keep_low(v)


def third_head_of(v, odd):
    return jnp.where(low_lanes(v.shape) == (odd == 0), v, jnp.zeros_like(v))


def output_gradients(dw, up, mixed):
    @pl.loop(0, 4)
    def _(t):
        third = third_head_of(mixed[4 + t // 2], t % 2)
        out = dot_tn(up[...], jnp.concatenate([mixed[t], third], axis=1))
        dw[t, :, 512:768] = out.astype(B16)


def head_gradients(t, dw, normed, dy):
    dw[t, :, 0:512] = dot_tn(normed[...], dy[t, :, 0:512]).astype(B16)
    third = dot_tn(normed[...], dy[t, :, 512:640])
    dw[t, :, 640:768] = (dw[t, :, 640:768].astype(F32) + third).astype(B16)


def norm_slopes(t, dy, w_ref, out):
    for n in range(3):
        cols = slice(256 * n, 256 * n + 256)
        part = dot_nt(dy[t, :, 0:512], w_ref[t, cols, 0:512])
        out[:, cols] += part + dot_nt(dy[t, :, 512:640], w_ref[t, cols, 640:768])


def space_backward_scores(sz, meta, d2, q, kv, logs, weights):
    rows, d, places = sz["rows"], sz["d"], sz["places"]
    nw = len(weights)

    def kernel(*refs):
        meta, d2, q, kv, logs = refs[:5]
        bufs, refs = refs[5 : 5 + nw], refs[5 + nw :]
        up_out, dy, w, dm, third, sems = refs
        up = up_out.ref
        copies = weight_copies(meta, bufs, [w], sems, sz["n"], first_column=512)
        start_all(copies)

        @pl.loop(0, 4)
        def _(r):
            up[row_slices(r), :] = d2[row_slices(r), :].astype(B16)

        wait_all(copies)
        up_out.send()
        mixed_slopes(up, w, dm)
        q, kv, logs = q.get(), kv.get(), logs.get()

        def slopes(j, at, f):
            qj, kj, vj, mj = q[j, at, :], kv[j, at, :], kv[6 + j, at, :], dm[j, at, :]
            mask = space_mask(places)
            dq = dk = dv = None
            for h, keep in enumerate((keep_low, keep_high)):
                qh, mh = keep(qj), keep(mj)
                s = dot_nt(kj, qh) * SCALING - logs[j * 4 + f, h : h + 1, :]
                p = jnp.exp(jnp.where(mask, s, NEGATIVE))
                dp = dot_nt(vj, mh)
                inner = jnp.sum(p * dp, axis=0, keepdims=True)
                ds = (p * (dp - inner) * SCALING).astype(B16)
                a, b, c = dot_tn(ds, keep(kj)), dot(ds, qh), dot(p.astype(B16), mh)
                dq, dk, dv = (a, b, c) if dq is None else (dq + a, dk + b, dv + c)
            return dq.astype(B16), dk.astype(B16), dv.astype(B16)

        @pl.loop(0, 4)
        def _(j):
            @pl.loop(0, 2)
            def _(g):
                ats = [row_slices(2 * g + i) for i in range(2)]
                pair = [slopes(j, ats[i], 2 * g + i) for i in range(2)]
                for at, (dq, dk, dv) in zip(ats, pair):
                    dy[j, at, 0:128] = dq
                    dy[j, at, 128:256] = dk
                    dy[j, at, 256:384] = dv

        @pl.loop(0, 2)
        def _(u):
            @pl.loop(0, 2)
            def _(g):
                ats = [row_slices(2 * g + i) for i in range(2)]
                pair = [slopes(4 + u, ats[i], 2 * g + i) for i in range(2)]
                for at, v in zip(ats, pair):
                    place_third(*v, dy, u, at)

    ins = [(meta, "s")] + [(d2, "v")] + [(v, "l") for v in (q, kv, logs)] + [(w, "a") for w in weights]
    outs = [((rows, d), B16, "e"), ((4, rows, 640), B16, "v")]
    scratch = [pltpu.VMEM((4, d, d), B16), pltpu.VMEM((6, rows, 128), B16)]
    scratch += [pltpu.VMEM((rows, 128), B16), copy_sems(sz, 1)]
    return run(kernel, "space_backward_scores", ins, outs, scratch, 30)


def weight_slopes(sz, name, meta, up, normed, mixed, slopes, fast):
    rows, d = sz["rows"], sz["d"]
    g_outs = gradient_outs(sz, 1, fast)
    join = len(slopes) == 3

    def kernel(*refs):
        meta, up, normed, mixed = refs[:4]
        given, refs = refs[4 : 4 + len(slopes)], refs[4 + len(slopes) :]
        dy = refs[0].ref if join else given[0]
        g_bufs, (dw, sems) = refs[1 if join else 0 : -2], refs[-2:]
        if join:
            dq, dkv, got = given

            def both(j, at):
                return (dkv[j, at, :].astype(F32) + got[j, at, :].astype(F32)).astype(B16)

            @pl.loop(0, 4)
            def _(r):
                at = row_slices(r)
                for j in range(4):
                    dy[j, at, 0:128] = dq[j, at, :]
                    dy[j, at, 128:256] = both(j, at)
                    dy[j, at, 256:384] = both(6 + j, at)
                for u in range(2):
                    place_third(dq[4 + u, at, :], both(4 + u, at), both(10 + u, at), dy, u, at)

            refs[0].send()
        back = weight_copies(meta, g_bufs, [dw], sems, sz["n"], back=True, shifts=join)
        group = len(back) // 4
        output_gradients(dw, up.get(), mixed.get())
        normed = normed.get()
        if not join:
            dy = dy.get()

        @pl.loop(0, 4)
        def _(k):
            t = 2 * (meta[0] ^ (k // 2)) + (meta[2] ^ (k % 2)) if fast else k
            head_gradients(t, dw, normed, dy)
            if fast:
                for i in range(4):
                    pl.when(k == i)(lambda i=i: start_all(back[i * group : i * group + group]))

        if not fast:
            start_all(back)
        wait_all(back)

    ins = [(meta, "s")] + [(v, "l") for v in (up, normed, mixed)]
    ins += [(v, "v" if join else "l") for v in slopes]
    outs = ([((4, rows, 640), B16, "e")] if join else []) + g_outs
    scratch = [pltpu.VMEM((4, d, d), B16), copy_sems(sz, 1)]
    return run(kernel, name, ins, outs, scratch, 14)


def input_slopes(sz, name, meta, vec, up, stream, dy, weights, gain_row, blocks):
    rows, d, places = sz["rows"], sz["d"], sz["places"]
    nw = len(weights)

    def kernel(*refs):
        meta, vec, up, stream, dy = refs[:5]
        bufs, refs = refs[5 : 5 + nw], refs[5 + nw :]
        w, dn, sems = refs[-3:]
        if blocks:
            outs, vgrad, dx = refs[:4], refs[4], refs[5]
        else:
            dx, vgrad = refs[:2]
        copies = weight_copies(meta, bufs, [w], sems, sz["n"])
        start_all(copies)
        vgrad[...] = jnp.zeros_like(vgrad)
        dn[...] = jnp.zeros_like(dn)
        fast = nw > 1
        group = len(copies) // 4
        if not fast:
            wait_all(copies)

        @pl.loop(0, 4)
        def _(k):
            t = k
            if fast:
                t = 2 * (meta[0] ^ (k // 2)) + (meta[2] ^ (k % 2))
                rows_here = w.shape[1] // (2 * sz["n"])
                piece = (bufs[0].at[0, 0:rows_here, :], w.at[0, 0:rows_here, :])
                for i in range(group):
                    pltpu.make_async_copy(*piece, sems.at[k * group + i]).wait()
            norm_slopes(t, dy, w, dn)

        up, stream = up.get(), stream.get()

        @pl.loop(0, 4)
        def _(r):
            at = row_slices(r)
            v = up[at, :]
            gain = vec[gain_row : gain_row + 1, :]
            down, gg, gs = norm_back(stream[at, :], gain, dn[at, :])
            dx[at, :] = v + down
            vgrad[0:1, :] += gg
            vgrad[1:2, :] += gs
            vgrad[2:3, :] += jnp.sum(v, axis=0, keepdims=True)

        if blocks:
            give_blocks(dx, outs, places)

    ins = [(meta, "s"), (vec, "v"), (up, "l"), (stream, "l"), (dy, "v")]
    ins += [(w, "a") for w in weights]
    outs = [((rows, d), F32, "v")]
    scratch = []
    if blocks:
        outs = [((2, places, d), F32, "v")] + [((2, places, d), B16, "v")] * 3
        scratch = [pltpu.VMEM((rows, d), F32)]
    outs += [((8, d), F32, "v")]
    scratch += [pltpu.VMEM((4, d, d), B16), pltpu.VMEM((rows, d), F32), copy_sems(sz, 1)]
    return run(kernel, name, ins, outs, scratch, 14)


def time_backward_scores(sz, meta, d1, q, kv, kvo, prob, weights):
    rows, d = sz["rows"], sz["d"]
    nw = len(weights)

    def kernel(*refs):
        meta, d1, q, kv, kvo, prob = refs[:6]
        bufs, refs = refs[6 : 6 + nw], refs[6 + nw :]
        up_out, dq, dkv_out, dkvo, w, dm, sums, spreads, ds, acc, sems = refs
        up, dkv = up_out.ref, dkv_out.ref
        copies = weight_copies(meta, bufs, [w], sems, sz["n"], first_column=512)
        start_all(copies)
        head_sums(sums)
        head_spreads(spreads)

        @pl.loop(0, 4)
        def _(r):
            up[row_slices(r), :] = d1[row_slices(r), :].astype(B16)

        wait_all(copies)
        up_out.send()
        mixed_slopes(up, w, dm)
        q, kv, kvo, prob = q.get(), kv.get(), kvo.get(), prob.get()
        for h, ref in enumerate((kv, kvo)):

            @pl.loop(0, 4)
            def _(g):
                ds[4 * h + g] = pair_sums(dm, ref, 6, g, sums)

        @pl.loop(0, 13)
        def _(r):
            at = row_slices(r, 16)
            p = [prob[g, at, :] for g in range(8)]
            dp = [ds[g, at, :] for g in range(8)]
            inner = functools.reduce(lambda a, b: a + b, [a * b for a, b in zip(p, dp)])
            for g in range(8):
                ds[g, at, :] = p[g] * (dp[g] - inner) * SCALING

        acc[...] = jnp.zeros_like(acc)
        for h, (ref, out) in enumerate(((kv, dkv), (kvo, dkvo))):

            @pl.loop(0, 4)
            def _(g):
                at = row_slices(g)
                both = jnp.concatenate([ds[4 * h + g], prob[4 * h + g]], axis=0).astype(B16)
                for jj in range(3):
                    k = two_tiles(ref, 2 * jj, at)
                    dk = dv = None
                    for f in range(4):
                        fr = slice(f * 208, f * 208 + 208)
                        e = dot(both, spreads[:, f * d + 256 * jj : f * d + 256 * jj + 256])
                        se, pe = e[:208], e[208:]
                        acc[fr, 256 * jj : 256 * jj + 256] += se * k
                        a = se * two_tiles(q, 2 * jj, fr)
                        b = pe * two_tiles(dm, 2 * jj, fr)
                        dk, dv = (a, b) if dk is None else (dk + a, dv + b)
                    dk, dv = dk.astype(B16), dv.astype(B16)
                    for i in range(2):
                        out[2 * jj + i, at, :] = dk[:, 128 * i : 128 * i + 128]
                        out[6 + 2 * jj + i, at, :] = dv[:, 128 * i : 128 * i + 128]

            if h == 0:
                dkv_out.send()

        for j in range(6):
            dq[j] = acc[:, 128 * j : 128 * j + 128].astype(B16)

    ins = [(meta, "s")] + [(d1, "v")] + [(v, "l") for v in (q, kv, kvo, prob)] + [(w, "a") for w in weights]
    outs = [
        ((rows, d), B16, "e"),
        ((6, rows, 128), B16, "v"),
        ((12, rows, 128), B16, "e"),
        ((12, rows, 128), B16, "v"),
    ]
    scratch = [
        pltpu.VMEM((4, d, d), B16),
        pltpu.VMEM((6, rows, 128), B16),
        pltpu.VMEM((4 * d, 128), B16),
        pltpu.VMEM((128, 4 * d), B16),
        pltpu.VMEM((8, 208, 128), F32),
        pltpu.VMEM((rows, d), F32),
        copy_sems(sz, 1),
    ]
    return run(kernel, "time_backward_scores", ins, outs, scratch, 23)


def pack_heads(qkv, proj, odd):
    q, k, v = qkv[:, 0], qkv[:, 1], qkv[:, 2]
    o = proj.T
    first = [q[:, :128], k[:, :128], v[:, :128]]
    even = first + [q[:, 128:], k[:, 128:], o[:, :128], o[:, 128:], v[:, 128:]]
    other = first + [k[:, 128:], q[:, 128:], o[:, :128], v[:, 128:], o[:, 128:]]
    return jnp.where(odd, jnp.concatenate(other, axis=1), jnp.concatenate(even, axis=1))


def unpack_heads(g, odd):
    def pick(a, b):
        return jnp.where(odd, g[:, b : b + 64], g[:, a : a + 64])

    q = jnp.concatenate([g[:, 0:128], pick(384, 448)], axis=1)
    k = jnp.concatenate([g[:, 128:256], pick(448, 384)], axis=1)
    v = jnp.concatenate([g[:, 256:384], pick(704, 640)], axis=1)
    o = jnp.concatenate([g[:, 512:640], pick(640, 704)], axis=1)
    return jnp.stack([q, k, v], axis=1), o.T


def local(mesh_shape, video, cotangent, *params):
    qkv_time, proj_time, qkv_space, proj_space, fc_in, fc_out = params[:6]
    vectors = params[6:]
    n = mesh_shape["shard"]
    d = proj_time.shape[0] * 4
    places = video.shape[2]
    rows_here = fc_in.shape[0]
    fast = rows_here % 16 == 0
    sz = {"n": n, "d": d, "places": places, "rows": 8 * PAD}
    x, y = lax.axis_index("x"), lax.axis_index("ctx")
    c, z = lax.axis_index("core"), lax.axis_index("shard")
    meta = jnp.stack([x, y, c, z]).astype(jnp.int32)
    every = ("shard", "ctx", "x", "core")
    count = 8 * n

    gather, reduce = (Gather, Reduce) if fast else (GatherWhole, ReduceWhole)
    per = d // count
    order = [0, 1, 2, 3, 4, 5, 6, 7, 9, 8]
    share = jnp.concatenate([vectors[i] for i in order])
    first_rows = pack_heads(qkv_time, proj_time, c == 1)
    if fast:
        kept = lax.reduce_precision(share, exponent_bits=8, mantissa_bits=7)
        high, low = kept.astype(B16), (share - kept).astype(B16)
        gap = jnp.zeros((384 - share.shape[0],), B16)
        row = jnp.concatenate([high, gap, low, gap])[None]
        first_rows = jnp.concatenate([first_rows, row, jnp.zeros((7, d), B16)], axis=0)

    def clips_of(v):
        return [
            lax.dynamic_index_in_dim(v, 2 * (x ^ dx) + (y ^ dy), 0, keepdims=False)
            for dx, dy in ((0, 0), (1, 0), (0, 1), (1, 1))
        ]

    def frames_back(blocks):
        return [blocks[0], over_x(blocks[1]), over_y(blocks[2]), over_xy(blocks[3])]

    def join_clips(blocks, dtype):
        out = jnp.zeros((4,) + blocks[0].shape, dtype)
        for k, b in enumerate(blocks):
            at = 2 * (x ^ (k % 2)) + (y ^ (k // 2))
            out = lax.dynamic_update_slice_in_dim(out, b.astype(dtype)[None], at, 0)
        return out

    g_t = gather([first_rows], n)
    g_s = gather([pack_heads(qkv_space, proj_space, c == 1)], n)
    g_m = gather([fc_in, fc_out.T], n)
    t_z = g_t.stage_z()
    cot_clips, video_clips = [clips_of(v) for v in after((cotangent, video), g_t.spread)]
    cot_blocks, video_blocks = frames_back(cot_clips), frames_back(video_clips)
    t_xy = g_t.stage_xy(*cot_blocks[1:], *video_blocks[1:3])
    s_z = g_s.stage_z(*t_z)
    t_rest = g_t.stage_rest()
    m_z = g_m.stage_z(*s_z)
    s_xy = g_s.stage_xy(*t_rest)
    w_time = g_t.stage_core()
    if fast:
        vec = norm_vectors(sz, meta, w_time)
    else:
        shares = lax.all_gather(share, every, axis=0, tiled=False)
        vec = shares[:, : VECTORS * per].reshape(count, VECTORS, per).transpose(1, 0, 2)
        hidden = shares[:, VECTORS * per :].reshape(4, d)
        vec = jnp.concatenate([vec.reshape(VECTORS, d), hidden, jnp.zeros((3, d), F32)], axis=0)
    vec_t = after(vec, *g_s.sent, g_m.spread)
    stream0, normed_t, q_t, kv_t = time_qkv(sz, meta, vec_t, video_blocks, w_time)

    kv_o = over_core(after(kv_t, *s_xy, *m_z))
    s_rest = g_s.stage_rest(kv_t)
    m_xy = g_m.stage_xy(kv_t)
    kv_o = after(kv_o, *s_rest, *g_m.sent)
    mixed_t, stream1, prob_t = time_mix(sz, meta, vec, stream0, q_t, kv_t, kv_o, w_time)

    w_space = g_s.stage_core()
    normed_s, q_s, kv_s = space_qkv(sz, meta, vec, stream1, w_space)
    m_rest = g_m.stage_rest(kv_s)
    kv_sb = after(kv_s, *g_m.sent)
    mixed_s, logs, stream2 = space_mix(sz, meta, vec, stream1, q_s, kv_sb, w_space)

    w_mlp = g_m.stage_core(stream2)
    res, d2, vg_m, parts_m = feed_forward(sz, meta, vec, stream2, cot_blocks, w_mlp, fast)

    r_m = reduce(parts_m, n, "mlp")
    m_core = r_m.stage_core()
    result_back = frames_back(res)
    up_s, dy_s = space_backward_scores(sz, meta, d2, q_s, kv_s, logs, w_space)

    m_rest = r_m.stage_rest(up_s)
    dy_s = after(dy_s, *result_back, *r_m.sent)
    parts_s = weight_slopes(sz, "space_weights", meta, up_s, normed_s, mixed_s, [dy_s], fast)
    r_s = reduce(parts_s, n, "space")
    s_core = r_s.stage_core(*m_rest)
    m_xy = r_m.stage_xy(*parts_s)
    d2b = after(d2, *parts_s, *r_m.sent)
    d1, vg_s = input_slopes(sz, "space_input", meta, vec, d2b, stream1, dy_s, w_space, 3, False)
    s_rest = r_s.stage_rest(d1)
    d1b = after(d1, *r_s.sent)
    up_t, dq, dkv, dkvo = time_backward_scores(sz, meta, d1b, q_t, kv_t, kv_o, prob_t, w_time)

    dkv_got = over_core(after(dkvo, *m_xy, *s_rest))
    first_z = ()
    if fast:
        r_m.xy = after(tuple(m_xy), dkvo)
        first_sent = joint_z([(r_m, 0)], n, "mlp_z")
        first_z = (over_z(first_sent),)
    s_xy = r_s.stage_xy(dkvo)
    dkv_got = after(dkv_got, *r_s.sent, first_sent) if fast else dkv_got
    dy_t, *parts_t = weight_slopes(
        sz, "time_weights", meta, up_t, normed_t, mixed_t, [dq, dkv, dkv_got], fast
    )

    r_t = reduce(parts_t, n, "time", True)
    t_core = r_t.stage_core(*s_xy, *first_z)
    t_rest = r_t.stage_rest()
    if fast:
        r_s.xy = after(tuple(s_xy), *r_t.sent)
        sent = joint_z([(r_s, 0), (r_m, 1)], n, "joint_z")
        got = over_z(sent)
    else:
        sent = ()
    t_xy = r_t.stage_xy(sent)
    d1c = after(d1, *r_t.sent)
    *dx, vg_t = input_slopes(sz, "time_input", meta, vec, d1c, stream0, dy_t, w_time, 0, True)

    t_z = r_t.stage_z(vg_t)
    vg_t2, result_back, dx = after((vg_t, tuple(result_back), tuple(dx)), *r_t.sent)
    video_back = frames_back(dx)
    if fast:
        vg_t2 = after(vg_t2, got)

    rows = jnp.concatenate([vg_t2[0:3], vg_s[0:3], vg_m[0:2]], axis=0)
    parts = jnp.concatenate(
        [
            rows.reshape(8, count, per).transpose(1, 0, 2).reshape(count, 8 * per),
            vg_m[4:8].reshape(count, 4 * per),
            vg_m[2].reshape(count, per),
        ],
        axis=1,
    )
    got_parts = lax.all_to_all(parts, every, split_axis=0, concat_axis=0, tiled=True)
    result = join_clips(result_back, B16)
    if fast:
        vec_got, video_back, r_t.z, joint, first = lax.optimization_barrier(
            (got_parts, tuple(video_back), tuple(r_t.z), got, first_z[0])
        )
        joint = jnp.sum(joint.astype(F32), axis=0)
        grad_s, grad_out = joint[0], joint[1]
        grad_in = jnp.sum(first.astype(F32), axis=0)[0]
    else:
        vec_got = got_parts
        grad_in, grad_out = r_m.results()
        (grad_s,) = r_s.results()
    (grad_t,) = r_t.results()
    grad_video = join_clips(video_back, F32)
    sums = jnp.sum(vec_got, axis=0)
    starts = [per * i for i in range(9)] + [per * 12]
    cuts = [sums[starts[i] : starts[i] + (4 * per if i == 8 else per)] for i in range(10)]

    qkv_t_grad, proj_t_grad = unpack_heads(grad_t, c == 1)
    qkv_s_grad, proj_s_grad = unpack_heads(grad_s, c == 1)
    return (
        result,
        grad_video,
        qkv_t_grad,
        proj_t_grad,
        qkv_s_grad,
        proj_s_grad,
        grad_in,
        grad_out.T,
        *cuts,
    )


def solution(mesh):
    shape = dict(mesh.shape)
    fine = Mesh(
        mesh.devices.reshape(shape["shard"], shape["ctx"], 2, shape["tp"] // 2),
        ("shard", "ctx", "x", "core"),
    )
    tp = ("x", "core")
    sc = ("shard", "ctx")
    tokens = P("shard", tp, "ctx", None)
    weights = (P(sc, None, tp), P(tp, sc), P(sc, None, tp), P(tp, sc), P(sc, tp), P(tp, sc))
    vectors = (P(("shard", "ctx", "x", "core")),) * 10
    return jax.shard_map(
        functools.partial(local, shape),
        mesh=fine,
        in_specs=(tokens, tokens) + weights + vectors,
        out_specs=(tokens, tokens) + weights + vectors,
        check_vma=False,
    )
```

```python
import functools

import jax
import jax.numpy as jnp
from jax import lax
from jax.experimental import pallas as pl
from jax.experimental.pallas import tpu as pltpu
from jax.sharding import Mesh
from jax.sharding import PartitionSpec as P

F32 = jnp.float32
B16 = jnp.bfloat16
HEAD_DIM = 64
SCALING = HEAD_DIM ** (-0.5)
EPSILON = 1e-06
NEGATIVE = -1e30
PAD = 104
NT_DIMS = (((1,), (1,)), ((), ()))
TN_DIMS = (((0,), (0,)), ((), ()))
FLIP = [(0, 1), (1, 0)]
VMEM_LIMIT = 64 * 1024 * 1024 - 65536


def over_x(v):
    return lax.ppermute(v, "x", FLIP)


def over_y(v):
    return lax.ppermute(v, "ctx", FLIP)


def over_xy(v):
    return lax.ppermute(v, ("ctx", "x"), [(i, 3 - i) for i in range(4)])


def over_core(v):
    return lax.ppermute(v, "core", FLIP)


def over_z(v):
    return lax.all_to_all(v, "shard", split_axis=0, concat_axis=0, tiled=True)


def after(values, *results):
    return lax.optimization_barrier((values, results))[0]


def layout(chunks, n):
    full = [(z, k) for z in range(n) for k in range(chunks)]
    h = len(full) // 2
    return [(0, 0, full), (1, 0, full), (0, 1, full), (1, 1, full[:h]), (1, 1, full[h:])]


class Gather:
    def __init__(self, owns, n):
        own = jnp.stack(owns)
        self.n = n
        self.spread = lax.optimization_barrier(jnp.broadcast_to(own[None], (n,) + own.shape))

    def stage_z(self, *deps):
        self.z = [over_z(after(self.spread, *deps))]
        return self.z

    def stage_xy(self, *deps):
        z = after(tuple(self.z), *deps)
        self.blk = z[0].reshape((-1,) + z[0].shape[-2:])
        self.x, self.y = over_x(self.blk), over_y(self.blk)
        self.sent = [self.blk]
        return [self.x, self.y]

    def stage_rest(self, *deps):
        h = self.blk.shape[0] // 2
        x, y = after((self.x, self.y), *deps)
        self.sent = [x[:h], y[h:]]
        self.rest = [over_y(self.sent[0]), over_x(self.sent[1])]
        self.far = [over_core(v) for v in (self.blk, x, y)]
        return self.rest

    def stage_core(self, *deps):
        rest = after(tuple(self.rest), *deps)
        return [self.blk, self.x, self.y] + self.rest + self.far + [over_core(v) for v in rest]


def block_sums(name, outs):
    terms = [t for ts, _, _ in outs for t in ts]
    tail = terms[0][0].shape[1:]

    def kernel(*refs):
        ins, res = refs[: len(terms)], refs[len(terms) :]
        k = 0
        for (ts, count, dtype), out in zip(outs, res):
            for i in range(count):
                acc = None
                for j, (_, blocks, _, first) in enumerate(ts):
                    if first <= i < first + blocks:
                        v = ins[k + j][i - first].astype(F32)
                        acc = v if acc is None else acc + v
                out[i] = acc.astype(dtype)
            k += len(ts)

    def spec(blocks, index):
        return pl.BlockSpec((blocks,) + tail, lambda i: (index, 0, 0))

    return pl.pallas_call(
        kernel,
        name=name,
        grid=(1,),
        in_specs=[spec(blocks, index) for _, blocks, index, _ in terms],
        out_specs=[pl.BlockSpec((count,) + tail, lambda i: (0, 0, 0)) for _, count, _ in outs],
        out_shape=[jax.ShapeDtypeStruct((count,) + tail, dt) for _, count, dt in outs],
        compiler_params=pltpu.CompilerParams(vmem_limit_bytes=VMEM_LIMIT),
        cost_estimate=pl.CostEstimate(flops=10**8, bytes_accessed=10**5, transcendentals=0),
    )(*[t[0] for t in terms])


class Reduce:
    def __init__(self, parts, n, name, shifts=False):
        self.near, self.far = parts
        self.shifts = shifts
        self.n, self.name = n, name
        self.size = self.near.shape[0] // 4

    def stage_core(self, *deps):
        self.got = over_core(after(self.far, *deps))
        return [self.got]

    def stage_rest(self, *deps):
        h = self.size // 2
        self.got = after(self.got, *deps)
        lo, hi = block_sums(
            self.name + "_rest",
            [([(v, h, k, 0) for v in (self.near, self.got)], h, B16) for k in (6, 7)],
        )
        self.sent = [lo, hi]
        self.rest = [over_y(lo), over_x(hi)]
        return self.rest

    def stage_xy(self, *deps):
        size, h = self.size, self.size // 2
        lo, hi = after(tuple(self.rest), *deps)
        both = (self.near, self.got)
        sx, sy = block_sums(
            self.name + "_xy",
            [
                ([(v, size, 1, 0) for v in both] + [(lo, h, 0, 0)], size, B16),
                ([(v, size, 2, 0) for v in both] + [(hi, h, 0, h)], size, B16),
            ],
        )
        self.sent = [sx, sy]
        self.xy = [over_x(sx), over_y(sy)]
        return self.xy

    def stage_z(self, *deps):
        rx, ry = after(tuple(self.xy), *deps)
        all_four = (self.near, self.got, rx, ry)
        if self.shifts:
            own, *self.sent = block_sums(
                self.name + "_z",
                [
                    ([(v, 1, d, 0) for v in all_four], 1, B16 if d else F32)
                    for d in range(self.n)
                ],
            )
            self.z = [own] + [
                lax.ppermute(v, "shard", [(i, (i + d) % self.n) for i in range(self.n)])
                for d, v in enumerate(self.sent, 1)
            ]
            return self.z[1:]
        self.sent = block_sums(
            self.name + "_z", [([(v, self.size, 0, 0) for v in all_four], self.size, B16)]
        )
        v = self.sent[0]
        self.z = [over_z(v.reshape((self.n, self.size // self.n) + v.shape[1:]))]
        return self.z

    def results(self, *deps):
        z = after(tuple(self.z), *deps)
        if self.shifts:
            return [functools.reduce(lambda a, b: a + b, [v[0].astype(F32) for v in z])]
        z = jnp.sum(z[0].astype(F32), axis=0)
        return [z[k] for k in range(z.shape[0])]


def joint_z(parts, n, name):
    terms, count = [], len(parts)
    for i, (r, k) in enumerate(parts):
        chunks = r.size // n
        for z in range(n):
            terms += [(v, 1, z * chunks + k, z * count + i) for v in (r.near, r.got, *r.xy)]
    (v,) = block_sums(name, [(terms, n * count, B16)])
    return v.reshape((n, count) + v.shape[1:])


EVERY = ("x", "core", "shard", "ctx")


def gather_whole(own):
    return lax.all_gather(own, EVERY, axis=0, tiled=False)


def reduce_whole(parts):
    return lax.psum_scatter(parts, EVERY, scatter_dimension=0, tiled=False).astype(F32)


class GatherWhole:
    sent = ()
    spread = ()

    def __init__(self, owns, n):
        d = owns[0].shape[1]
        self.out = [gather_whole(v).reshape(4, d, d) for v in owns]

    def stage_z(self, *deps):
        return []

    stage_xy = stage_rest = stage_z

    def stage_core(self, *deps):
        return self.out


class ReduceWhole:
    sent = ()

    def __init__(self, parts, n, name, shifts=False):
        self.parts = parts

    def stage_z(self, *deps):
        return []

    stage_core = stage_rest = stage_xy = stage_z

    def results(self, *deps):
        rows = self.parts[0].shape[1] // (2 * lax.axis_size("shard"))
        return [reduce_whole(p.reshape(-1, rows, p.shape[2]).astype(F32)) for p in self.parts]


def dot(a, b):
    return jnp.dot(a, b, preferred_element_type=F32)


def dot_nt(a, b):
    return lax.dot_general(a, b, NT_DIMS, preferred_element_type=F32)


def dot_tn(a, b):
    return lax.dot_general(a, b, TN_DIMS, preferred_element_type=F32)


def low_lanes(shape):
    return lax.broadcasted_iota(jnp.int32, shape, 1) % 128 < 64


def keep_low(v):
    return jnp.where(low_lanes(v.shape), v, jnp.zeros_like(v))


def keep_high(v):
    return jnp.where(low_lanes(v.shape), jnp.zeros_like(v), v)


def swap_halves(v):
    return jnp.concatenate([v[:, 64:], v[:, :64]], axis=1)


def norm_parts(x):
    centred = x - jnp.mean(x, axis=-1, keepdims=True)
    rstd = lax.rsqrt(jnp.mean(centred * centred, axis=-1, keepdims=True) + EPSILON)
    return centred * rstd, rstd


def norm_back(x, gain, up):
    unit, rstd = norm_parts(x)
    w = up * gain
    inner = jnp.mean(w * unit, axis=-1, keepdims=True)
    down = rstd * (w - jnp.mean(w, axis=-1, keepdims=True) - unit * inner)
    return down, jnp.sum(up * unit, axis=0, keepdims=True), jnp.sum(up, axis=0, keepdims=True)


def weight_copies(meta, bufs, w_refs, sems, n, back=False, shifts=False, first_column=0):
    moves = []
    if bufs[0].shape == w_refs[0].shape:
        moves = list(zip(bufs, w_refs))
    else:
        x, y, c = meta[0], meta[1], meta[2]
        rows = w_refs[0].shape[1] // (2 * n)
        groups = {}
        cols = slice(first_column, w_refs[0].shape[2])
        for dc in range(2):
            first = 0
            for k, (dx, dy, blocks) in enumerate(layout(len(w_refs), n)):
                tp = 2 * (x ^ dx) + (c ^ dc)
                for i, (z, chunk) in enumerate(blocks):
                    if shifts:
                        z = lax.rem(meta[3] + z, n)
                    row = pl.multiple_of((z * 2 + (y ^ dy)) * rows, rows)
                    piece = bufs[dc].at[first + i] if back else bufs[dc * 5 + k].at[i, 0:rows, cols]
                    whole = w_refs[chunk].at[tp, pl.ds(row, rows), cols]
                    groups.setdefault((dx, dc), []).append((piece, whole))
                first += len(blocks)
        moves = [m for g in sorted(groups) for m in groups[g]]
    if back:
        moves = [(whole, piece) for piece, whole in moves]
    return [pltpu.make_async_copy(*m, sems.at[i]) for i, m in enumerate(moves)]


def copy_sems(sz, chunks):
    return pltpu.SemaphoreType.DMA((8 * chunks * sz["n"],))


def start_all(copies):
    for c in copies:
        c.start()


def wait_all(copies):
    for c in copies:
        c.wait()


def take_blocks(blocks, dst, places):
    for k, blk in enumerate(blocks):
        dx, dy = k % 2, k // 2
        for f in range(2):
            row = (2 * dx + f) * 2 * PAD + dy * PAD
            dst[row + PAD - 8 : row + PAD, :] = jnp.zeros((8, dst.shape[1]), dst.dtype)
            dst[row : row + places, :] = blk[f].astype(dst.dtype)


def give_blocks(src, blocks, places):
    for k, blk in enumerate(blocks):
        dx, dy = k % 2, k // 2
        for f in range(2):
            row = (2 * dx + f) * 2 * PAD + dy * PAD
            blk[f] = src[row : row + places, :].astype(blk.dtype)


def project_heads(normed, w_ref, q_out, kv_out):
    @pl.loop(0, 2)
    def _(u):
        thirds = []
        for t in (2 * u, 2 * u + 1):
            xn = normed[...]
            y = dot(xn, w_ref[t, :, 0:512]).astype(B16)
            q_out[t] = y[:, 0:128]
            kv_out[t] = y[:, 128:256]
            kv_out[6 + t] = y[:, 256:384]
            thirds.append((y[:, 384:512], dot(xn, w_ref[t, :, 640:768]).astype(B16)))
        (a3, a5), (b3, b5) = thirds
        low = low_lanes(a3.shape)
        q_out[4 + u] = jnp.where(low, a3, b3)
        kv_out[4 + u] = swap_halves(jnp.where(low, b3, a3))
        kv_out[10 + u] = swap_halves(jnp.where(low, b5, a5))


def third_head(v, t):
    return keep_low(v) if t % 2 == 0 else keep_high(v)


def project_out(mixed, w_ref, stream, bias, out):
    for n in range(3):
        cols = slice(256 * n, 256 * n + 256)
        acc = stream[:, cols] + bias[:, cols]
        for t in range(4):
            m = jnp.concatenate([mixed[t], third_head(mixed[4 + t // 2], t)], axis=1)
            acc = acc + dot_nt(m, w_ref[t, cols, 512:768])
        out[:, cols] = acc


class Late:
    def __init__(self, source, ref, sem):
        self.ref, self.copy = ref, pltpu.make_async_copy(source, ref, sem)
        self.copy.start()

    def get(self):
        self.copy.wait()
        return self.ref


class Early:
    def __init__(self, ref, target, sem):
        self.ref, self.copy = ref, pltpu.make_async_copy(ref, target, sem)

    def send(self):
        self.copy.start()


def run(kernel, name, ins, outs, scratch, micros):
    space = {
        "v": pl.BlockSpec(memory_space=pltpu.VMEM),
        "s": pl.BlockSpec(memory_space=pltpu.SMEM),
        "a": pl.BlockSpec(memory_space=pl.ANY),
    }
    space["l"] = space["e"] = space["a"]
    late = [i for i, (_, k) in enumerate(ins) if k == "l"]
    early = [i for i, (_, _, k) in enumerate(outs) if k == "e"]
    extra = [pltpu.VMEM(ins[i][0].shape, ins[i][0].dtype) for i in late]
    extra += [pltpu.VMEM(outs[i][0], outs[i][1]) for i in early]
    if extra:
        extra.append(pltpu.SemaphoreType.DMA((len(extra),)))

    def body(*refs):
        refs = list(refs)
        held = refs[len(ins) + len(outs) + len(scratch) :]
        refs = refs[: len(ins) + len(outs) + len(scratch)]
        for j, i in enumerate(late):
            refs[i] = Late(refs[i], held[j], held[-1].at[j])
        for j, i in enumerate(early, len(late)):
            refs[len(ins) + i] = Early(held[j], refs[len(ins) + i], held[-1].at[j])
        kernel(*refs)
        for i in early:
            refs[len(ins) + i].copy.wait()

    return pl.pallas_call(
        body,
        name=name,
        in_specs=[space[s] for _, s in ins],
        out_specs=[space[s] for _, _, s in outs],
        out_shape=[jax.ShapeDtypeStruct(s, d) for s, d, _ in outs],
        scratch_shapes=list(scratch) + extra,
        compiler_params=pltpu.CompilerParams(vmem_limit_bytes=VMEM_LIMIT),
        cost_estimate=pl.CostEstimate(
            flops=micros * 10**9, bytes_accessed=micros * 3 * 10**6, transcendentals=0
        ),
    )(*[a for a, _ in ins])


def row_slices(r, step=208):
    return pl.ds(pl.multiple_of(r * step, step), step)


VECTORS = 9


def norm_vectors(sz, meta, weights):
    d, n, nw = sz["d"], sz["n"], len(weights)
    count, rows = 8 * n, d // (2 * n)
    per = d // count
    hidden = VECTORS * per

    def kernel(*refs):
        meta, bufs = refs[0], refs[1 : 1 + nw]
        out, shares, sems = refs[1 + nw :]
        x, y, c = meta[0], meta[1], meta[2]
        copies = []
        for dc in range(2):
            for k, (dx, dy, blocks) in enumerate(layout(1, n)):
                tp = 2 * (x ^ dx) + (c ^ dc)
                for i, (z, _) in enumerate(blocks):
                    dev = (z * 2 + (y ^ dy)) * 4 + tp
                    piece = bufs[dc * 5 + k].at[i, rows : rows + 8, :]
                    copies.append(
                        pltpu.make_async_copy(piece, shares.at[dev], sems.at[len(copies)])
                    )
        start_all(copies)
        lane = lax.broadcasted_iota(jnp.int32, (128, d), 1)
        row = lax.broadcasted_iota(jnp.int32, (128, d), 0)
        one = ((lane % per == row) & (row < per)).astype(F32).astype(B16)
        four = ((lane % (4 * per) == row) & (row < 4 * per)).astype(F32).astype(B16)
        dev = lax.broadcasted_iota(jnp.int32, (count, d), 0)
        lanes = lax.broadcasted_iota(jnp.int32, (count, d), 1)
        mine = lanes // per == dev
        ours = lanes // (4 * per) == dev % 8
        wait_all(copies)
        rows_in = shares[:, 0, :].astype(F32)
        pad = jnp.zeros((count, 128), F32)
        rows_in = jnp.concatenate([rows_in, pad], axis=1)

        def spread(first, pick):
            parts = [rows_in[:, o + first : o + first + 128].astype(B16) for o in (0, 384)]
            return dot(parts[0], pick) + dot(parts[1], pick)

        for v in range(VECTORS):
            got = jnp.where(mine, spread(v * per, one), 0.0)
            out[v : v + 1, :] = jnp.sum(got, axis=0, keepdims=True)
        got = jnp.where(ours, spread(hidden, four), 0.0)
        for t in range(4):
            part = got[t * 8 : t * 8 + 8] if count == 32 else got
            out[VECTORS + t : VECTORS + t + 1, :] = jnp.sum(part, axis=0, keepdims=True)

    ins = [(meta, "s")] + [(w, "a") for w in weights]
    outs = [((16, d), F32, "v")]
    scratch = [pltpu.VMEM((count, 8, d), B16), copy_sems(sz, 1)]
    return run(kernel, "norm_vectors", ins, outs, scratch, 2)[0]


def time_qkv(sz, meta, vec, blocks, weights):
    rows, d = sz["rows"], sz["d"]
    nb, nw = len(blocks), len(weights)

    def kernel(*refs):
        meta, vec = refs[0], refs[1]
        blks, bufs = refs[2 : 2 + nb], refs[2 + nb : 2 + nb + nw]
        x, normed, q, kv, w, sems = refs[2 + nb + nw :]
        copies = weight_copies(meta, bufs, [w], sems, sz["n"])
        start_all(copies)
        take_blocks(blks, x, sz["places"])

        @pl.loop(0, 4)
        def _(r):
            at = row_slices(r)
            unit, _ = norm_parts(x[at, :])
            normed[at, :] = (unit * vec[0:1, :] + vec[1:2, :]).astype(B16)

        wait_all(copies)
        project_heads(normed, w, q, kv)

    ins = [(meta, "s"), (vec, "v")] + [(b, "v") for b in blocks] + [(w, "a") for w in weights]
    outs = [
        ((rows, d), F32, "v"),
        ((rows, d), B16, "v"),
        ((6, rows, 128), B16, "v"),
        ((12, rows, 128), B16, "v"),
    ]
    scratch = [pltpu.VMEM((4, d, d), B16), copy_sems(sz, 1)]
    return run(kernel, "time_qkv", ins, outs, scratch, 12)


def head_sums(ref):
    for f in range(4):
        for j in range(6):
            col = lax.broadcasted_iota(jnp.int32, (128, 128), 1)
            lane = lax.broadcasted_iota(jnp.int32, (128, 128), 0)
            hit = col == 16 * f + 2 * j + lane // 64
            ref[(f * 6 + j) * 128 : (f * 6 + j) * 128 + 128, :] = hit.astype(F32).astype(B16)


def head_spreads(ref):
    for f in range(4):
        for j in range(6):
            row = lax.broadcasted_iota(jnp.int32, (128, 128), 0)
            lane = lax.broadcasted_iota(jnp.int32, (128, 128), 1)
            hit = row == 16 * f + 2 * j + lane // 64
            ref[:, (f * 6 + j) * 128 : (f * 6 + j) * 128 + 128] = hit.astype(F32).astype(B16)


def pair_sums(a_ref, b_ref, b_tile, g, sums):
    at = row_slices(g)
    products = [
        a_ref[j, f * 208 : f * 208 + 208, :] * b_ref[b_tile + j, at, :]
        for f in range(4)
        for j in range(6)
    ]
    return dot(jnp.concatenate(products, axis=1), sums[...])


def two_tiles(ref, tile, at):
    return jnp.concatenate([ref[tile, at, :], ref[tile + 1, at, :]], axis=1).astype(F32)


def time_mix(sz, meta, vec, stream, q, kv, kvo, weights):
    rows, d = sz["rows"], sz["d"]
    nw = len(weights)

    def kernel(*refs):
        meta, vec, stream, q, kv, kvo = refs[:6]
        bufs = refs[6 : 6 + nw]
        mixed_out, out, prob_out, w, sums, spreads, acc, sems = refs[6 + nw :]
        mixed, prob = mixed_out.ref, prob_out.ref
        copies = weight_copies(meta, bufs, [w], sems, sz["n"], first_column=512)
        start_all(copies)
        head_sums(sums)
        head_spreads(spreads)
        for h in range(2):
            if h == 1:
                kvo = kvo.get()
            ref = (kv, kvo)[h]

            @pl.loop(0, 4)
            def _(g, ref=ref, h=h):
                prob[4 * h + g] = pair_sums(q, ref, 0, g, sums) * SCALING

        @pl.loop(0, 13)
        def _(r):
            at = row_slices(r, 16)
            s = [prob[g, at, :] for g in range(8)]
            top = functools.reduce(jnp.maximum, s)
            e = [jnp.exp(v - top) for v in s]
            inv = 1.0 / functools.reduce(lambda a, b: a + b, e)
            for g in range(8):
                prob[g, at, :] = e[g] * inv

        prob_out.send()
        acc[...] = jnp.zeros_like(acc)
        for h, ref in enumerate((kv, kvo)):

            @pl.loop(0, 4)
            def _(g):
                at = row_slices(g)
                p = prob[4 * h + g].astype(B16)
                for jj in range(3):
                    v = two_tiles(ref, 6 + 2 * jj, at)
                    for f in range(4):
                        lanes = slice(f * d + 256 * jj, f * d + 256 * jj + 256)
                        acc[f * 208 : f * 208 + 208, 256 * jj : 256 * jj + 256] += (
                            dot(p, spreads[:, lanes]) * v
                        )

        for j in range(6):
            mixed[j] = acc[:, 128 * j : 128 * j + 128].astype(B16)
        mixed_out.send()
        wait_all(copies)
        project_out(mixed, w, stream.get(), vec[2:3, :], out)

    ins = [(meta, "s"), (vec, "v"), (stream, "l"), (q, "v"), (kv, "v"), (kvo, "l")]
    ins += [(w, "a") for w in weights]
    outs = [((6, rows, 128), B16, "e"), ((rows, d), F32, "v"), ((8, 208, 128), F32, "e")]
    scratch = [
        pltpu.VMEM((4, d, d), B16),
        pltpu.VMEM((4 * d, 128), B16),
        pltpu.VMEM((128, 4 * d), B16),
        pltpu.VMEM((rows, d), F32),
        copy_sems(sz, 1),
    ]
    return run(kernel, "time_mix", ins, outs, scratch, 17)


def space_mask(places):
    return lax.broadcasted_iota(jnp.int32, (208, 208), 0) % PAD < places


def space_qkv(sz, meta, vec, stream, weights):
    rows, d = sz["rows"], sz["d"]
    nw = len(weights)

    def kernel(*refs):
        meta, vec, stream = refs[:3]
        bufs = refs[3 : 3 + nw]
        normed, q, kv, w, sems = refs[3 + nw :]
        copies = weight_copies(meta, bufs, [w], sems, sz["n"])
        start_all(copies)

        @pl.loop(0, 4)
        def _(r):
            at = row_slices(r)
            unit, _ = norm_parts(stream[at, :])
            normed[at, :] = (unit * vec[3:4, :] + vec[4:5, :]).astype(B16)

        wait_all(copies)
        project_heads(normed, w, q, kv)

    ins = [(meta, "s"), (vec, "v"), (stream, "v")] + [(w, "a") for w in weights]
    outs = [((rows, d), B16, "v"), ((6, rows, 128), B16, "v"), ((12, rows, 128), B16, "v")]
    scratch = [pltpu.VMEM((4, d, d), B16), copy_sems(sz, 1)]
    return run(kernel, "space_qkv", ins, outs, scratch, 12)


def space_mix(sz, meta, vec, stream, q, kv, weights):
    rows, d, places = sz["rows"], sz["d"], sz["places"]
    nw = len(weights)

    def kernel(*refs):
        meta, vec, stream, q, kv = refs[:5]
        bufs = refs[5 : 5 + nw]
        mixed_out, logs, out, w, sems = refs[5 + nw :]
        mixed = mixed_out.ref
        copies = weight_copies(meta, bufs, [w], sems, sz["n"], first_column=512)
        start_all(copies)

        def mix(j, f):
            at = row_slices(f)
            qj, kj, vj = q[j, at, :], kv[j, at, :], kv[6 + j, at, :]
            mask = space_mask(places)
            o = None
            for h, keep in enumerate((keep_low, keep_high)):
                s = jnp.where(mask, dot_nt(kj, keep(qj)) * SCALING, NEGATIVE)
                top = jnp.max(s, axis=0, keepdims=True)
                e = jnp.exp(s - top)
                size = jnp.sum(e, axis=0, keepdims=True)
                logs[j * 4 + f, h : h + 1, :] = top + jnp.log(size)
                part = dot_tn((e * (1.0 / size)).astype(B16), keep(vj))
                o = part if o is None else o + part
            return o.astype(B16)

        @pl.loop(0, 6)
        def _(j):
            frames = [mix(j, f) for f in range(4)]
            for f in range(4):
                mixed[j, row_slices(f), :] = frames[f]

        mixed_out.send()
        wait_all(copies)
        project_out(mixed, w, stream.get(), vec[5:6, :], out)

    ins = [(meta, "s"), (vec, "v"), (stream, "l"), (q, "v"), (kv, "v")]
    ins += [(w, "a") for w in weights]
    outs = [((6, rows, 128), B16, "e"), ((24, 8, 208), F32, "v"), ((rows, d), F32, "v")]
    scratch = [pltpu.VMEM((4, d, d), B16), copy_sems(sz, 1)]
    return run(kernel, "space_mix", ins, outs, scratch, 17)


def gradient_outs(sz, chunks, fast):
    d, n = sz["d"], sz["n"]
    if not fast:
        return [((4, d, d), B16, "a")] * chunks
    return [((4 * chunks * n, d // (2 * n), d), B16, "a")] * 2


def gelu_pair(x):
    half = 0.5 * (1.0 + lax.erf(x * 0.7071067811865476))
    slope = half + x * (0.3989422804014327 * jnp.exp(-0.5 * x * x))
    return x * half, slope


def feed_forward(sz, meta, vec, stream, blocks, weights, fast):
    rows, d, places = sz["rows"], sz["d"], sz["places"]
    nb, nw = len(blocks), len(weights)
    g_outs = gradient_outs(sz, 2, fast)
    ng = len(g_outs)

    def kernel(*refs):
        meta, vec, stream = refs[:3]
        blks = refs[3 : 3 + nb]
        refs = refs[3 + nb :]
        bufs, refs = refs[:nw], refs[nw:]
        res, refs = refs[:nb], refs[nb:]
        d2, vgrad = refs[0], refs[1]
        g_bufs, refs = refs[2 : 2 + ng], refs[2 + ng :]
        w1, w2, dw1, dw2, dz, dzr, normed, act, dpre, y, dn, sems, back_sems = refs
        copies = weight_copies(meta, bufs, [w1, w2], sems, sz["n"])
        start_all(copies)
        take_blocks(blks, dz, places)
        vgrad[...] = jnp.zeros_like(vgrad)

        @pl.loop(0, 4)
        def _(r):
            at = pl.ds(pl.multiple_of(r * 208, 208), 208)
            unit, _ = norm_parts(stream[at, :])
            normed[at, :] = (unit * vec[6:7, :] + vec[7:8, :]).astype(B16)
            up = dz[at, :]
            dzr[at, :] = up.astype(B16)
            vgrad[2:3, :] += jnp.sum(up, axis=0, keepdims=True)
            y[at, :] = stream[at, :] + vec[8:9, :]
            dn[at, :] = jnp.zeros_like(up)

        back = weight_copies(meta, g_bufs, [dw1, dw2], back_sems, sz["n"], back=True)
        group = len(copies) // 4
        if not fast:
            wait_all(copies)

        @pl.loop(0, 4)
        def _(k):
            t = k
            if fast:
                t = 2 * (meta[0] ^ (k // 2)) + (meta[2] ^ (k % 2))
                rows_here = w1.shape[1] // (2 * sz["n"])
                piece = (bufs[0].at[0, 0:rows_here, :], w1.at[0, 0:rows_here, :])
                for i in range(group):
                    pltpu.make_async_copy(*piece, sems.at[k * group + i]).wait()
            thirds = [slice(256 * i, 256 * i + 256) for i in range(3)]
            for cols in thirds:
                pre = dot(normed[...], w1[t, :, cols]) + vec[pl.ds(9 + t, 1), cols]
                a, slope = gelu_pair(pre)
                act[:, cols] = a.astype(B16)
                g = (dot(dzr[...], w2[t, :, cols]) * slope).astype(B16)
                dpre[:, cols] = g
                vgrad[pl.ds(4 + t, 1), cols] += jnp.sum(g.astype(F32), axis=0, keepdims=True)
            for cols in thirds:
                y[:, cols] += dot_nt(act[...], w2[t, cols, :])
                dn[:, cols] += dot_nt(dpre[...], w1[t, cols, :])
            for cols in thirds:
                dw1[t, :, cols] = dot_tn(normed[...], dpre[:, cols]).astype(B16)
                dw2[t, :, cols] = dot_tn(dzr[...], act[:, cols]).astype(B16)
            if fast:
                for i in range(4):
                    pl.when(k == i)(lambda i=i: start_all(back[i * group : i * group + group]))

        if not fast:
            start_all(back)
        give_blocks(y, res, places)

        @pl.loop(0, 4)
        def _(r):
            at = pl.ds(pl.multiple_of(r * 208, 208), 208)
            down, gg, gs = norm_back(stream[at, :], vec[6:7, :], dn[at, :])
            d2[at, :] = dz[at, :] + down
            vgrad[0:1, :] += gg
            vgrad[1:2, :] += gs

        wait_all(back)

    ins = [(meta, "s"), (vec, "v"), (stream, "v")] + [(b, "v") for b in blocks]
    ins += [(w, "a") for w in weights]
    outs = [((2, places, d), B16, "v")] * nb + [((rows, d), F32, "v"), ((8, d), F32, "v")]
    outs += g_outs
    scratch = [pltpu.VMEM((4, d, d), B16)] * 4
    scratch += [pltpu.VMEM((rows, d), F32), pltpu.VMEM((rows, d), B16), pltpu.VMEM((rows, d), B16)]
    scratch += [pltpu.VMEM((rows, d), B16)] * 2 + [pltpu.VMEM((rows, d), F32)] * 2
    scratch += [copy_sems(sz, 2)] * 2
    r = run(kernel, "feed_forward", ins, outs, scratch, 47)
    return r[:nb], r[nb], r[nb + 1], r[nb + 2 :]


def mixed_slopes(up, w_ref, dm):
    for u in range(2):
        thirds = []
        for t in (2 * u, 2 * u + 1):
            v = dot(up[...], w_ref[t, :, 512:768]).astype(B16)
            dm[t] = v[:, 0:128]
            thirds.append(v[:, 128:256])
        dm[4 + u] = jnp.where(low_lanes(thirds[0].shape), *thirds)


def place_third(dq, dk, dv, dy, u, at):
    k, v = swap_halves(dk), swap_halves(dv)
    low = low_lanes(dq.shape)
    dy[2 * u, at, 384:512] = jnp.where(low, dq, k)
    dy[2 * u + 1, at, 384:512] = jnp.where(low, k, dq)
    dy[2 * u, at, 512:640] = keep_high(v)
    dy[2 * u + 1, at, 512:640] = keep_low(v)


def third_head_of(v, odd):
    return jnp.where(low_lanes(v.shape) == (odd == 0), v, jnp.zeros_like(v))


def output_gradients(dw, up, mixed):
    @pl.loop(0, 4)
    def _(t):
        third = third_head_of(mixed[4 + t // 2], t % 2)
        out = dot_tn(up[...], jnp.concatenate([mixed[t], third], axis=1))
        dw[t, :, 512:768] = out.astype(B16)


def head_gradients(t, dw, normed, dy):
    dw[t, :, 0:512] = dot_tn(normed[...], dy[t, :, 0:512]).astype(B16)
    third = dot_tn(normed[...], dy[t, :, 512:640])
    dw[t, :, 640:768] = (dw[t, :, 640:768].astype(F32) + third).astype(B16)


def norm_slopes(t, dy, w_ref, out):
    for n in range(3):
        cols = slice(256 * n, 256 * n + 256)
        part = dot_nt(dy[t, :, 0:512], w_ref[t, cols, 0:512])
        out[:, cols] += part + dot_nt(dy[t, :, 512:640], w_ref[t, cols, 640:768])


def space_backward_scores(sz, meta, d2, q, kv, logs, weights):
    rows, d, places = sz["rows"], sz["d"], sz["places"]
    nw = len(weights)

    def kernel(*refs):
        meta, d2, q, kv, logs = refs[:5]
        bufs, refs = refs[5 : 5 + nw], refs[5 + nw :]
        up_out, dy, w, dm, third, sems = refs
        up = up_out.ref
        copies = weight_copies(meta, bufs, [w], sems, sz["n"], first_column=512)
        start_all(copies)

        @pl.loop(0, 4)
        def _(r):
            up[row_slices(r), :] = d2[row_slices(r), :].astype(B16)

        wait_all(copies)
        up_out.send()
        mixed_slopes(up, w, dm)
        q, kv, logs = q.get(), kv.get(), logs.get()

        def slopes(j, at, f):
            qj, kj, vj, mj = q[j, at, :], kv[j, at, :], kv[6 + j, at, :], dm[j, at, :]
            mask = space_mask(places)
            dq = dk = dv = None
            for h, keep in enumerate((keep_low, keep_high)):
                qh, mh = keep(qj), keep(mj)
                s = dot_nt(kj, qh) * SCALING - logs[j * 4 + f, h : h + 1, :]
                p = jnp.exp(jnp.where(mask, s, NEGATIVE))
                dp = dot_nt(vj, mh)
                inner = jnp.sum(p * dp, axis=0, keepdims=True)
                ds = (p * (dp - inner) * SCALING).astype(B16)
                a, b, c = dot_tn(ds, keep(kj)), dot(ds, qh), dot(p.astype(B16), mh)
                dq, dk, dv = (a, b, c) if dq is None else (dq + a, dk + b, dv + c)
            return dq.astype(B16), dk.astype(B16), dv.astype(B16)

        @pl.loop(0, 4)
        def _(j):
            ats = [row_slices(f) for f in range(4)]
            frames = [slopes(j, ats[f], f) for f in range(4)]
            for at, (dq, dk, dv) in zip(ats, frames):
                dy[j, at, 0:128] = dq
                dy[j, at, 128:256] = dk
                dy[j, at, 256:384] = dv

        @pl.loop(0, 2)
        def _(u):
            ats = [row_slices(f) for f in range(4)]
            frames = [slopes(4 + u, ats[f], f) for f in range(4)]
            for at, v in zip(ats, frames):
                place_third(*v, dy, u, at)

    ins = [(meta, "s")] + [(d2, "v")] + [(v, "l") for v in (q, kv, logs)] + [(w, "a") for w in weights]
    outs = [((rows, d), B16, "e"), ((4, rows, 640), B16, "v")]
    scratch = [pltpu.VMEM((4, d, d), B16), pltpu.VMEM((6, rows, 128), B16)]
    scratch += [pltpu.VMEM((rows, 128), B16), copy_sems(sz, 1)]
    return run(kernel, "space_backward_scores", ins, outs, scratch, 30)


def weight_slopes(sz, name, meta, up, normed, mixed, slopes, fast):
    rows, d = sz["rows"], sz["d"]
    g_outs = gradient_outs(sz, 1, fast)
    join = len(slopes) == 3

    def kernel(*refs):
        meta, up, normed, mixed = refs[:4]
        given, refs = refs[4 : 4 + len(slopes)], refs[4 + len(slopes) :]
        dy = refs[0].ref if join else given[0]
        g_bufs, (dw, sems) = refs[1 if join else 0 : -2], refs[-2:]
        if join:
            dq, dkv, got = given

            def both(j, at):
                return (dkv[j, at, :].astype(F32) + got[j, at, :].astype(F32)).astype(B16)

            @pl.loop(0, 4)
            def _(r):
                at = row_slices(r)
                for j in range(4):
                    dy[j, at, 0:128] = dq[j, at, :]
                    dy[j, at, 128:256] = both(j, at)
                    dy[j, at, 256:384] = both(6 + j, at)
                for u in range(2):
                    place_third(dq[4 + u, at, :], both(4 + u, at), both(10 + u, at), dy, u, at)

            refs[0].send()
        back = weight_copies(meta, g_bufs, [dw], sems, sz["n"], back=True, shifts=join)
        group = len(back) // 4
        output_gradients(dw, up.get(), mixed.get())
        normed = normed.get()
        if not join:
            dy = dy.get()

        @pl.loop(0, 4)
        def _(k):
            t = 2 * (meta[0] ^ (k // 2)) + (meta[2] ^ (k % 2)) if fast else k
            head_gradients(t, dw, normed, dy)
            if fast:
                for i in range(4):
                    pl.when(k == i)(lambda i=i: start_all(back[i * group : i * group + group]))

        if not fast:
            start_all(back)
        wait_all(back)

    ins = [(meta, "s")] + [(v, "l") for v in (up, normed, mixed)]
    ins += [(v, "v" if join else "l") for v in slopes]
    outs = ([((4, rows, 640), B16, "e")] if join else []) + g_outs
    scratch = [pltpu.VMEM((4, d, d), B16), copy_sems(sz, 1)]
    return run(kernel, name, ins, outs, scratch, 14)


def input_slopes(sz, name, meta, vec, up, stream, dy, weights, gain_row, blocks):
    rows, d, places = sz["rows"], sz["d"], sz["places"]
    nw = len(weights)

    def kernel(*refs):
        meta, vec, up, stream, dy = refs[:5]
        bufs, refs = refs[5 : 5 + nw], refs[5 + nw :]
        w, dn, sems = refs[-3:]
        if blocks:
            outs, vgrad, dx = refs[:4], refs[4], refs[5]
        else:
            dx, vgrad = refs[:2]
        copies = weight_copies(meta, bufs, [w], sems, sz["n"])
        start_all(copies)
        vgrad[...] = jnp.zeros_like(vgrad)
        dn[...] = jnp.zeros_like(dn)
        fast = nw > 1
        group = len(copies) // 4
        if not fast:
            wait_all(copies)

        @pl.loop(0, 4)
        def _(k):
            t = k
            if fast:
                t = 2 * (meta[0] ^ (k // 2)) + (meta[2] ^ (k % 2))
                rows_here = w.shape[1] // (2 * sz["n"])
                piece = (bufs[0].at[0, 0:rows_here, :], w.at[0, 0:rows_here, :])
                for i in range(group):
                    pltpu.make_async_copy(*piece, sems.at[k * group + i]).wait()
            norm_slopes(t, dy, w, dn)

        up, stream = up.get(), stream.get()

        @pl.loop(0, 4)
        def _(r):
            at = row_slices(r)
            v = up[at, :]
            gain = vec[gain_row : gain_row + 1, :]
            down, gg, gs = norm_back(stream[at, :], gain, dn[at, :])
            dx[at, :] = v + down
            vgrad[0:1, :] += gg
            vgrad[1:2, :] += gs
            vgrad[2:3, :] += jnp.sum(v, axis=0, keepdims=True)

        if blocks:
            give_blocks(dx, outs, places)

    ins = [(meta, "s"), (vec, "v"), (up, "l"), (stream, "l"), (dy, "v")]
    ins += [(w, "a") for w in weights]
    outs = [((rows, d), F32, "v")]
    scratch = []
    if blocks:
        outs = [((2, places, d), F32, "v")] + [((2, places, d), B16, "v")] * 3
        scratch = [pltpu.VMEM((rows, d), F32)]
    outs += [((8, d), F32, "v")]
    scratch += [pltpu.VMEM((4, d, d), B16), pltpu.VMEM((rows, d), F32), copy_sems(sz, 1)]
    return run(kernel, name, ins, outs, scratch, 14)


def time_backward_scores(sz, meta, d1, q, kv, kvo, prob, weights):
    rows, d = sz["rows"], sz["d"]
    nw = len(weights)

    def kernel(*refs):
        meta, d1, q, kv, kvo, prob = refs[:6]
        bufs, refs = refs[6 : 6 + nw], refs[6 + nw :]
        up_out, dq, dkv_out, dkvo, w, dm, sums, spreads, ds, acc, sems = refs
        up, dkv = up_out.ref, dkv_out.ref
        copies = weight_copies(meta, bufs, [w], sems, sz["n"], first_column=512)
        start_all(copies)
        head_sums(sums)
        head_spreads(spreads)

        @pl.loop(0, 4)
        def _(r):
            up[row_slices(r), :] = d1[row_slices(r), :].astype(B16)

        wait_all(copies)
        up_out.send()
        mixed_slopes(up, w, dm)
        q, kv, kvo, prob = q.get(), kv.get(), kvo.get(), prob.get()
        for h, ref in enumerate((kv, kvo)):

            @pl.loop(0, 4)
            def _(g):
                ds[4 * h + g] = pair_sums(dm, ref, 6, g, sums)

        @pl.loop(0, 13)
        def _(r):
            at = row_slices(r, 16)
            p = [prob[g, at, :] for g in range(8)]
            dp = [ds[g, at, :] for g in range(8)]
            inner = functools.reduce(lambda a, b: a + b, [a * b for a, b in zip(p, dp)])
            for g in range(8):
                ds[g, at, :] = p[g] * (dp[g] - inner) * SCALING

        acc[...] = jnp.zeros_like(acc)
        for h, (ref, out) in enumerate(((kv, dkv), (kvo, dkvo))):

            @pl.loop(0, 4)
            def _(g):
                at = row_slices(g)
                both = jnp.concatenate([ds[4 * h + g], prob[4 * h + g]], axis=0).astype(B16)
                for jj in range(3):
                    k = two_tiles(ref, 2 * jj, at)
                    dk = dv = None
                    for f in range(4):
                        fr = slice(f * 208, f * 208 + 208)
                        e = dot(both, spreads[:, f * d + 256 * jj : f * d + 256 * jj + 256])
                        se, pe = e[:208], e[208:]
                        acc[fr, 256 * jj : 256 * jj + 256] += se * k
                        a = se * two_tiles(q, 2 * jj, fr)
                        b = pe * two_tiles(dm, 2 * jj, fr)
                        dk, dv = (a, b) if dk is None else (dk + a, dv + b)
                    dk, dv = dk.astype(B16), dv.astype(B16)
                    for i in range(2):
                        out[2 * jj + i, at, :] = dk[:, 128 * i : 128 * i + 128]
                        out[6 + 2 * jj + i, at, :] = dv[:, 128 * i : 128 * i + 128]

            if h == 0:
                dkv_out.send()

        for j in range(6):
            dq[j] = acc[:, 128 * j : 128 * j + 128].astype(B16)

    ins = [(meta, "s")] + [(d1, "v")] + [(v, "l") for v in (q, kv, kvo, prob)] + [(w, "a") for w in weights]
    outs = [
        ((rows, d), B16, "e"),
        ((6, rows, 128), B16, "v"),
        ((12, rows, 128), B16, "e"),
        ((12, rows, 128), B16, "v"),
    ]
    scratch = [
        pltpu.VMEM((4, d, d), B16),
        pltpu.VMEM((6, rows, 128), B16),
        pltpu.VMEM((4 * d, 128), B16),
        pltpu.VMEM((128, 4 * d), B16),
        pltpu.VMEM((8, 208, 128), F32),
        pltpu.VMEM((rows, d), F32),
        copy_sems(sz, 1),
    ]
    return run(kernel, "time_backward_scores", ins, outs, scratch, 23)


def pack_heads(qkv, proj, odd):
    q, k, v = qkv[:, 0], qkv[:, 1], qkv[:, 2]
    o = proj.T
    first = [q[:, :128], k[:, :128], v[:, :128]]
    even = first + [q[:, 128:], k[:, 128:], o[:, :128], o[:, 128:], v[:, 128:]]
    other = first + [k[:, 128:], q[:, 128:], o[:, :128], v[:, 128:], o[:, 128:]]
    return jnp.where(odd, jnp.concatenate(other, axis=1), jnp.concatenate(even, axis=1))


def unpack_heads(g, odd):
    def pick(a, b):
        return jnp.where(odd, g[:, b : b + 64], g[:, a : a + 64])

    q = jnp.concatenate([g[:, 0:128], pick(384, 448)], axis=1)
    k = jnp.concatenate([g[:, 128:256], pick(448, 384)], axis=1)
    v = jnp.concatenate([g[:, 256:384], pick(704, 640)], axis=1)
    o = jnp.concatenate([g[:, 512:640], pick(640, 704)], axis=1)
    return jnp.stack([q, k, v], axis=1), o.T


def local(mesh_shape, video, cotangent, *params):
    qkv_time, proj_time, qkv_space, proj_space, fc_in, fc_out = params[:6]
    vectors = params[6:]
    n = mesh_shape["shard"]
    d = proj_time.shape[0] * 4
    places = video.shape[2]
    rows_here = fc_in.shape[0]
    fast = rows_here % 16 == 0
    sz = {"n": n, "d": d, "places": places, "rows": 8 * PAD}
    x, y = lax.axis_index("x"), lax.axis_index("ctx")
    c, z = lax.axis_index("core"), lax.axis_index("shard")
    meta = jnp.stack([x, y, c, z]).astype(jnp.int32)
    every = ("shard", "ctx", "x", "core")
    count = 8 * n

    gather, reduce = (Gather, Reduce) if fast else (GatherWhole, ReduceWhole)
    per = d // count
    order = [0, 1, 2, 3, 4, 5, 6, 7, 9, 8]
    share = jnp.concatenate([vectors[i] for i in order])
    first_rows = pack_heads(qkv_time, proj_time, c == 1)
    if fast:
        kept = lax.reduce_precision(share, exponent_bits=8, mantissa_bits=7)
        high, low = kept.astype(B16), (share - kept).astype(B16)
        gap = jnp.zeros((384 - share.shape[0],), B16)
        row = jnp.concatenate([high, gap, low, gap])[None]
        first_rows = jnp.concatenate([first_rows, row, jnp.zeros((7, d), B16)], axis=0)

    def clips_of(v):
        return [
            lax.dynamic_index_in_dim(v, 2 * (x ^ dx) + (y ^ dy), 0, keepdims=False)
            for dx, dy in ((0, 0), (1, 0), (0, 1), (1, 1))
        ]

    def frames_back(blocks):
        return [blocks[0], over_x(blocks[1]), over_y(blocks[2]), over_xy(blocks[3])]

    def join_clips(blocks, dtype):
        out = jnp.zeros((4,) + blocks[0].shape, dtype)
        for k, b in enumerate(blocks):
            at = 2 * (x ^ (k % 2)) + (y ^ (k // 2))
            out = lax.dynamic_update_slice_in_dim(out, b.astype(dtype)[None], at, 0)
        return out

    g_t = gather([first_rows], n)
    g_s = gather([pack_heads(qkv_space, proj_space, c == 1)], n)
    g_m = gather([fc_in, fc_out.T], n)
    t_z = g_t.stage_z()
    cot_clips, video_clips = [clips_of(v) for v in after((cotangent, video), g_t.spread)]
    cot_blocks, video_blocks = frames_back(cot_clips), frames_back(video_clips)
    t_xy = g_t.stage_xy(*cot_blocks[1:], *video_blocks[1:3])
    s_z = g_s.stage_z(*t_z)
    t_rest = g_t.stage_rest()
    m_z = g_m.stage_z(*s_z)
    s_xy = g_s.stage_xy(*t_rest)
    w_time = g_t.stage_core()
    if fast:
        vec = norm_vectors(sz, meta, w_time)
    else:
        shares = lax.all_gather(share, every, axis=0, tiled=False)
        vec = shares[:, : VECTORS * per].reshape(count, VECTORS, per).transpose(1, 0, 2)
        hidden = shares[:, VECTORS * per :].reshape(4, d)
        vec = jnp.concatenate([vec.reshape(VECTORS, d), hidden, jnp.zeros((3, d), F32)], axis=0)
    vec_t = after(vec, *g_s.sent, g_m.spread)
    stream0, normed_t, q_t, kv_t = time_qkv(sz, meta, vec_t, video_blocks, w_time)

    kv_o = over_core(after(kv_t, *s_xy, *m_z))
    s_rest = g_s.stage_rest(kv_t)
    m_xy = g_m.stage_xy(kv_t)
    kv_o = after(kv_o, *s_rest, *g_m.sent)
    mixed_t, stream1, prob_t = time_mix(sz, meta, vec, stream0, q_t, kv_t, kv_o, w_time)

    w_space = g_s.stage_core()
    normed_s, q_s, kv_s = space_qkv(sz, meta, vec, stream1, w_space)
    m_rest = g_m.stage_rest(kv_s)
    kv_sb = after(kv_s, *g_m.sent)
    mixed_s, logs, stream2 = space_mix(sz, meta, vec, stream1, q_s, kv_sb, w_space)

    w_mlp = g_m.stage_core(stream2)
    res, d2, vg_m, parts_m = feed_forward(sz, meta, vec, stream2, cot_blocks, w_mlp, fast)

    r_m = reduce(parts_m, n, "mlp")
    m_core = r_m.stage_core()
    result_back = frames_back(res)
    up_s, dy_s = space_backward_scores(sz, meta, d2, q_s, kv_s, logs, w_space)

    m_rest = r_m.stage_rest(up_s)
    dy_s = after(dy_s, *result_back, *r_m.sent)
    parts_s = weight_slopes(sz, "space_weights", meta, up_s, normed_s, mixed_s, [dy_s], fast)
    r_s = reduce(parts_s, n, "space")
    s_core = r_s.stage_core(*m_rest)
    m_xy = r_m.stage_xy(*parts_s)
    d2b = after(d2, *parts_s, *r_m.sent)
    d1, vg_s = input_slopes(sz, "space_input", meta, vec, d2b, stream1, dy_s, w_space, 3, False)
    s_rest = r_s.stage_rest(d1)
    d1b = after(d1, *r_s.sent)
    up_t, dq, dkv, dkvo = time_backward_scores(sz, meta, d1b, q_t, kv_t, kv_o, prob_t, w_time)

    dkv_got = over_core(after(dkvo, *m_xy, *s_rest))
    first_z = ()
    if fast:
        r_m.xy = after(tuple(m_xy), dkvo)
        first_sent = joint_z([(r_m, 0)], n, "mlp_z")
        first_z = (over_z(first_sent),)
    s_xy = r_s.stage_xy(dkvo)
    dkv_got = after(dkv_got, *r_s.sent, first_sent) if fast else dkv_got
    dy_t, *parts_t = weight_slopes(
        sz, "time_weights", meta, up_t, normed_t, mixed_t, [dq, dkv, dkv_got], fast
    )

    r_t = reduce(parts_t, n, "time", True)
    t_core = r_t.stage_core(*s_xy, *first_z)
    t_rest = r_t.stage_rest()
    if fast:
        r_s.xy = after(tuple(s_xy), *r_t.sent)
        sent = joint_z([(r_s, 0), (r_m, 1)], n, "joint_z")
        got = over_z(sent)
    else:
        sent = ()
    t_xy = r_t.stage_xy(sent)
    d1c = after(d1, *r_t.sent)
    *dx, vg_t = input_slopes(sz, "time_input", meta, vec, d1c, stream0, dy_t, w_time, 0, True)

    t_z = r_t.stage_z(vg_t)
    vg_t2, result_back, dx = after((vg_t, tuple(result_back), tuple(dx)), *r_t.sent)
    video_back = frames_back(dx)
    if fast:
        vg_t2 = after(vg_t2, got)

    rows = jnp.concatenate([vg_t2[0:3], vg_s[0:3], vg_m[0:2]], axis=0)
    parts = jnp.concatenate(
        [
            rows.reshape(8, count, per).transpose(1, 0, 2).reshape(count, 8 * per),
            vg_m[4:8].reshape(count, 4 * per),
            vg_m[2].reshape(count, per),
        ],
        axis=1,
    )
    got_parts = lax.all_to_all(parts, every, split_axis=0, concat_axis=0, tiled=True)
    result = join_clips(result_back, B16)
    if fast:
        vec_got, video_back, r_t.z, joint, first = lax.optimization_barrier(
            (got_parts, tuple(video_back), tuple(r_t.z), got, first_z[0])
        )
        joint = jnp.sum(joint.astype(F32), axis=0)
        grad_s, grad_out = joint[0], joint[1]
        grad_in = jnp.sum(first.astype(F32), axis=0)[0]
    else:
        vec_got = got_parts
        grad_in, grad_out = r_m.results()
        (grad_s,) = r_s.results()
    (grad_t,) = r_t.results()
    grad_video = join_clips(video_back, F32)
    sums = jnp.sum(vec_got, axis=0)
    starts = [per * i for i in range(9)] + [per * 12]
    cuts = [sums[starts[i] : starts[i] + (4 * per if i == 8 else per)] for i in range(10)]

    qkv_t_grad, proj_t_grad = unpack_heads(grad_t, c == 1)
    qkv_s_grad, proj_s_grad = unpack_heads(grad_s, c == 1)
    return (
        result,
        grad_video,
        qkv_t_grad,
        proj_t_grad,
        qkv_s_grad,
        proj_s_grad,
        grad_in,
        grad_out.T,
        *cuts,
    )


def solution(mesh):
    shape = dict(mesh.shape)
    fine = Mesh(
        mesh.devices.reshape(shape["shard"], shape["ctx"], 2, shape["tp"] // 2),
        ("shard", "ctx", "x", "core"),
    )
    tp = ("x", "core")
    sc = ("shard", "ctx")
    tokens = P("shard", tp, "ctx", None)
    weights = (P(sc, None, tp), P(tp, sc), P(sc, None, tp), P(tp, sc), P(sc, tp), P(tp, sc))
    vectors = (P(("shard", "ctx", "x", "core")),) * 10
    return jax.shard_map(
        functools.partial(local, shape),
        mesh=fine,
        in_specs=(tokens, tokens) + weights + vectors,
        out_specs=(tokens, tokens) + weights + vectors,
        check_vma=False,
    )
```

```python
import functools

import jax
import jax.numpy as jnp
from jax import lax
from jax.experimental import pallas as pl
from jax.experimental.pallas import tpu as pltpu
from jax.sharding import Mesh
from jax.sharding import PartitionSpec as P

F32 = jnp.float32
B16 = jnp.bfloat16
HEAD_DIM = 64
SCALING = HEAD_DIM ** (-0.5)
EPSILON = 1e-06
NEGATIVE = -1e30
PAD = 104
NT_DIMS = (((1,), (1,)), ((), ()))
TN_DIMS = (((0,), (0,)), ((), ()))
FLIP = [(0, 1), (1, 0)]
VMEM_LIMIT = 64 * 1024 * 1024 - 65536


def over_x(v):
    return lax.ppermute(v, "x", FLIP)


def over_y(v):
    return lax.ppermute(v, "ctx", FLIP)


def over_xy(v):
    return lax.ppermute(v, ("ctx", "x"), [(i, 3 - i) for i in range(4)])


def over_core(v):
    return lax.ppermute(v, "core", FLIP)


def over_z(v):
    return lax.all_to_all(v, "shard", split_axis=0, concat_axis=0, tiled=True)


def after(values, *results):
    return lax.optimization_barrier((values, results))[0]


def layout(chunks, n):
    full = [(z, k) for z in range(n) for k in range(chunks)]
    h = len(full) // 2
    return [(0, 0, full), (1, 0, full), (0, 1, full), (1, 1, full[:h]), (1, 1, full[h:])]


class Gather:
    def __init__(self, owns, n):
        own = jnp.stack(owns)
        self.n = n
        self.spread = lax.optimization_barrier(jnp.broadcast_to(own[None], (n,) + own.shape))

    def stage_z(self, *deps):
        self.z = [over_z(after(self.spread, *deps))]
        return self.z

    def stage_xy(self, *deps):
        z = after(tuple(self.z), *deps)
        self.blk = z[0].reshape((-1,) + z[0].shape[-2:])
        self.x, self.y = over_x(self.blk), over_y(self.blk)
        self.sent = [self.blk]
        return [self.x, self.y]

    def stage_rest(self, *deps):
        h = self.blk.shape[0] // 2
        x, y = after((self.x, self.y), *deps)
        self.sent = [x[:h], y[h:]]
        self.rest = [over_y(self.sent[0]), over_x(self.sent[1])]
        self.far = [over_core(v) for v in (self.blk, x, y)]
        return self.rest

    def stage_core(self, *deps):
        rest = after(tuple(self.rest), *deps)
        return [self.blk, self.x, self.y] + self.rest + self.far + [over_core(v) for v in rest]


def block_sums(name, outs):
    terms = [t for ts, _, _ in outs for t in ts]
    tail = terms[0][0].shape[1:]

    def kernel(*refs):
        ins, res = refs[: len(terms)], refs[len(terms) :]
        k = 0
        for (ts, count, dtype), out in zip(outs, res):
            for i in range(count):
                acc = None
                for j, (_, blocks, _, first) in enumerate(ts):
                    if first <= i < first + blocks:
                        v = ins[k + j][i - first].astype(F32)
                        acc = v if acc is None else acc + v
                out[i] = acc.astype(dtype)
            k += len(ts)

    def spec(blocks, index):
        return pl.BlockSpec((blocks,) + tail, lambda i: (index, 0, 0))

    return pl.pallas_call(
        kernel,
        name=name,
        grid=(1,),
        in_specs=[spec(blocks, index) for _, blocks, index, _ in terms],
        out_specs=[pl.BlockSpec((count,) + tail, lambda i: (0, 0, 0)) for _, count, _ in outs],
        out_shape=[jax.ShapeDtypeStruct((count,) + tail, dt) for _, count, dt in outs],
        compiler_params=pltpu.CompilerParams(vmem_limit_bytes=VMEM_LIMIT),
        cost_estimate=pl.CostEstimate(flops=10**8, bytes_accessed=10**5, transcendentals=0),
    )(*[t[0] for t in terms])


class Reduce:
    def __init__(self, parts, n, name, shifts=False):
        self.near, self.far = parts
        self.shifts = shifts
        self.n, self.name = n, name
        self.size = self.near.shape[0] // 4

    def stage_core(self, *deps):
        self.got = over_core(after(self.far, *deps))
        return [self.got]

    def stage_rest(self, *deps):
        h = self.size // 2
        self.got = after(self.got, *deps)
        lo, hi = block_sums(
            self.name + "_rest",
            [([(v, h, k, 0) for v in (self.near, self.got)], h, B16) for k in (6, 7)],
        )
        self.sent = [lo, hi]
        self.rest = [over_y(lo), over_x(hi)]
        return self.rest

    def stage_xy(self, *deps):
        size, h = self.size, self.size // 2
        lo, hi = after(tuple(self.rest), *deps)
        both = (self.near, self.got)
        sx, sy = block_sums(
            self.name + "_xy",
            [
                ([(v, size, 1, 0) for v in both] + [(lo, h, 0, 0)], size, B16),
                ([(v, size, 2, 0) for v in both] + [(hi, h, 0, h)], size, B16),
            ],
        )
        self.sent = [sx, sy]
        self.xy = [over_x(sx), over_y(sy)]
        return self.xy

    def stage_z(self, *deps):
        rx, ry = after(tuple(self.xy), *deps)
        all_four = (self.near, self.got, rx, ry)
        if self.shifts:
            own, *self.sent = block_sums(
                self.name + "_z",
                [
                    ([(v, 1, d, 0) for v in all_four], 1, B16 if d else F32)
                    for d in range(self.n)
                ],
            )
            self.z = [own] + [
                lax.ppermute(v, "shard", [(i, (i + d) % self.n) for i in range(self.n)])
                for d, v in enumerate(self.sent, 1)
            ]
            return self.z[1:]
        self.sent = block_sums(
            self.name + "_z", [([(v, self.size, 0, 0) for v in all_four], self.size, B16)]
        )
        v = self.sent[0]
        self.z = [over_z(v.reshape((self.n, self.size // self.n) + v.shape[1:]))]
        return self.z

    def results(self, *deps):
        z = after(tuple(self.z), *deps)
        if self.shifts:
            return [functools.reduce(lambda a, b: a + b, [v[0].astype(F32) for v in z])]
        z = jnp.sum(z[0].astype(F32), axis=0)
        return [z[k] for k in range(z.shape[0])]


def joint_z(parts, n, name):
    terms, count = [], len(parts)
    for i, (r, k) in enumerate(parts):
        chunks = r.size // n
        for z in range(n):
            terms += [(v, 1, z * chunks + k, z * count + i) for v in (r.near, r.got, *r.xy)]
    (v,) = block_sums(name, [(terms, n * count, B16)])
    return v.reshape((n, count) + v.shape[1:])


EVERY = ("x", "core", "shard", "ctx")


def gather_whole(own):
    return lax.all_gather(own, EVERY, axis=0, tiled=False)


def reduce_whole(parts):
    return lax.psum_scatter(parts, EVERY, scatter_dimension=0, tiled=False).astype(F32)


class GatherWhole:
    sent = ()
    spread = ()

    def __init__(self, owns, n):
        d = owns[0].shape[1]
        self.out = [gather_whole(v).reshape(4, d, d) for v in owns]

    def stage_z(self, *deps):
        return []

    stage_xy = stage_rest = stage_z

    def stage_core(self, *deps):
        return self.out


class ReduceWhole:
    sent = ()

    def __init__(self, parts, n, name, shifts=False):
        self.parts = parts

    def stage_z(self, *deps):
        return []

    stage_core = stage_rest = stage_xy = stage_z

    def results(self, *deps):
        rows = self.parts[0].shape[1] // (2 * lax.axis_size("shard"))
        return [reduce_whole(p.reshape(-1, rows, p.shape[2]).astype(F32)) for p in self.parts]


def dot(a, b):
    return jnp.dot(a, b, preferred_element_type=F32)


def dot_nt(a, b):
    return lax.dot_general(a, b, NT_DIMS, preferred_element_type=F32)


def dot_tn(a, b):
    return lax.dot_general(a, b, TN_DIMS, preferred_element_type=F32)


def low_lanes(shape):
    return lax.broadcasted_iota(jnp.int32, shape, 1) % 128 < 64


def keep_low(v):
    return jnp.where(low_lanes(v.shape), v, jnp.zeros_like(v))


def keep_high(v):
    return jnp.where(low_lanes(v.shape), jnp.zeros_like(v), v)


def swap_halves(v):
    return jnp.concatenate([v[:, 64:], v[:, :64]], axis=1)


def norm_parts(x):
    centred = x - jnp.mean(x, axis=-1, keepdims=True)
    rstd = lax.rsqrt(jnp.mean(centred * centred, axis=-1, keepdims=True) + EPSILON)
    return centred * rstd, rstd


def norm_back(x, gain, up):
    unit, rstd = norm_parts(x)
    w = up * gain
    inner = jnp.mean(w * unit, axis=-1, keepdims=True)
    down = rstd * (w - jnp.mean(w, axis=-1, keepdims=True) - unit * inner)
    return down, jnp.sum(up * unit, axis=0, keepdims=True), jnp.sum(up, axis=0, keepdims=True)


def weight_copies(meta, bufs, w_refs, sems, n, back=False, shifts=False, first_column=0):
    moves = []
    if bufs[0].shape == w_refs[0].shape:
        moves = list(zip(bufs, w_refs))
    else:
        x, y, c = meta[0], meta[1], meta[2]
        rows = w_refs[0].shape[1] // (2 * n)
        groups = {}
        cols = slice(first_column, w_refs[0].shape[2])
        for dc in range(2):
            first = 0
            for k, (dx, dy, blocks) in enumerate(layout(len(w_refs), n)):
                tp = 2 * (x ^ dx) + (c ^ dc)
                for i, (z, chunk) in enumerate(blocks):
                    if shifts:
                        z = lax.rem(meta[3] + z, n)
                    row = pl.multiple_of((z * 2 + (y ^ dy)) * rows, rows)
                    piece = bufs[dc].at[first + i] if back else bufs[dc * 5 + k].at[i, 0:rows, cols]
                    whole = w_refs[chunk].at[tp, pl.ds(row, rows), cols]
                    groups.setdefault((dx, dc), []).append((piece, whole))
                first += len(blocks)
        moves = [m for g in sorted(groups) for m in groups[g]]
    if back:
        moves = [(whole, piece) for piece, whole in moves]
    return [pltpu.make_async_copy(*m, sems.at[i]) for i, m in enumerate(moves)]


def copy_sems(sz, chunks):
    return pltpu.SemaphoreType.DMA((8 * chunks * sz["n"],))


def start_all(copies):
    for c in copies:
        c.start()


def wait_all(copies):
    for c in copies:
        c.wait()


def take_blocks(blocks, dst, places):
    for k, blk in enumerate(blocks):
        dx, dy = k % 2, k // 2
        for f in range(2):
            row = (2 * dx + f) * 2 * PAD + dy * PAD
            dst[row + PAD - 8 : row + PAD, :] = jnp.zeros((8, dst.shape[1]), dst.dtype)
            dst[row : row + places, :] = blk[f].astype(dst.dtype)


def give_blocks(src, blocks, places):
    for k, blk in enumerate(blocks):
        dx, dy = k % 2, k // 2
        for f in range(2):
            row = (2 * dx + f) * 2 * PAD + dy * PAD
            blk[f] = src[row : row + places, :].astype(blk.dtype)


def project_heads(normed, w_ref, q_out, kv_out):
    @pl.loop(0, 2)
    def _(u):
        thirds = []
        for t in (2 * u, 2 * u + 1):
            xn = normed[...]
            y = dot(xn, w_ref[t, :, 0:512]).astype(B16)
            q_out[t] = y[:, 0:128]
            kv_out[t] = y[:, 128:256]
            kv_out[6 + t] = y[:, 256:384]
            thirds.append((y[:, 384:512], dot(xn, w_ref[t, :, 640:768]).astype(B16)))
        (a3, a5), (b3, b5) = thirds
        low = low_lanes(a3.shape)
        q_out[4 + u] = jnp.where(low, a3, b3)
        kv_out[4 + u] = swap_halves(jnp.where(low, b3, a3))
        kv_out[10 + u] = swap_halves(jnp.where(low, b5, a5))


def third_head(v, t):
    return keep_low(v) if t % 2 == 0 else keep_high(v)


def project_out(mixed, w_ref, stream, bias, out):
    for n in range(3):
        cols = slice(256 * n, 256 * n + 256)
        acc = stream[:, cols] + bias[:, cols]
        for t in range(4):
            m = jnp.concatenate([mixed[t], third_head(mixed[4 + t // 2], t)], axis=1)
            acc = acc + dot_nt(m, w_ref[t, cols, 512:768])
        out[:, cols] = acc


class Late:
    def __init__(self, source, ref, sem):
        self.ref, self.copy = ref, pltpu.make_async_copy(source, ref, sem)
        self.copy.start()

    def get(self):
        self.copy.wait()
        return self.ref


class Early:
    def __init__(self, ref, target, sem):
        self.ref, self.copy = ref, pltpu.make_async_copy(ref, target, sem)

    def send(self):
        self.copy.start()


def run(kernel, name, ins, outs, scratch, micros):
    space = {
        "v": pl.BlockSpec(memory_space=pltpu.VMEM),
        "s": pl.BlockSpec(memory_space=pltpu.SMEM),
        "a": pl.BlockSpec(memory_space=pl.ANY),
    }
    space["l"] = space["e"] = space["a"]
    late = [i for i, (_, k) in enumerate(ins) if k == "l"]
    early = [i for i, (_, _, k) in enumerate(outs) if k == "e"]
    extra = [pltpu.VMEM(ins[i][0].shape, ins[i][0].dtype) for i in late]
    extra += [pltpu.VMEM(outs[i][0], outs[i][1]) for i in early]
    if extra:
        extra.append(pltpu.SemaphoreType.DMA((len(extra),)))

    def body(*refs):
        refs = list(refs)
        held = refs[len(ins) + len(outs) + len(scratch) :]
        refs = refs[: len(ins) + len(outs) + len(scratch)]
        for j, i in enumerate(late):
            refs[i] = Late(refs[i], held[j], held[-1].at[j])
        for j, i in enumerate(early, len(late)):
            refs[len(ins) + i] = Early(held[j], refs[len(ins) + i], held[-1].at[j])
        kernel(*refs)
        for i in early:
            refs[len(ins) + i].copy.wait()

    return pl.pallas_call(
        body,
        name=name,
        in_specs=[space[s] for _, s in ins],
        out_specs=[space[s] for _, _, s in outs],
        out_shape=[jax.ShapeDtypeStruct(s, d) for s, d, _ in outs],
        scratch_shapes=list(scratch) + extra,
        compiler_params=pltpu.CompilerParams(vmem_limit_bytes=VMEM_LIMIT),
        cost_estimate=pl.CostEstimate(
            flops=micros * 10**9, bytes_accessed=micros * 3 * 10**6, transcendentals=0
        ),
    )(*[a for a, _ in ins])


def row_slices(r, step=208):
    return pl.ds(pl.multiple_of(r * step, step), step)


VECTORS = 9


def norm_vectors(sz, meta, weights):
    d, n, nw = sz["d"], sz["n"], len(weights)
    count, rows = 8 * n, d // (2 * n)
    per = d // count
    hidden = VECTORS * per

    def kernel(*refs):
        meta, bufs = refs[0], refs[1 : 1 + nw]
        out, shares, sems = refs[1 + nw :]
        x, y, c = meta[0], meta[1], meta[2]
        copies = []
        for dc in range(2):
            for k, (dx, dy, blocks) in enumerate(layout(1, n)):
                tp = 2 * (x ^ dx) + (c ^ dc)
                for i, (z, _) in enumerate(blocks):
                    dev = (z * 2 + (y ^ dy)) * 4 + tp
                    piece = bufs[dc * 5 + k].at[i, rows : rows + 8, :]
                    copies.append(
                        pltpu.make_async_copy(piece, shares.at[dev], sems.at[len(copies)])
                    )
        start_all(copies)
        lane = lax.broadcasted_iota(jnp.int32, (128, d), 1)
        row = lax.broadcasted_iota(jnp.int32, (128, d), 0)
        one = ((lane % per == row) & (row < per)).astype(F32).astype(B16)
        four = ((lane % (4 * per) == row) & (row < 4 * per)).astype(F32).astype(B16)
        dev = lax.broadcasted_iota(jnp.int32, (count, d), 0)
        lanes = lax.broadcasted_iota(jnp.int32, (count, d), 1)
        mine = lanes // per == dev
        ours = lanes // (4 * per) == dev % 8
        wait_all(copies)
        rows_in = shares[:, 0, :].astype(F32)
        pad = jnp.zeros((count, 128), F32)
        rows_in = jnp.concatenate([rows_in, pad], axis=1)

        def spread(first, pick):
            parts = [rows_in[:, o + first : o + first + 128].astype(B16) for o in (0, 384)]
            return dot(parts[0], pick) + dot(parts[1], pick)

        for v in range(VECTORS):
            got = jnp.where(mine, spread(v * per, one), 0.0)
            out[v : v + 1, :] = jnp.sum(got, axis=0, keepdims=True)
        got = jnp.where(ours, spread(hidden, four), 0.0)
        for t in range(4):
            part = got[t * 8 : t * 8 + 8] if count == 32 else got
            out[VECTORS + t : VECTORS + t + 1, :] = jnp.sum(part, axis=0, keepdims=True)

    ins = [(meta, "s")] + [(w, "a") for w in weights]
    outs = [((16, d), F32, "v")]
    scratch = [pltpu.VMEM((count, 8, d), B16), copy_sems(sz, 1)]
    return run(kernel, "norm_vectors", ins, outs, scratch, 2)[0]


def time_qkv(sz, meta, vec, blocks, weights):
    rows, d = sz["rows"], sz["d"]
    nb, nw = len(blocks), len(weights)

    def kernel(*refs):
        meta, vec = refs[0], refs[1]
        blks, bufs = refs[2 : 2 + nb], refs[2 + nb : 2 + nb + nw]
        x, normed, q, kv, w, sems = refs[2 + nb + nw :]
        copies = weight_copies(meta, bufs, [w], sems, sz["n"])
        start_all(copies)
        take_blocks(blks, x, sz["places"])

        @pl.loop(0, 4)
        def _(r):
            at = row_slices(r)
            unit, _ = norm_parts(x[at, :])
            normed[at, :] = (unit * vec[0:1, :] + vec[1:2, :]).astype(B16)

        wait_all(copies)
        project_heads(normed, w, q, kv)

    ins = [(meta, "s"), (vec, "v")] + [(b, "v") for b in blocks] + [(w, "a") for w in weights]
    outs = [
        ((rows, d), F32, "v"),
        ((rows, d), B16, "v"),
        ((6, rows, 128), B16, "v"),
        ((12, rows, 128), B16, "v"),
    ]
    scratch = [pltpu.VMEM((4, d, d), B16), copy_sems(sz, 1)]
    return run(kernel, "time_qkv", ins, outs, scratch, 12)


def head_sums(ref):
    for f in range(4):
        for j in range(6):
            col = lax.broadcasted_iota(jnp.int32, (128, 128), 1)
            lane = lax.broadcasted_iota(jnp.int32, (128, 128), 0)
            hit = col == 16 * f + 2 * j + lane // 64
            ref[(f * 6 + j) * 128 : (f * 6 + j) * 128 + 128, :] = hit.astype(F32).astype(B16)


def head_spreads(ref):
    for f in range(4):
        for j in range(6):
            row = lax.broadcasted_iota(jnp.int32, (128, 128), 0)
            lane = lax.broadcasted_iota(jnp.int32, (128, 128), 1)
            hit = row == 16 * f + 2 * j + lane // 64
            ref[:, (f * 6 + j) * 128 : (f * 6 + j) * 128 + 128] = hit.astype(F32).astype(B16)


def pair_sums(a_ref, b_ref, b_tile, g, sums):
    at = row_slices(g)
    products = [
        a_ref[j, f * 208 : f * 208 + 208, :] * b_ref[b_tile + j, at, :]
        for f in range(4)
        for j in range(6)
    ]
    return dot(jnp.concatenate(products, axis=1), sums[...])


def two_tiles(ref, tile, at):
    return jnp.concatenate([ref[tile, at, :], ref[tile + 1, at, :]], axis=1).astype(F32)


def time_mix(sz, meta, vec, stream, q, kv, kvo, weights):
    rows, d = sz["rows"], sz["d"]
    nw = len(weights)

    def kernel(*refs):
        meta, vec, stream, q, kv, kvo = refs[:6]
        bufs = refs[6 : 6 + nw]
        mixed_out, out, prob_out, w, sums, spreads, acc, sems = refs[6 + nw :]
        mixed, prob = mixed_out.ref, prob_out.ref
        copies = weight_copies(meta, bufs, [w], sems, sz["n"], first_column=512)
        start_all(copies)
        head_sums(sums)
        head_spreads(spreads)
        for h in range(2):
            if h == 1:
                kvo = kvo.get()
            ref = (kv, kvo)[h]

            @pl.loop(0, 4)
            def _(g, ref=ref, h=h):
                prob[4 * h + g] = pair_sums(q, ref, 0, g, sums) * SCALING

        @pl.loop(0, 13)
        def _(r):
            at = row_slices(r, 16)
            s = [prob[g, at, :] for g in range(8)]
            top = functools.reduce(jnp.maximum, s)
            e = [jnp.exp(v - top) for v in s]
            inv = 1.0 / functools.reduce(lambda a, b: a + b, e)
            for g in range(8):
                prob[g, at, :] = e[g] * inv

        prob_out.send()
        acc[...] = jnp.zeros_like(acc)
        for h, ref in enumerate((kv, kvo)):

            @pl.loop(0, 4)
            def _(g):
                at = row_slices(g)
                p = prob[4 * h + g].astype(B16)
                for jj in range(3):
                    v = two_tiles(ref, 6 + 2 * jj, at)
                    for f in range(4):
                        lanes = slice(f * d + 256 * jj, f * d + 256 * jj + 256)
                        acc[f * 208 : f * 208 + 208, 256 * jj : 256 * jj + 256] += (
                            dot(p, spreads[:, lanes]) * v
                        )

        for j in range(6):
            mixed[j] = acc[:, 128 * j : 128 * j + 128].astype(B16)
        mixed_out.send()
        wait_all(copies)
        project_out(mixed, w, stream.get(), vec[2:3, :], out)

    ins = [(meta, "s"), (vec, "v"), (stream, "l"), (q, "v"), (kv, "v"), (kvo, "l")]
    ins += [(w, "a") for w in weights]
    outs = [((6, rows, 128), B16, "e"), ((rows, d), F32, "v"), ((8, 208, 128), F32, "e")]
    scratch = [
        pltpu.VMEM((4, d, d), B16),
        pltpu.VMEM((4 * d, 128), B16),
        pltpu.VMEM((128, 4 * d), B16),
        pltpu.VMEM((rows, d), F32),
        copy_sems(sz, 1),
    ]
    return run(kernel, "time_mix", ins, outs, scratch, 17)


def space_mask(places):
    return lax.broadcasted_iota(jnp.int32, (208, 208), 0) % PAD < places


def space_qkv(sz, meta, vec, stream, weights):
    rows, d = sz["rows"], sz["d"]
    nw = len(weights)

    def kernel(*refs):
        meta, vec, stream = refs[:3]
        bufs = refs[3 : 3 + nw]
        normed, q, kv, w, sems = refs[3 + nw :]
        copies = weight_copies(meta, bufs, [w], sems, sz["n"])
        start_all(copies)

        @pl.loop(0, 4)
        def _(r):
            at = row_slices(r)
            unit, _ = norm_parts(stream[at, :])
            normed[at, :] = (unit * vec[3:4, :] + vec[4:5, :]).astype(B16)

        wait_all(copies)
        project_heads(normed, w, q, kv)

    ins = [(meta, "s"), (vec, "v"), (stream, "v")] + [(w, "a") for w in weights]
    outs = [((rows, d), B16, "v"), ((6, rows, 128), B16, "v"), ((12, rows, 128), B16, "v")]
    scratch = [pltpu.VMEM((4, d, d), B16), copy_sems(sz, 1)]
    return run(kernel, "space_qkv", ins, outs, scratch, 12)


def space_mix(sz, meta, vec, stream, q, kv, weights):
    rows, d, places = sz["rows"], sz["d"], sz["places"]
    nw = len(weights)

    def kernel(*refs):
        meta, vec, stream, q, kv = refs[:5]
        bufs = refs[5 : 5 + nw]
        mixed_out, logs, out, w, sems = refs[5 + nw :]
        mixed = mixed_out.ref
        copies = weight_copies(meta, bufs, [w], sems, sz["n"], first_column=512)
        start_all(copies)

        def mix(j, f):
            at = row_slices(f)
            qj, kj, vj = q[j, at, :], kv[j, at, :], kv[6 + j, at, :]
            mask = space_mask(places)
            o = None
            for h, keep in enumerate((keep_low, keep_high)):
                s = jnp.where(mask, dot_nt(kj, keep(qj)) * SCALING, NEGATIVE)
                top = jnp.max(s, axis=0, keepdims=True)
                e = jnp.exp(s - top)
                size = jnp.sum(e, axis=0, keepdims=True)
                logs[j * 4 + f, h : h + 1, :] = top + jnp.log(size)
                part = dot_tn((e * (1.0 / size)).astype(B16), keep(vj))
                o = part if o is None else o + part
            return o.astype(B16)

        @pl.loop(0, 6)
        def _(j):
            frames = [mix(j, f) for f in range(4)]
            for f in range(4):
                mixed[j, row_slices(f), :] = frames[f]

        mixed_out.send()
        wait_all(copies)
        project_out(mixed, w, stream.get(), vec[5:6, :], out)

    ins = [(meta, "s"), (vec, "v"), (stream, "l"), (q, "v"), (kv, "v")]
    ins += [(w, "a") for w in weights]
    outs = [((6, rows, 128), B16, "e"), ((24, 8, 208), F32, "v"), ((rows, d), F32, "v")]
    scratch = [pltpu.VMEM((4, d, d), B16), copy_sems(sz, 1)]
    return run(kernel, "space_mix", ins, outs, scratch, 17)


def gradient_outs(sz, chunks, fast):
    d, n = sz["d"], sz["n"]
    if not fast:
        return [((4, d, d), B16, "a")] * chunks
    return [((4 * chunks * n, d // (2 * n), d), B16, "a")] * 2


def gelu_pair(x):
    half = 0.5 * (1.0 + lax.erf(x * 0.7071067811865476))
    slope = half + x * (0.3989422804014327 * jnp.exp(-0.5 * x * x))
    return x * half, slope


def feed_forward(sz, meta, vec, stream, blocks, weights, fast):
    rows, d, places = sz["rows"], sz["d"], sz["places"]
    nb, nw = len(blocks), len(weights)
    g_outs = gradient_outs(sz, 2, fast)
    ng = len(g_outs)

    def kernel(*refs):
        meta, vec, stream = refs[:3]
        blks = refs[3 : 3 + nb]
        refs = refs[3 + nb :]
        bufs, refs = refs[:nw], refs[nw:]
        res, refs = refs[:nb], refs[nb:]
        d2, vgrad = refs[0], refs[1]
        g_bufs, refs = refs[2 : 2 + ng], refs[2 + ng :]
        w1, w2, dw1, dw2, dz, dzr, normed, act, dpre, y, dn, sems, back_sems = refs
        copies = weight_copies(meta, bufs, [w1, w2], sems, sz["n"])
        start_all(copies)
        take_blocks(blks, dz, places)
        vgrad[...] = jnp.zeros_like(vgrad)

        @pl.loop(0, 4)
        def _(r):
            at = pl.ds(pl.multiple_of(r * 208, 208), 208)
            unit, _ = norm_parts(stream[at, :])
            normed[at, :] = (unit * vec[6:7, :] + vec[7:8, :]).astype(B16)
            up = dz[at, :]
            dzr[at, :] = up.astype(B16)
            vgrad[2:3, :] += jnp.sum(up, axis=0, keepdims=True)
            y[at, :] = stream[at, :] + vec[8:9, :]
            dn[at, :] = jnp.zeros_like(up)

        back = weight_copies(meta, g_bufs, [dw1, dw2], back_sems, sz["n"], back=True)
        group = len(copies) // 4
        if not fast:
            wait_all(copies)

        @pl.loop(0, 4)
        def _(k):
            t = k
            if fast:
                t = 2 * (meta[0] ^ (k // 2)) + (meta[2] ^ (k % 2))
                rows_here = w1.shape[1] // (2 * sz["n"])
                piece = (bufs[0].at[0, 0:rows_here, :], w1.at[0, 0:rows_here, :])
                for i in range(group):
                    pltpu.make_async_copy(*piece, sems.at[k * group + i]).wait()
            thirds = [slice(256 * i, 256 * i + 256) for i in range(3)]
            for cols in thirds:
                pre = dot(normed[...], w1[t, :, cols]) + vec[pl.ds(9 + t, 1), cols]
                a, slope = gelu_pair(pre)
                act[:, cols] = a.astype(B16)
                g = (dot(dzr[...], w2[t, :, cols]) * slope).astype(B16)
                dpre[:, cols] = g
                vgrad[pl.ds(4 + t, 1), cols] += jnp.sum(g.astype(F32), axis=0, keepdims=True)
            for cols in thirds:
                y[:, cols] += dot_nt(act[...], w2[t, cols, :])
                dn[:, cols] += dot_nt(dpre[...], w1[t, cols, :])
            for cols in thirds:
                dw1[t, :, cols] = dot_tn(normed[...], dpre[:, cols]).astype(B16)
                dw2[t, :, cols] = dot_tn(dzr[...], act[:, cols]).astype(B16)
            if fast:
                for i in range(4):
                    pl.when(k == i)(lambda i=i: start_all(back[i * group : i * group + group]))

        if not fast:
            start_all(back)
        give_blocks(y, res, places)

        @pl.loop(0, 4)
        def _(r):
            at = pl.ds(pl.multiple_of(r * 208, 208), 208)
            down, gg, gs = norm_back(stream[at, :], vec[6:7, :], dn[at, :])
            d2[at, :] = dz[at, :] + down
            vgrad[0:1, :] += gg
            vgrad[1:2, :] += gs

        wait_all(back)

    ins = [(meta, "s"), (vec, "v"), (stream, "v")] + [(b, "v") for b in blocks]
    ins += [(w, "a") for w in weights]
    outs = [((2, places, d), B16, "v")] * nb + [((rows, d), F32, "v"), ((8, d), F32, "v")]
    outs += g_outs
    scratch = [pltpu.VMEM((4, d, d), B16)] * 4
    scratch += [pltpu.VMEM((rows, d), F32), pltpu.VMEM((rows, d), B16), pltpu.VMEM((rows, d), B16)]
    scratch += [pltpu.VMEM((rows, d), B16)] * 2 + [pltpu.VMEM((rows, d), F32)] * 2
    scratch += [copy_sems(sz, 2)] * 2
    r = run(kernel, "feed_forward", ins, outs, scratch, 47)
    return r[:nb], r[nb], r[nb + 1], r[nb + 2 :]


def mixed_slopes(up, w_ref, dm):
    for u in range(2):
        thirds = []
        for t in (2 * u, 2 * u + 1):
            v = dot(up[...], w_ref[t, :, 512:768]).astype(B16)
            dm[t] = v[:, 0:128]
            thirds.append(v[:, 128:256])
        dm[4 + u] = jnp.where(low_lanes(thirds[0].shape), *thirds)


def place_third(dq, dk, dv, dy, u, at):
    k, v = swap_halves(dk), swap_halves(dv)
    low = low_lanes(dq.shape)
    dy[2 * u, at, 384:512] = jnp.where(low, dq, k)
    dy[2 * u + 1, at, 384:512] = jnp.where(low, k, dq)
    dy[2 * u, at, 512:640] = keep_high(v)
    dy[2 * u + 1, at, 512:640] = keep_low(v)


def third_head_of(v, odd):
    return jnp.where(low_lanes(v.shape) == (odd == 0), v, jnp.zeros_like(v))


def output_gradients(dw, up, mixed):
    @pl.loop(0, 4)
    def _(t):
        third = third_head_of(mixed[4 + t // 2], t % 2)
        out = dot_tn(up[...], jnp.concatenate([mixed[t], third], axis=1))
        dw[t, :, 512:768] = out.astype(B16)


def head_gradients(t, dw, normed, dy):
    dw[t, :, 0:512] = dot_tn(normed[...], dy[t, :, 0:512]).astype(B16)
    third = dot_tn(normed[...], dy[t, :, 512:640])
    dw[t, :, 640:768] = (dw[t, :, 640:768].astype(F32) + third).astype(B16)


def norm_slopes(t, dy, w_ref, out):
    for n in range(3):
        cols = slice(256 * n, 256 * n + 256)
        part = dot_nt(dy[t, :, 0:512], w_ref[t, cols, 0:512])
        out[:, cols] += part + dot_nt(dy[t, :, 512:640], w_ref[t, cols, 640:768])


def space_backward_scores(sz, meta, d2, q, kv, logs, weights):
    rows, d, places = sz["rows"], sz["d"], sz["places"]
    nw = len(weights)

    def kernel(*refs):
        meta, d2, q, kv, logs = refs[:5]
        bufs, refs = refs[5 : 5 + nw], refs[5 + nw :]
        up_out, dy, w, dm, third, sems = refs
        up = up_out.ref
        copies = weight_copies(meta, bufs, [w], sems, sz["n"], first_column=512)
        start_all(copies)

        @pl.loop(0, 4)
        def _(r):
            up[row_slices(r), :] = d2[row_slices(r), :].astype(B16)

        wait_all(copies)
        up_out.send()
        mixed_slopes(up, w, dm)
        q, kv, logs = q.get(), kv.get(), logs.get()

        def slopes(j, at, f):
            qj, kj, vj, mj = q[j, at, :], kv[j, at, :], kv[6 + j, at, :], dm[j, at, :]
            mask = space_mask(places)
            dq = dk = dv = None
            for h, keep in enumerate((keep_low, keep_high)):
                qh, mh = keep(qj), keep(mj)
                s = dot_nt(kj, qh) * SCALING - logs[j * 4 + f, h : h + 1, :]
                p = jnp.exp(jnp.where(mask, s, NEGATIVE))
                dp = dot_nt(vj, mh)
                inner = jnp.sum(p * dp, axis=0, keepdims=True)
                ds = (p * (dp - inner) * SCALING).astype(B16)
                a, b, c = dot_tn(ds, keep(kj)), dot(ds, qh), dot(p.astype(B16), mh)
                dq, dk, dv = (a, b, c) if dq is None else (dq + a, dk + b, dv + c)
            return dq.astype(B16), dk.astype(B16), dv.astype(B16)

        @pl.loop(0, 4)
        def _(j):
            ats = [row_slices(f) for f in range(4)]
            frames = [slopes(j, ats[f], f) for f in range(4)]
            for at, (dq, dk, dv) in zip(ats, frames):
                dy[j, at, 0:128] = dq
                dy[j, at, 128:256] = dk
                dy[j, at, 256:384] = dv

        @pl.loop(0, 2)
        def _(u):
            ats = [row_slices(f) for f in range(4)]
            frames = [slopes(4 + u, ats[f], f) for f in range(4)]
            for at, v in zip(ats, frames):
                place_third(*v, dy, u, at)

    ins = [(meta, "s")] + [(d2, "v")] + [(v, "l") for v in (q, kv, logs)] + [(w, "a") for w in weights]
    outs = [((rows, d), B16, "e"), ((4, rows, 640), B16, "v")]
    scratch = [pltpu.VMEM((4, d, d), B16), pltpu.VMEM((6, rows, 128), B16)]
    scratch += [pltpu.VMEM((rows, 128), B16), copy_sems(sz, 1)]
    return run(kernel, "space_backward_scores", ins, outs, scratch, 30)


def weight_slopes(sz, name, meta, up, normed, mixed, slopes, fast):
    rows, d = sz["rows"], sz["d"]
    g_outs = gradient_outs(sz, 1, fast)
    join = len(slopes) == 3

    def kernel(*refs):
        meta, up, normed, mixed = refs[:4]
        given, refs = refs[4 : 4 + len(slopes)], refs[4 + len(slopes) :]
        dy = refs[0].ref if join else given[0]
        g_bufs, (dw, sems) = refs[1 if join else 0 : -2], refs[-2:]
        if join:
            dq, dkv, got = given

            def both(j, at):
                return (dkv[j, at, :].astype(F32) + got[j, at, :].astype(F32)).astype(B16)

            @pl.loop(0, 4)
            def _(r):
                at = row_slices(r)
                for j in range(4):
                    dy[j, at, 0:128] = dq[j, at, :]
                    dy[j, at, 128:256] = both(j, at)
                    dy[j, at, 256:384] = both(6 + j, at)
                for u in range(2):
                    place_third(dq[4 + u, at, :], both(4 + u, at), both(10 + u, at), dy, u, at)

            refs[0].send()
        back = weight_copies(meta, g_bufs, [dw], sems, sz["n"], back=True, shifts=join)
        group = len(back) // 4
        output_gradients(dw, up.get(), mixed.get())
        normed = normed.get()
        if not join:
            dy = dy.get()

        @pl.loop(0, 4)
        def _(k):
            t = 2 * (meta[0] ^ (k // 2)) + (meta[2] ^ (k % 2)) if fast else k
            head_gradients(t, dw, normed, dy)
            if fast:
                for i in range(4):
                    pl.when(k == i)(lambda i=i: start_all(back[i * group : i * group + group]))

        if not fast:
            start_all(back)
        wait_all(back)

    ins = [(meta, "s")] + [(v, "l") for v in (up, normed, mixed)]
    ins += [(v, "v" if join else "l") for v in slopes]
    outs = ([((4, rows, 640), B16, "e")] if join else []) + g_outs
    scratch = [pltpu.VMEM((4, d, d), B16), copy_sems(sz, 1)]
    return run(kernel, name, ins, outs, scratch, 14)


def input_slopes(sz, name, meta, vec, up, stream, dy, weights, gain_row, blocks):
    rows, d, places = sz["rows"], sz["d"], sz["places"]
    nw = len(weights)

    def kernel(*refs):
        meta, vec, up, stream, dy = refs[:5]
        bufs, refs = refs[5 : 5 + nw], refs[5 + nw :]
        w, dn, sems = refs[-3:]
        if blocks:
            outs, vgrad, dx = refs[:4], refs[4], refs[5]
        else:
            dx, vgrad = refs[:2]
        copies = weight_copies(meta, bufs, [w], sems, sz["n"])
        start_all(copies)
        vgrad[...] = jnp.zeros_like(vgrad)
        dn[...] = jnp.zeros_like(dn)
        fast = nw > 1
        group = len(copies) // 4
        if not fast:
            wait_all(copies)

        @pl.loop(0, 4)
        def _(k):
            t = k
            if fast:
                t = 2 * (meta[0] ^ (k // 2)) + (meta[2] ^ (k % 2))
                rows_here = w.shape[1] // (2 * sz["n"])
                piece = (bufs[0].at[0, 0:rows_here, :], w.at[0, 0:rows_here, :])
                for i in range(group):
                    pltpu.make_async_copy(*piece, sems.at[k * group + i]).wait()
            norm_slopes(t, dy, w, dn)

        up, stream = up.get(), stream.get()

        @pl.loop(0, 4)
        def _(r):
            at = row_slices(r)
            v = up[at, :]
            gain = vec[gain_row : gain_row + 1, :]
            down, gg, gs = norm_back(stream[at, :], gain, dn[at, :])
            dx[at, :] = v + down
            vgrad[0:1, :] += gg
            vgrad[1:2, :] += gs
            vgrad[2:3, :] += jnp.sum(v, axis=0, keepdims=True)

        if blocks:
            give_blocks(dx, outs, places)

    ins = [(meta, "s"), (vec, "v"), (up, "l"), (stream, "l"), (dy, "v")]
    ins += [(w, "a") for w in weights]
    outs = [((rows, d), F32, "v")]
    scratch = []
    if blocks:
        outs = [((2, places, d), F32, "v")] + [((2, places, d), B16, "v")] * 3
        scratch = [pltpu.VMEM((rows, d), F32)]
    outs += [((8, d), F32, "v")]
    scratch += [pltpu.VMEM((4, d, d), B16), pltpu.VMEM((rows, d), F32), copy_sems(sz, 1)]
    return run(kernel, name, ins, outs, scratch, 14)


def time_backward_scores(sz, meta, d1, q, kv, kvo, prob, weights):
    rows, d = sz["rows"], sz["d"]
    nw = len(weights)

    def kernel(*refs):
        meta, d1, q, kv, kvo, prob = refs[:6]
        bufs, refs = refs[6 : 6 + nw], refs[6 + nw :]
        up_out, dq, dkv_out, dkvo, w, dm, sums, spreads, ds, acc, sems = refs
        up, dkv = up_out.ref, dkv_out.ref
        copies = weight_copies(meta, bufs, [w], sems, sz["n"], first_column=512)
        start_all(copies)
        head_sums(sums)
        head_spreads(spreads)

        @pl.loop(0, 4)
        def _(r):
            up[row_slices(r), :] = d1[row_slices(r), :].astype(B16)

        wait_all(copies)
        up_out.send()
        mixed_slopes(up, w, dm)
        q, kv, kvo, prob = q.get(), kv.get(), kvo.get(), prob.get()
        for h, ref in enumerate((kv, kvo)):

            @pl.loop(0, 4)
            def _(g):
                ds[4 * h + g] = pair_sums(dm, ref, 6, g, sums)

        @pl.loop(0, 13)
        def _(r):
            at = row_slices(r, 16)
            p = [prob[g, at, :] for g in range(8)]
            dp = [ds[g, at, :] for g in range(8)]
            inner = functools.reduce(lambda a, b: a + b, [a * b for a, b in zip(p, dp)])
            for g in range(8):
                ds[g, at, :] = p[g] * (dp[g] - inner) * SCALING

        acc[...] = jnp.zeros_like(acc)
        for h, (ref, out) in enumerate(((kv, dkv), (kvo, dkvo))):

            @pl.loop(0, 4)
            def _(g):
                at = row_slices(g)
                both = jnp.concatenate([ds[4 * h + g], prob[4 * h + g]], axis=0).astype(B16)
                for jj in range(3):
                    k = two_tiles(ref, 2 * jj, at)
                    dk = dv = None
                    for f in range(4):
                        fr = slice(f * 208, f * 208 + 208)
                        e = dot(both, spreads[:, f * d + 256 * jj : f * d + 256 * jj + 256])
                        se, pe = e[:208], e[208:]
                        acc[fr, 256 * jj : 256 * jj + 256] += se * k
                        a = se * two_tiles(q, 2 * jj, fr)
                        b = pe * two_tiles(dm, 2 * jj, fr)
                        dk, dv = (a, b) if dk is None else (dk + a, dv + b)
                    dk, dv = dk.astype(B16), dv.astype(B16)
                    for i in range(2):
                        out[2 * jj + i, at, :] = dk[:, 128 * i : 128 * i + 128]
                        out[6 + 2 * jj + i, at, :] = dv[:, 128 * i : 128 * i + 128]

            if h == 0:
                dkv_out.send()

        for j in range(6):
            dq[j] = acc[:, 128 * j : 128 * j + 128].astype(B16)

    ins = [(meta, "s")] + [(d1, "v")] + [(v, "l") for v in (q, kv, kvo, prob)] + [(w, "a") for w in weights]
    outs = [
        ((rows, d), B16, "e"),
        ((6, rows, 128), B16, "v"),
        ((12, rows, 128), B16, "e"),
        ((12, rows, 128), B16, "v"),
    ]
    scratch = [
        pltpu.VMEM((4, d, d), B16),
        pltpu.VMEM((6, rows, 128), B16),
        pltpu.VMEM((4 * d, 128), B16),
        pltpu.VMEM((128, 4 * d), B16),
        pltpu.VMEM((8, 208, 128), F32),
        pltpu.VMEM((rows, d), F32),
        copy_sems(sz, 1),
    ]
    return run(kernel, "time_backward_scores", ins, outs, scratch, 23)


def pack_heads(qkv, proj, odd):
    q, k, v = qkv[:, 0], qkv[:, 1], qkv[:, 2]
    o = proj.T
    first = [q[:, :128], k[:, :128], v[:, :128]]
    even = first + [q[:, 128:], k[:, 128:], o[:, :128], o[:, 128:], v[:, 128:]]
    other = first + [k[:, 128:], q[:, 128:], o[:, :128], v[:, 128:], o[:, 128:]]
    return jnp.where(odd, jnp.concatenate(other, axis=1), jnp.concatenate(even, axis=1))


def unpack_heads(g, odd):
    def pick(a, b):
        return jnp.where(odd, g[:, b : b + 64], g[:, a : a + 64])

    q = jnp.concatenate([g[:, 0:128], pick(384, 448)], axis=1)
    k = jnp.concatenate([g[:, 128:256], pick(448, 384)], axis=1)
    v = jnp.concatenate([g[:, 256:384], pick(704, 640)], axis=1)
    o = jnp.concatenate([g[:, 512:640], pick(640, 704)], axis=1)
    return jnp.stack([q, k, v], axis=1), o.T


def join_clips(meta, blocks, dtype):
    shape = blocks[0].shape

    def kernel(meta, *refs):
        for k in range(4):

            @pl.when(pl.program_id(0) == k)
            def _(k=k):
                refs[4][0] = refs[k][...].astype(dtype)

    def place(k, m):
        return (2 * (m[0] ^ (k & 1)) + (m[1] ^ (k >> 1)), 0, 0, 0)

    return pl.pallas_call(
        kernel,
        name="join_clips",
        grid_spec=pltpu.PrefetchScalarGridSpec(
            num_scalar_prefetch=1,
            grid=(4,),
            in_specs=[pl.BlockSpec(shape, lambda k, m: (0, 0, 0))] * 4,
            out_specs=pl.BlockSpec((1,) + shape, place),
        ),
        out_shape=jax.ShapeDtypeStruct((4,) + shape, dtype),
        compiler_params=pltpu.CompilerParams(vmem_limit_bytes=VMEM_LIMIT),
        cost_estimate=pl.CostEstimate(flops=10**8, bytes_accessed=10**5, transcendentals=0),
    )(meta, *blocks)


def local(mesh_shape, video, cotangent, *params):
    qkv_time, proj_time, qkv_space, proj_space, fc_in, fc_out = params[:6]
    vectors = params[6:]
    n = mesh_shape["shard"]
    d = proj_time.shape[0] * 4
    places = video.shape[2]
    rows_here = fc_in.shape[0]
    fast = rows_here % 16 == 0
    sz = {"n": n, "d": d, "places": places, "rows": 8 * PAD}
    x, y = lax.axis_index("x"), lax.axis_index("ctx")
    c, z = lax.axis_index("core"), lax.axis_index("shard")
    meta = jnp.stack([x, y, c, z]).astype(jnp.int32)
    every = ("shard", "ctx", "x", "core")
    count = 8 * n

    gather, reduce = (Gather, Reduce) if fast else (GatherWhole, ReduceWhole)
    per = d // count
    order = [0, 1, 2, 3, 4, 5, 6, 7, 9, 8]
    share = jnp.concatenate([vectors[i] for i in order])
    first_rows = pack_heads(qkv_time, proj_time, c == 1)
    if fast:
        kept = lax.reduce_precision(share, exponent_bits=8, mantissa_bits=7)
        high, low = kept.astype(B16), (share - kept).astype(B16)
        gap = jnp.zeros((384 - share.shape[0],), B16)
        row = jnp.concatenate([high, gap, low, gap])[None]
        first_rows = jnp.concatenate([first_rows, row, jnp.zeros((7, d), B16)], axis=0)

    def clips_of(v):
        return [
            lax.dynamic_index_in_dim(v, 2 * (x ^ dx) + (y ^ dy), 0, keepdims=False)
            for dx, dy in ((0, 0), (1, 0), (0, 1), (1, 1))
        ]

    def frames_back(blocks):
        return [blocks[0], over_x(blocks[1]), over_y(blocks[2]), over_xy(blocks[3])]

    g_t = gather([first_rows], n)
    g_s = gather([pack_heads(qkv_space, proj_space, c == 1)], n)
    g_m = gather([fc_in, fc_out.T], n)
    t_z = g_t.stage_z()
    cot_clips, video_clips = [clips_of(v) for v in after((cotangent, video), g_t.spread)]
    cot_blocks, video_blocks = frames_back(cot_clips), frames_back(video_clips)
    t_xy = g_t.stage_xy(*cot_blocks[1:], *video_blocks[1:3])
    s_z = g_s.stage_z(*t_z)
    t_rest = g_t.stage_rest()
    m_z = g_m.stage_z(*s_z)
    s_xy = g_s.stage_xy(*t_rest)
    w_time = g_t.stage_core()
    if fast:
        vec = norm_vectors(sz, meta, w_time)
    else:
        shares = lax.all_gather(share, every, axis=0, tiled=False)
        vec = shares[:, : VECTORS * per].reshape(count, VECTORS, per).transpose(1, 0, 2)
        hidden = shares[:, VECTORS * per :].reshape(4, d)
        vec = jnp.concatenate([vec.reshape(VECTORS, d), hidden, jnp.zeros((3, d), F32)], axis=0)
    vec_t = after(vec, *g_s.sent, g_m.spread)
    stream0, normed_t, q_t, kv_t = time_qkv(sz, meta, vec_t, video_blocks, w_time)

    kv_o = over_core(after(kv_t, *s_xy, *m_z))
    s_rest = g_s.stage_rest(kv_t)
    m_xy = g_m.stage_xy(kv_t)
    kv_o = after(kv_o, *s_rest, *g_m.sent)
    mixed_t, stream1, prob_t = time_mix(sz, meta, vec, stream0, q_t, kv_t, kv_o, w_time)

    w_space = g_s.stage_core()
    normed_s, q_s, kv_s = space_qkv(sz, meta, vec, stream1, w_space)
    m_rest = g_m.stage_rest(kv_s)
    kv_sb = after(kv_s, *g_m.sent)
    mixed_s, logs, stream2 = space_mix(sz, meta, vec, stream1, q_s, kv_sb, w_space)

    w_mlp = g_m.stage_core(stream2)
    res, d2, vg_m, parts_m = feed_forward(sz, meta, vec, stream2, cot_blocks, w_mlp, fast)

    r_m = reduce(parts_m, n, "mlp")
    m_core = r_m.stage_core()
    result_back = frames_back(res)
    up_s, dy_s = space_backward_scores(sz, meta, d2, q_s, kv_s, logs, w_space)

    m_rest = r_m.stage_rest(up_s)
    dy_s = after(dy_s, *result_back, *r_m.sent)
    parts_s = weight_slopes(sz, "space_weights", meta, up_s, normed_s, mixed_s, [dy_s], fast)
    r_s = reduce(parts_s, n, "space")
    s_core = r_s.stage_core(*m_rest)
    m_xy = r_m.stage_xy(*parts_s)
    d2b = after(d2, *parts_s, *r_m.sent)
    d1, vg_s = input_slopes(sz, "space_input", meta, vec, d2b, stream1, dy_s, w_space, 3, False)
    s_rest = r_s.stage_rest(d1)
    d1b = after(d1, *r_s.sent)
    up_t, dq, dkv, dkvo = time_backward_scores(sz, meta, d1b, q_t, kv_t, kv_o, prob_t, w_time)

    dkv_got = over_core(after(dkvo, *m_xy, *s_rest))
    first_z = ()
    if fast:
        r_m.xy = after(tuple(m_xy), dkvo)
        first_sent = joint_z([(r_m, 0)], n, "mlp_z")
        first_z = (over_z(first_sent),)
    s_xy = r_s.stage_xy(dkvo)
    dkv_got = after(dkv_got, *r_s.sent, first_sent) if fast else dkv_got
    dy_t, *parts_t = weight_slopes(
        sz, "time_weights", meta, up_t, normed_t, mixed_t, [dq, dkv, dkv_got], fast
    )

    r_t = reduce(parts_t, n, "time", True)
    t_core = r_t.stage_core(*s_xy, *first_z)
    t_rest = r_t.stage_rest()
    if fast:
        r_s.xy = after(tuple(s_xy), *r_t.sent)
        sent = joint_z([(r_s, 0), (r_m, 1)], n, "joint_z")
        got = over_z(sent)
    else:
        sent = ()
    t_xy = r_t.stage_xy(sent)
    d1c = after(d1, *r_t.sent)
    *dx, vg_t = input_slopes(sz, "time_input", meta, vec, d1c, stream0, dy_t, w_time, 0, True)

    t_z = r_t.stage_z(vg_t)
    vg_t2, result_back, dx = after((vg_t, tuple(result_back), tuple(dx)), *r_t.sent)
    video_back = frames_back(dx)
    if fast:
        vg_t2 = after(vg_t2, got)

    rows = jnp.concatenate([vg_t2[0:3], vg_s[0:3], vg_m[0:2]], axis=0)
    parts = jnp.concatenate(
        [
            rows.reshape(8, count, per).transpose(1, 0, 2).reshape(count, 8 * per),
            vg_m[4:8].reshape(count, 4 * per),
            vg_m[2].reshape(count, per),
        ],
        axis=1,
    )
    got_parts = lax.all_to_all(parts, every, split_axis=0, concat_axis=0, tiled=True)
    result = join_clips(meta, result_back, B16)
    if fast:
        vec_got, video_back, r_t.z, joint, first = lax.optimization_barrier(
            (got_parts, tuple(video_back), tuple(r_t.z), got, first_z[0])
        )
        joint = jnp.sum(joint.astype(F32), axis=0)
        grad_s, grad_out = joint[0], joint[1]
        grad_in = jnp.sum(first.astype(F32), axis=0)[0]
    else:
        vec_got = got_parts
        grad_in, grad_out = r_m.results()
        (grad_s,) = r_s.results()
    (grad_t,) = r_t.results()
    grad_video = join_clips(meta, video_back, F32)
    sums = jnp.sum(vec_got, axis=0)
    starts = [per * i for i in range(9)] + [per * 12]
    cuts = [sums[starts[i] : starts[i] + (4 * per if i == 8 else per)] for i in range(10)]

    qkv_t_grad, proj_t_grad = unpack_heads(grad_t, c == 1)
    qkv_s_grad, proj_s_grad = unpack_heads(grad_s, c == 1)
    return (
        result,
        grad_video,
        qkv_t_grad,
        proj_t_grad,
        qkv_s_grad,
        proj_s_grad,
        grad_in,
        grad_out.T,
        *cuts,
    )


def solution(mesh):
    shape = dict(mesh.shape)
    fine = Mesh(
        mesh.devices.reshape(shape["shard"], shape["ctx"], 2, shape["tp"] // 2),
        ("shard", "ctx", "x", "core"),
    )
    tp = ("x", "core")
    sc = ("shard", "ctx")
    tokens = P("shard", tp, "ctx", None)
    weights = (P(sc, None, tp), P(tp, sc), P(sc, None, tp), P(tp, sc), P(sc, tp), P(tp, sc))
    vectors = (P(("shard", "ctx", "x", "core")),) * 10
    return jax.shard_map(
        functools.partial(local, shape),
        mesh=fine,
        in_specs=(tokens, tokens) + weights + vectors,
        out_specs=(tokens, tokens) + weights + vectors,
        check_vma=False,
    )
```
